256 devices in a mesh: dp: 8 (over x, core), ulysses: 32 (over z, y).
Axes of the slice: x: 4, y: 4, z: 8, core: 2. Of those that a mesh axis runs over, the one named last changes fastest.
Arguments:
- normalized_input: bfloat16 [8, 4096, 4096], P('dp', 'ulysses'), may hold values from -6 to 6
- frozen_queries: bfloat16 [8, 4096, 4096], P('dp', 'ulysses'), may hold values from -40 to 40
- frozen_keys: bfloat16 [8, 4096, 4096], P('dp', 'ulysses'), may hold values from -8 to 8
- frozen_values: bfloat16 [8, 4096, 4096], P('dp', 'ulysses'), may hold values from -6 to 6
- output_gradient: bfloat16 [8, 4096, 4096], P('dp', 'ulysses'), may hold values from -0.125 to 0.125
- adapter_down_maps: bfloat16 [2, 4096, 64], replicated, may hold values from -0.09375 to 0.09375
- adapter_up_maps: bfloat16 [2, 64, 4096], replicated, may hold values from -0.75 to 0.75
- shifted: int32 [32], replicated, may hold values from 0 to 1, as said below
Outputs:
- grad_down: float32 [2, 4096, 64], P(None, 'ulysses')
- grad_up: float32 [2, 64, 4096], P(None, None, 'ulysses')
The draws below stay inside these ranges and needn't reach their ends.
Inputs may be any that keep to these rules, and one draw needn't show every extreme that they name: `shifted`: exactly half of the 32 heads are marked 1, the others 0.
All inputs are finite; a program needn't handle non-finite values.
Results may differ from the reference program's by a relative error of at most 0.0067.
Values may be sent and summed in bfloat16 or wider, within the bound.
No kernel may reach another device: no remote copies, remote signals or barrier semaphores. Data moves between devices by JAX's collectives and lax.ppermute only.
A program may use at most 64 MiB of HBM per device.

```python
import math
import jax
import jax.numpy as jnp
from jax import lax

HEADS = 32
HD = 128
ADAPTER_RANK = 64
GROUP = 1024
MODEL_WIDTH = 4096
SHIFT = 512
SLICE_TOKENS = 4096
BOOK_SLICES = 8


def shared_pair(key):
    full_shape = (BOOK_SLICES, SLICE_TOKENS, MODEL_WIDTH)
    query_key = jax.random.fold_in(key, 101)
    keys_key = jax.random.fold_in(key, 202)
    key_vals = jnp.clip(jax.random.normal(keys_key, full_shape, jnp.float32), -6.0, 6.0)
    query_vals = jnp.clip(jax.random.normal(query_key, full_shape, jnp.float32), -6.0, 6.0)
    return (query_vals, key_vals)


def draw_frozen_queries(key, part):
    return shared_pair(key)[0].astype(jnp.bfloat16)


def draw_frozen_keys(key, part):
    return shared_pair(key)[1].astype(jnp.bfloat16)


def draw_shifted(key, part):
    order = jax.random.permutation(key, HEADS)
    return (order < HEADS // 2).astype(jnp.int32)


def level_of(rng, dims, split, low, top_value):
    def one(position, blocks):
        steps = jax.random.uniform(jax.random.fold_in(jax.random.fold_in(rng, 6), position), (blocks,), jnp.float32, low / len(split), top_value / len(split))
        return jnp.repeat(jnp.exp(steps), dims[position] // blocks).reshape((-1,) + (1,) * (len(dims) - position - 1))

    factor_of = one(*split[0])
    for cut in split[1:]:
        factor_of = factor_of * one(*cut)
    return factor_of


def normal_values(rng, shape, scale, limit, shards=(), kind=jnp.bfloat16):
    entries = scale * jax.random.normal(rng, shape, jnp.float32)
    if shards:
        entries = entries * level_of(rng, shape, shards, -0.22, 0.18)
    return jnp.clip(entries, -limit, limit).astype(kind)


def setup_inputs(seed: int = 0) -> dict:
    splits = jax.random.split(jax.random.key(seed), 9)
    normalized_input = normal_values(splits[0], (BOOK_SLICES, SLICE_TOKENS, MODEL_WIDTH), 1.0, 6.0, ((0, 8), (1, 32)))
    frozen_queries = draw_frozen_queries(jax.random.fold_in(splits[8], 71), 0)
    frozen_keys = draw_frozen_keys(jax.random.fold_in(splits[8], 71), 0)
    frozen_values = normal_values(splits[3], (BOOK_SLICES, SLICE_TOKENS, MODEL_WIDTH), 1.0, 6.0, ((0, 8), (1, 32)))
    output_gradient = normal_values(splits[4], (BOOK_SLICES, SLICE_TOKENS, MODEL_WIDTH), ((SLICE_TOKENS * BOOK_SLICES // 16) ** -0.5), 0.125, ((0, 8), (1, 32)))
    adapter_down_maps = normal_values(splits[5], (2, MODEL_WIDTH, ADAPTER_RANK), MODEL_WIDTH ** -0.5, 0.09375)
    adapter_up_maps = normal_values(splits[6], (2, ADAPTER_RANK, MODEL_WIDTH), ADAPTER_RANK ** -0.5, 0.75)
    shifted = draw_shifted(jax.random.fold_in(splits[8], 71), 0)
    return dict(normalized_input=normalized_input, frozen_queries=frozen_queries, frozen_keys=frozen_keys, frozen_values=frozen_values, output_gradient=output_gradient, adapter_down_maps=adapter_down_maps, adapter_up_maps=adapter_up_maps, shifted=shifted)


adapter_scale = 0.5

def group_backward(query_matrix, key_rows, value_matrix, upstream):
    factor = 1.0 / math.sqrt(query_matrix.shape[-1])
    scores = jnp.dot(query_matrix, key_rows.T, preferred_element_type=jnp.float32) * factor
    row_ids = lax.broadcasted_iota(jnp.int32, scores.shape, 0)
    column_ids = lax.broadcasted_iota(jnp.int32, scores.shape, 1)
    scores = jnp.where(column_ids <= row_ids, scores, -jnp.inf)
    row_top = lax.optimization_barrier(jnp.max(scores, axis=1, keepdims=True))
    weights = jnp.exp(scores - row_top)
    row_total = lax.optimization_barrier(jnp.sum(weights, axis=1, keepdims=True))
    attention = (weights / row_total).astype(jnp.bfloat16)
    output = jnp.dot(attention, value_matrix, preferred_element_type=jnp.float32)
    group_values = jnp.dot(attention.T, upstream, preferred_element_type=jnp.float32).astype(jnp.bfloat16)
    grad_attention = jnp.dot(upstream, value_matrix.T, preferred_element_type=jnp.float32)
    center = lax.optimization_barrier(jnp.sum(upstream.astype(jnp.float32) * output, axis=1, keepdims=True))
    grad_scores = (attention.astype(jnp.float32) * (grad_attention - center)).astype(jnp.bfloat16)
    group_queries = (jnp.dot(grad_scores, key_rows, preferred_element_type=jnp.float32) * factor).astype(jnp.bfloat16)
    return (group_queries, group_values)

def run_group(bundle):
    return group_backward(*bundle)

def head_backward(query_matrix, key_rows, value_matrix, upstream, flag):
    offset = flag * SHIFT
    head_width = query_matrix.shape[-1]
    blocks = tuple((jnp.roll(member, -offset, axis=0).reshape(-1, GROUP, head_width) for member in (query_matrix, key_rows, value_matrix, upstream)))
    grad_query, grad_value = lax.map(run_group, blocks)
    grad_query = jnp.roll(grad_query.reshape(-1, head_width), offset, axis=0)
    grad_value = jnp.roll(grad_value.reshape(-1, head_width), offset, axis=0)
    return (grad_query, grad_value)

def run_head(bundle):
    return head_backward(*bundle)

def to_heads(member):
    return member.reshape(BOOK_SLICES, SLICE_TOKENS, HEADS, HD).transpose(0, 2, 1, 3).reshape(BOOK_SLICES * HEADS, SLICE_TOKENS, HD)

def to_tokens(member):
    return member.reshape(BOOK_SLICES, HEADS, SLICE_TOKENS, HD).transpose(0, 2, 1, 3).reshape(BOOK_SLICES * SLICE_TOKENS, MODEL_WIDTH)

def reference(normalized_input, frozen_queries, frozen_keys, frozen_values, output_gradient, adapter_down_maps, adapter_up_maps, shifted):
    flattened_tokens = normalized_input.reshape(BOOK_SLICES * SLICE_TOKENS, MODEL_WIDTH)
    query_rank_rows = jnp.dot(flattened_tokens, adapter_down_maps[0], preferred_element_type=jnp.float32).astype(jnp.bfloat16)
    value_rank_rows = jnp.dot(flattened_tokens, adapter_down_maps[1], preferred_element_type=jnp.float32).astype(jnp.bfloat16)
    query_matrix = (frozen_queries.reshape(BOOK_SLICES * SLICE_TOKENS, MODEL_WIDTH).astype(jnp.float32) + adapter_scale * jnp.dot(query_rank_rows, adapter_up_maps[0], preferred_element_type=jnp.float32)).astype(jnp.bfloat16)
    value_matrix = (frozen_values.reshape(BOOK_SLICES * SLICE_TOKENS, MODEL_WIDTH).astype(jnp.float32) + adapter_scale * jnp.dot(value_rank_rows, adapter_up_maps[1], preferred_element_type=jnp.float32)).astype(jnp.bfloat16)
    head_flags = jnp.tile(shifted, BOOK_SLICES).astype(jnp.int32)
    grad_query, grad_value = lax.map(run_head, (to_heads(query_matrix), to_heads(frozen_keys), to_heads(value_matrix), to_heads(output_gradient), head_flags))
    query_gradient_rows = to_tokens(grad_query)
    value_gradient_rows = to_tokens(grad_value)
    query_up_map = adapter_scale * jnp.dot(query_rank_rows.T, query_gradient_rows, preferred_element_type=jnp.float32)
    value_up_map = adapter_scale * jnp.dot(value_rank_rows.T, value_gradient_rows, preferred_element_type=jnp.float32)
    query_backprop = jnp.dot(query_gradient_rows, adapter_up_maps[0].T, preferred_element_type=jnp.float32).astype(jnp.bfloat16)
    value_backprop = jnp.dot(value_gradient_rows, adapter_up_maps[1].T, preferred_element_type=jnp.float32).astype(jnp.bfloat16)
    query_down_map = adapter_scale * jnp.dot(flattened_tokens.T, query_backprop, preferred_element_type=jnp.float32)
    value_down_map = adapter_scale * jnp.dot(flattened_tokens.T, value_backprop, preferred_element_type=jnp.float32)
    return (jnp.stack([query_down_map, value_down_map]), jnp.stack([query_up_map, value_up_map]))
```

```python
import math

import jax
import jax.numpy as jnp
from jax import lax
from jax.experimental import pallas as pl
from jax.experimental.pallas import tpu as pltpu
from jax.sharding import PartitionSpec as P

HEADS = 32
HD = 128
GROUP = 1024
SHIFT = 512
RANK = 64
ROWS = 128
ZS, YS = 8, 4
MEMBERS = 8
RB = 256
BF16, F32 = jnp.bfloat16, jnp.float32

adapter_scale = 0.5

PLAIN_GROUPS = [[MEMBERS * g + i for i in range(MEMBERS)] for g in range(4)]
SHIFT_GROUPS = [[(MEMBERS * g + 4 + i) % HEADS for i in range(MEMBERS)] for g in range(4)]
Y_GROUPS = [[YS * z + y for y in range(YS)] for z in range(ZS)]


def z_shift(dz):
    return [(z * YS + y, ((z + dz) % ZS) * YS + y) for z in range(ZS) for y in range(YS)]


def exchange(member, axis, groups=None):
    return lax.all_to_all(member, axis, 0, 0, tiled=True, axis_index_groups=groups)


def prepare_kernel(heads, low_ref, fq_ref, fk_ref, fv_ref, go_ref, up_ref, out_ref, qb, vb, ub, sems):
    copies = []
    for j in range(MEMBERS):
        cols = pl.ds(pl.multiple_of(heads[j] * HD, HD), HD)
        row = [
            pltpu.make_async_copy(fq_ref.at[:, cols], qb.at[j], sems.at[j, 0]),
            pltpu.make_async_copy(fv_ref.at[:, cols], vb.at[j], sems.at[j, 1]),
            pltpu.make_async_copy(up_ref.at[:, cols], ub.at[j], sems.at[j, 2]),
            pltpu.make_async_copy(fk_ref.at[:, cols], out_ref.at[j, :, pl.ds(HD, HD)], sems.at[j, 3]),
            pltpu.make_async_copy(go_ref.at[:, cols], out_ref.at[j, :, pl.ds(3 * HD, HD)], sems.at[j, 4]),
        ]
        for copy in row:
            copy.start()
        copies.append(row)
    low = low_ref[...]
    for j in range(MEMBERS):
        for copy in copies[j][:3]:
            copy.wait()
        up = ub[j]
        raised_q = jnp.dot(low[:, :RANK], up[:RANK], preferred_element_type=F32)
        raised_v = jnp.dot(low[:, RANK:], up[RANK:], preferred_element_type=F32)
        out_ref[j, :, pl.ds(0, HD)] = (qb[j].astype(F32) + adapter_scale * raised_q).astype(BF16)
        out_ref[j, :, pl.ds(2 * HD, HD)] = (vb[j].astype(F32) + adapter_scale * raised_v).astype(BF16)
    for j in range(MEMBERS):
        for copy in copies[j][3:]:
            copy.wait()


def prepare(heads, low, fq, fk, fv, go, up):
    anywhere = pl.BlockSpec(memory_space=pl.ANY)
    return pl.pallas_call(
        prepare_kernel,
        out_shape=jax.ShapeDtypeStruct((MEMBERS, ROWS, 4 * HD), BF16),
        grid_spec=pltpu.PrefetchScalarGridSpec(
            num_scalar_prefetch=1,
            grid=(1,),
            in_specs=[pl.BlockSpec((ROWS, 2 * RANK), lambda i, h: (0, 0))] + [anywhere] * 5,
            out_specs=pl.BlockSpec((MEMBERS, ROWS, 4 * HD), lambda i, h: (0, 0, 0)),
            scratch_shapes=[pltpu.VMEM((MEMBERS, ROWS, HD), BF16)] * 3
            + [pltpu.SemaphoreType.DMA((MEMBERS, 5))],
        ),
        cost_estimate=pl.CostEstimate(flops=4 * 10**7, bytes_accessed=2 * 10**6, transcendentals=0),
    )(heads, low, fq, fk, fv, go, up)


def dot_t(a, b):
    return lax.dot_general(a, b, (((1,), (1,)), ((), ())), preferred_element_type=F32)


def dot_0(a, b):
    return lax.dot_general(a, b, (((0,), (0,)), ((), ())), preferred_element_type=F32)


def attention_kernel(first, head, x_ref, low_ref, up_ref, *refs):
    if first:
        back_ref, upgrad_ref, dv_acc, dq_buf = refs
    else:
        before_ref, back_ref, upgrad_ref, dv_acc, dq_buf = refs
    factor = 1.0 / math.sqrt(HD)
    bend = factor * math.log2(math.e)
    row_ids = lax.broadcasted_iota(jnp.int32, (RB, RB), 0)
    column_ids = lax.broadcasted_iota(jnp.int32, (RB, RB), 1)
    keep = column_ids <= row_ids
    for i in range(GROUP // RB):
        n = (i + 1) * RB
        rows = pl.ds(i * RB, RB)
        q = x_ref[rows, pl.ds(0, HD)]
        g = x_ref[rows, pl.ds(3 * HD, HD)]
        k = x_ref[pl.ds(0, n), pl.ds(HD, HD)]
        v = x_ref[pl.ds(0, n), pl.ds(2 * HD, HD)]
        scores = dot_t(q, k)
        last = jnp.where(keep, scores[:, i * RB :], -1e30)
        scores = last if i == 0 else jnp.concatenate([scores[:, : i * RB], last], axis=1)
        top = jnp.max(scores, axis=1, keepdims=True)
        weights = jnp.exp2((scores - top) * bend)
        total = jnp.sum(weights, axis=1, keepdims=True)
        attention = (weights * (1.0 / total)).astype(BF16)
        output = jnp.dot(attention, v, preferred_element_type=F32)
        grad_attention = dot_t(g, v)
        center = jnp.sum(g.astype(F32) * output, axis=1, keepdims=True)
        grad_scores = (attention.astype(F32) * (grad_attention - center)).astype(BF16)
        dq = jnp.dot(grad_scores, k, preferred_element_type=F32) * factor
        dq_buf[rows, :] = dq.astype(BF16)
        dv = dot_0(attention, g)
        if i:
            dv_acc[pl.ds(0, i * RB), :] += dv[: i * RB]
        dv_acc[rows, :] = dv[i * RB :]
    dq = dq_buf[...]
    dv = dv_acc[...].astype(BF16)
    low = low_ref[...]
    up = up_ref[...]
    upgrad_ref[pl.ds(0, RANK), :] = adapter_scale * dot_0(low[:, :RANK], dq)
    upgrad_ref[pl.ds(RANK, RANK), :] = adapter_scale * dot_0(low[:, RANK:], dv)
    lanes = lax.broadcasted_iota(jnp.int32, (GROUP, 2 * RANK), 1)
    back = jnp.where(lanes < RANK, dot_t(dq, up), dot_t(dv, up))
    if first:
        back_ref[...] = back
    else:
        back_ref[...] = (back + before_ref[...]).astype(BF16)


def attention_chunk(head, arrived, low, up, before=None):
    first = before is None
    whole = lambda shape: pl.BlockSpec(shape, lambda i, h: (0, 0))

    def body(*refs):
        attention_kernel(first, *refs)

    more = [] if first else [before]
    return pl.pallas_call(
        body,
        name="attention_first" if first else "attention_second",
        out_shape=(
            jax.ShapeDtypeStruct((GROUP, 2 * RANK), F32 if first else BF16),
            jax.ShapeDtypeStruct((2 * RANK, HD), F32),
        ),
        grid_spec=pltpu.PrefetchScalarGridSpec(
            num_scalar_prefetch=1,
            grid=(1,),
            in_specs=[
                whole((GROUP, 4 * HD)),
                whole((GROUP, 2 * RANK)),
                pl.BlockSpec((2 * RANK, HD), lambda i, h: (0, h[0])),
            ]
            + [whole((GROUP, 2 * RANK))] * len(more),
            out_specs=[whole((GROUP, 2 * RANK)), whole((2 * RANK, HD))],
            scratch_shapes=[pltpu.VMEM((GROUP, HD), F32), pltpu.VMEM((GROUP, HD), BF16)],
        ),
        compiler_params=pltpu.CompilerParams(vmem_limit_bytes=48 * 2**20),
        cost_estimate=pl.CostEstimate(flops=3 * 10**9, bytes_accessed=2 * 10**6, transcendentals=10**6),
    )(head, arrived.reshape(GROUP, 4 * HD), low, up, *more)


def per_device(
    normalized_input,
    frozen_queries,
    frozen_keys,
    frozen_values,
    output_gradient,
    adapter_down_maps,
    adapter_up_maps,
    shifted,
):
    token_rows = normalized_input[0]
    me = lax.axis_index("ulysses")
    z = me // YS
    even = z % 2 == 0
    up = adapter_up_maps.reshape(2 * RANK, HEADS * HD)

    flags = shifted.astype(jnp.int32)
    index = jnp.arange(HEADS, dtype=jnp.int32)
    before = jnp.sum(jnp.where(index[None, :] < index[:, None], flags[None, :], 0), axis=1)
    place = jnp.where(flags > 0, HEADS // 2 + before, index - before)
    order = jnp.sum(jnp.where(place[None, :] == index[:, None], index[None, :], 0), axis=1)

    low = jnp.einsum("jp,kpi->jki", token_rows, adapter_down_maps, preferred_element_type=F32)
    low = low.astype(BF16).reshape(ROWS, 2 * RANK)

    own = exchange(jnp.broadcast_to(low[None], (YS, ROWS, 2 * RANK)), "ulysses", Y_GROUPS)
    own = own.reshape(YS * ROWS, 2 * RANK)
    later = lax.ppermute(own, "ulysses", z_shift(-1))
    earlier = lax.ppermute(own, "ulysses", z_shift(1))
    leading = jnp.concatenate([own, later], axis=0)
    trailing = jnp.concatenate([earlier, own], axis=0)
    low_plain = jnp.where(even, leading, trailing)
    low_shift = jnp.where(even, trailing, leading)

    seats = (me % MEMBERS, (me + 4) % MEMBERS)
    back, upgrads, held = [], [], []
    for part in range(2):
        groups = (PLAIN_GROUPS, SHIFT_GROUPS)[part]
        lows = (low_plain, low_shift)[part]
        partial = None
        for c in (2 * part, 2 * part + 1):
            heads = order[c * MEMBERS : (c + 1) * MEMBERS]
            sent = prepare(
                heads, low, frozen_queries[0], frozen_keys[0], frozen_values[0], output_gradient[0], up
            )
            arrived = exchange(sent, "ulysses", groups)
            head = lax.dynamic_slice_in_dim(heads, seats[part], 1)
            partial, upgrad = attention_chunk(head, arrived, lows, up, partial)
            upgrads.append(upgrad)
            held.append(head)
        summed = exchange(partial.reshape(MEMBERS, ROWS, 2 * RANK), "ulysses", groups)
        back.append(jnp.sum(summed.astype(F32), axis=0))
    back_rank = (back[0] + back[1]).astype(BF16)

    down = adapter_scale * jnp.einsum("tc,tk->ck", token_rows, back_rank, preferred_element_type=F32)
    down = down.astype(BF16).reshape(HEADS, 8, 16, 2 * RANK).transpose(1, 0, 2, 3)
    ups = jnp.stack(upgrads).astype(BF16).reshape(4, 8, 16, HD).transpose(1, 0, 2, 3)
    both = jnp.concatenate([down, ups], axis=1)
    both = jnp.sum(exchange(both, "dp").astype(F32), axis=0)
    heads = jnp.concatenate(held)
    slots = jnp.sum(
        jnp.where((heads[None, :] == index[:, None])[:, :, None, None], both[None, HEADS:], 0.0), axis=1
    )
    both = jnp.concatenate([both[:HEADS], slots], axis=1).astype(BF16)
    both = jnp.sum(exchange(both, "ulysses").astype(F32), axis=0)
    both = exchange(jnp.broadcast_to(both[None], (8, 32, HD)), "dp")
    grad_down = both[:, :16].reshape(HD, 2, RANK).transpose(1, 0, 2)
    grad_up = both[:, 16:].reshape(2, RANK, HD)
    return (grad_down, grad_up)


def solution(mesh):
    rows = P("dp", "ulysses", None)
    in_specs = (rows, rows, rows, rows, rows, P(), P(), P())
    out_specs = (P(None, "ulysses", None), P(None, None, "ulysses"))
    return jax.shard_map(
        per_device, mesh=mesh, in_specs=in_specs, out_specs=out_specs, check_vma=False
    )
```

```python
import math

import jax
import jax.numpy as jnp
import numpy as np
from jax import lax
from jax.experimental import pallas as pl
from jax.experimental.pallas import tpu as pltpu
from jax.sharding import PartitionSpec as P

HEADS = 32
HD = 128
WIDTH = HEADS * HD
GROUP = 1024
PLANE = 512
RANK = 64
BOTH = 2 * RANK
ROWS = 128
ZS, YS = 8, 4
XS, CS = 4, 2
SLICES = XS * CS
MEMBERS = 8
PIECE = 16
RB = 256
BF16, F32 = jnp.bfloat16, jnp.float32

adapter_scale = 0.5

PLAIN_GROUPS = [[MEMBERS * g + i for i in range(MEMBERS)] for g in range(4)]
SHIFT_GROUPS = [[(MEMBERS * g + 4 + i) % HEADS for i in range(MEMBERS)] for g in range(4)]
PLAIN_SWAP = [(u, u ^ 4) for u in range(HEADS)]
CORE_SWAP = [(d, d ^ 1) for d in range(SLICES)]
ANYWHERE = pl.BlockSpec(memory_space=pl.ANY)
SCALARS = pl.BlockSpec(memory_space=pltpu.SMEM)

SPOTS = np.array(
    [[u % 4, u % 8, (u + 4) % 8, PLANE * (u // 4 % 2), PLANE * (1 - u // 4 % 2), 0, 0, 0] for u in range(HEADS)],
    np.int32,
)
SPOT_Y, SPOT_PLAIN, SPOT_SHIFT, SPOT_OWN_PLAIN, SPOT_OWN_SHIFT = range(5)


def z_shift(dz):
    return [(z * YS + y, ((z + dz) % ZS) * YS + y) for z in range(ZS) for y in range(YS)]


def y_shift(dy):
    return [(z * YS + y, z * YS + (y + dy) % YS) for z in range(ZS) for y in range(YS)]


def x_shift(dx):
    return [(x * CS + c, ((x + dx) % XS) * CS + c) for x in range(XS) for c in range(CS)]


def exchange(member, axis, groups=None):
    return lax.all_to_all(member, axis, 0, 0, tiled=True, axis_index_groups=groups)


def after(values, *others):
    return lax.optimization_barrier((values, others))[0]


def block(shape):
    return pl.BlockSpec(shape, lambda i, *s: (0,) * len(shape))


def dot_t(a, b):
    return lax.dot_general(a, b, (((1,), (1,)), ((), ())), preferred_element_type=F32)


def dot_0(a, b):
    return lax.dot_general(a, b, (((0,), (0,)), ((), ())), preferred_element_type=F32)


def call(kernel, name, scalars, in_specs, out_specs, out_shape, scratch, cost, vmem=40):
    return pl.pallas_call(
        kernel,
        name=name,
        out_shape=out_shape,
        grid_spec=pltpu.PrefetchScalarGridSpec(
            num_scalar_prefetch=scalars,
            grid=(1,),
            in_specs=in_specs,
            out_specs=out_specs,
            scratch_shapes=scratch,
        ),
        compiler_params=pltpu.CompilerParams(vmem_limit_bytes=vmem * 2**20),
        cost_estimate=pl.CostEstimate(flops=cost[0], bytes_accessed=cost[1], transcendentals=0),
    )


def prepare_first_kernel(flags, fk_ref, go_ref, out_ref, order, sems):
    def place(h, ones):
        flag = flags[h]
        order[jnp.where(flag > 0, HEADS // 2 + ones, h - ones)] = h
        return ones + jnp.where(flag > 0, 1, 0)

    lax.fori_loop(0, HEADS, place, 0, unroll=True)
    copies = []
    for p in range(2 * MEMBERS):
        item, seat = divmod(p, MEMBERS)
        cols = pl.ds(pl.multiple_of(order[p] * HD, HD), HD)
        for t, ref in enumerate((fk_ref, go_ref)):
            spot = out_ref.at[seat, :, pl.ds((2 * item + t) * HD, HD)]
            copies.append(pltpu.make_async_copy(ref.at[:, cols], spot, sems.at[p, t]))
            copies[-1].start()
    for copy in copies:
        copy.wait()


def prepare_first(flags, fk, go):
    return call(
        prepare_first_kernel,
        "prepare_first",
        1,
        [ANYWHERE] * 2,
        [block((MEMBERS, ROWS, 4 * HD)), SCALARS],
        (jax.ShapeDtypeStruct((MEMBERS, ROWS, 4 * HD), BF16), jax.ShapeDtypeStruct((HEADS,), jnp.int32)),
        [pltpu.SemaphoreType.DMA((2 * MEMBERS, 2))],
        (0, 2 * 10**6),
    )(flags, fk, go)


def prepare_rest_kernel(order, x_ref, down_ref, fq_ref, fv_ref, up_ref, fk_ref, go_ref, *refs):
    a_ref, b_ref, c_ref, low_ref, sems = refs
    copies = []
    for p in range(2 * MEMBERS):
        item, seat = divmod(p, MEMBERS)
        cols = pl.ds(pl.multiple_of(order[2 * MEMBERS + p] * HD, HD), HD)
        for t, ref in ((1, fk_ref), (3, go_ref)):
            spot = (b_ref, c_ref)[item].at[seat, :, pl.ds(t * HD, HD)]
            copies.append(pltpu.make_async_copy(ref.at[:, cols], spot, sems.at[p, t // 2]))
            copies[-1].start()
    low = dot_t(x_ref[...], down_ref[...]).astype(BF16)
    low_ref[...] = low
    for p in range(4 * MEMBERS):
        item, seat = divmod(p, MEMBERS)
        cols = pl.ds(pl.multiple_of(order[p] * HD, HD), HD)
        raised_q = jnp.dot(low[:, :RANK], up_ref[pl.ds(0, RANK), cols], preferred_element_type=F32)
        raised_v = jnp.dot(low[:, RANK:], up_ref[pl.ds(RANK, RANK), cols], preferred_element_type=F32)
        q = (fq_ref[:, cols].astype(F32) + adapter_scale * raised_q).astype(BF16)
        v = (fv_ref[:, cols].astype(F32) + adapter_scale * raised_v).astype(BF16)
        if item < 2:
            a_ref[seat, :, pl.ds(2 * item * HD, HD)] = q
            a_ref[seat, :, pl.ds((2 * item + 1) * HD, HD)] = v
        else:
            out = (b_ref, c_ref)[item - 2]
            out[seat, :, pl.ds(0, HD)] = q
            out[seat, :, pl.ds(2 * HD, HD)] = v
    for copy in copies:
        copy.wait()


def prepare_rest(order, x, down, fq, fv, up, fk, go):
    chunk = jax.ShapeDtypeStruct((MEMBERS, ROWS, 4 * HD), BF16)
    return call(
        prepare_rest_kernel,
        "prepare_rest",
        1,
        [block((ROWS, WIDTH)), block((BOTH, WIDTH))]
        + [block((ROWS, WIDTH))] * 2
        + [block((BOTH, WIDTH))]
        + [ANYWHERE] * 2,
        [block((MEMBERS, ROWS, 4 * HD))] * 3 + [block((ROWS, BOTH))],
        (chunk,) * 3 + (jax.ShapeDtypeStruct((ROWS, BOTH), BF16),),
        [pltpu.SemaphoreType.DMA((2 * MEMBERS, 2))],
        (4 * 10**9, 10 * 10**6),
    )(order, x, down, fq, fv, up, fk, go)


def turn_kernel(spot, x_ref, out_ref):
    x, core = spot[0] // CS, spot[0] % CS
    for u in range(HEADS):
        turned = x_ref[:, pl.ds(u * HD, HD)].T
        for d in range(SLICES):
            other = (core + d) % CS
            step = (d // CS - x + XS) % XS
            out_ref[other, step, pl.ds(u * PIECE, PIECE), :] = turned[d * PIECE : (d + 1) * PIECE]


def turn(spot, x):
    shape = (CS, XS, HEADS * PIECE, ROWS)
    return call(
        turn_kernel,
        "turn_input",
        1,
        [block(x.shape)],
        block(shape),
        jax.ShapeDtypeStruct(shape, BF16),
        [],
        (10**9, 2 * 10**6),
    )(spot, x)


def attention_kernel(kind, order, spot, q_ref, k_ref, v_ref, g_ref, up_ref, *refs):
    if kind == "first":
        back_ref, grads_ref, dv_acc = refs
    elif kind == "plain":
        before_ref, mine_ref, theirs_ref, grads_ref, dv_acc, sum_ref = refs
    else:
        before_ref, mine_ref, theirs_ref, back_ref, grads_ref, dv_acc, sum_ref = refs
    factor = 1.0 / math.sqrt(HD)
    bend = factor * math.log2(math.e)
    row_ids = lax.broadcasted_iota(jnp.int32, (RB, RB), 0)
    column_ids = lax.broadcasted_iota(jnp.int32, (RB, RB), 1)
    keep = column_ids <= row_ids
    for i in range(GROUP // RB):
        n = (i + 1) * RB
        rows = pl.ds(i * RB, RB)
        q = q_ref[rows, :]
        g = g_ref[rows, :]
        k = k_ref[pl.ds(0, n), :]
        v = v_ref[pl.ds(0, n), :]
        scores = dot_t(q, k)
        last = jnp.where(keep, scores[:, i * RB :], -1e30)
        scores = last if i == 0 else jnp.concatenate([scores[:, : i * RB], last], axis=1)
        top = jnp.max(scores, axis=1, keepdims=True)
        weights = jnp.exp2((scores - top) * bend)
        total = jnp.sum(weights, axis=1, keepdims=True)
        attention = (weights * (1.0 / total)).astype(BF16)
        output = jnp.dot(attention, v, preferred_element_type=F32)
        grad_attention = dot_t(g, v)
        center = jnp.sum(g.astype(F32) * output, axis=1, keepdims=True)
        grad_scores = (attention.astype(F32) * (grad_attention - center)).astype(BF16)
        dq = jnp.dot(grad_scores, k, preferred_element_type=F32) * factor
        grads_ref[rows, pl.ds(0, HD)] = dq.astype(BF16)
        dv = dot_0(attention, g)
        if i:
            dv_acc[pl.ds(0, i * RB), :] += dv[: i * RB]
        dv_acc[rows, :] = dv[i * RB :]
    dq = grads_ref[:, pl.ds(0, HD)]
    dv = dv_acc[...].astype(BF16)
    grads_ref[:, pl.ds(HD, HD)] = dv
    up = up_ref[...]
    lanes = lax.broadcasted_iota(jnp.int32, (GROUP, BOTH), 1)
    back = jnp.where(lanes < RANK, dot_t(dq, up), dot_t(dv, up))
    if kind == "first":
        back_ref[...] = back
        return
    sum_ref[...] = back + before_ref[...]
    if kind == "plain":
        own = pl.multiple_of(spot[SPOT_OWN_PLAIN], PLANE)
        mine_ref[...] = sum_ref[pl.ds(own, PLANE), :]
        theirs_ref[...] = sum_ref[pl.ds(PLANE - own, PLANE), :].astype(BF16)
    else:
        own = pl.multiple_of(spot[SPOT_OWN_SHIFT], PLANE)
        sum_ref[pl.ds(own, PLANE), :] += mine_ref[...] + theirs_ref[...].astype(F32)
        back_ref[...] = sum_ref[...].astype(BF16)


def attention_item(kind, item, order, spot, members, up, *more):
    arrays = [array.reshape(GROUP, 4 * HD) for array, _ in members]
    columns = [pl.BlockSpec((GROUP, HD), lambda i, *s, column=column: (0, column)) for _, column in members]
    seat = SPOT_PLAIN if item < 2 else SPOT_SHIFT
    shapes = {
        "first": [((GROUP, BOTH), F32)],
        "plain": [((PLANE, BOTH), F32), ((PLANE, BOTH), BF16)],
        "shifted": [((GROUP, BOTH), BF16)],
    }[kind] + [((GROUP, 2 * HD), BF16)]
    scratch = [pltpu.VMEM((GROUP, HD), F32)]
    if kind != "first":
        scratch.append(pltpu.VMEM((GROUP, BOTH), F32))

    def body(*refs):
        attention_kernel(kind, *refs)

    return call(
        body,
        "attention_" + kind,
        2,
        columns
        + [pl.BlockSpec((BOTH, HD), lambda i, order, spot: (0, order[item * MEMBERS + spot[seat]]))]
        + [block(array.shape) for array in more],
        [block(shape) for shape, _ in shapes],
        [jax.ShapeDtypeStruct(*shape) for shape in shapes],
        scratch,
        (4 * 10**9, 3 * 10**6),
    )(order, spot, *arrays, up, *more)


def up_gradient_kernel(spot, own_ref, later_ref, earlier_ref, *refs):
    out_ref, low_a, low_b = refs[-3:]
    y = spot[SPOT_Y]

    def fill(low, first, second):
        for half, ref in enumerate((first, second)):
            for s in range(YS):
                low[pl.ds(half * PLANE + s * ROWS, ROWS), :] = ref[(y - s + YS) % YS]

    @pl.when(spot[SPOT_OWN_PLAIN] == 0)
    def _():
        fill(low_a, own_ref, later_ref)
        fill(low_b, earlier_ref, own_ref)

    @pl.when(spot[SPOT_OWN_PLAIN] != 0)
    def _():
        fill(low_a, earlier_ref, own_ref)
        fill(low_b, own_ref, later_ref)

    for item, grads in enumerate(refs[:4]):
        low = (low_a, low_b)[item // 2][...]
        for m in range(2):
            part = adapter_scale * dot_0(low[:, m * RANK : (m + 1) * RANK], grads[:, pl.ds(m * HD, HD)])
            part = part.astype(BF16)
            for e in range(RANK // PIECE):
                d = m * (RANK // PIECE) + e
                out_ref[d, pl.ds(item * PIECE, PIECE), :] = part[e * PIECE : (e + 1) * PIECE]


def up_gradients(spot, own, later, earlier, grads):
    shape = (SLICES, 4 * PIECE, HD)
    return call(
        up_gradient_kernel,
        "up_gradients",
        1,
        [block((YS, ROWS, BOTH))] * 3 + [block((GROUP, 2 * HD))] * 4,
        block(shape),
        jax.ShapeDtypeStruct(shape, BF16),
        [pltpu.VMEM((GROUP, BOTH), BF16)] * 2,
        (2 * 10**9, 3 * 10**6),
    )(spot, own, later, earlier, *grads)


def gather_kernel(summed_ref, ups_ref, out_ref):
    back = jnp.sum(summed_ref[...].astype(F32), axis=0).astype(BF16)
    for d in range(SLICES):
        out_ref[d, pl.ds(0, ROWS), :] = back
    out_ref[:, pl.ds(ROWS, 4 * PIECE), :] = ups_ref[...]


def gather_parts(summed, ups):
    shape = (SLICES, ROWS + 4 * PIECE, HD)
    return call(
        gather_kernel,
        "gather_parts",
        0,
        [block(summed.shape), block(ups.shape)],
        block(shape),
        jax.ShapeDtypeStruct(shape, BF16),
        [],
        (10**7, 10**6),
    )(summed, ups)


def merge_kernel(order, spot, place, both_ref, *refs):
    x_refs, out_ref = refs[:-1], refs[-1]
    x, core = place[0] // CS, place[0] % CS
    total = jnp.zeros((HEADS * PIECE, BOTH), F32)
    for dx in range(XS):
        for other in range(CS):
            s = (x - dx + XS) % XS * CS + (core + other) % CS
            back = both_ref[s, pl.ds(0, ROWS), :]
            total += jnp.dot(x_refs[dx][other], back, preferred_element_type=F32)
    total = (adapter_scale * total).astype(BF16)
    for u in range(HEADS):
        out_ref[u, pl.ds(0, PIECE), :] = total[u * PIECE : (u + 1) * PIECE]
        out_ref[u, pl.ds(PIECE, PIECE), :] = jnp.zeros((PIECE, HD), BF16)
    ups = jnp.sum(both_ref[:, pl.ds(ROWS, 4 * PIECE), :].astype(F32), axis=0).astype(BF16)
    for item in range(4):
        seat = spot[SPOT_PLAIN if item < 2 else SPOT_SHIFT]
        head = order[item * MEMBERS + seat]
        out_ref[head, pl.ds(PIECE, PIECE), :] = ups[item * PIECE : (item + 1) * PIECE]


def merge(order, spot, place, both, pieces):
    shape = (HEADS, 2 * PIECE, HD)
    return call(
        merge_kernel,
        "merge_gradients",
        3,
        [block(both.shape)] + [block(piece.shape) for piece in pieces],
        block(shape),
        jax.ShapeDtypeStruct(shape, BF16),
        [],
        (2 * 10**8, 2 * 10**6),
    )(order, spot, place, both, *pieces)


def spread_kernel(in_ref, out_ref):
    total = jnp.sum(in_ref[...].astype(F32), axis=0)
    for d in range(SLICES):
        out_ref[d] = total


def spread(both):
    shape = (SLICES, 2 * PIECE, HD)
    return call(
        spread_kernel,
        "spread_sums",
        0,
        [block(both.shape)],
        block(shape),
        jax.ShapeDtypeStruct(shape, F32),
        [],
        (10**6, 10**6),
    )(both)


def finish_kernel(in_ref, down_ref, up_ref):
    down = in_ref[:, pl.ds(0, PIECE), :].reshape(HD, BOTH).T
    up = in_ref[:, pl.ds(PIECE, PIECE), :].reshape(BOTH, HD)
    for m in range(2):
        down_ref[m] = down[m * RANK : (m + 1) * RANK]
        up_ref[m] = up[m * RANK : (m + 1) * RANK]


def finish(both):
    shape = (2, RANK, HD)
    return call(
        finish_kernel,
        "finish",
        0,
        [block(both.shape)],
        [block(shape)] * 2,
        [jax.ShapeDtypeStruct(shape, F32)] * 2,
        [],
        (10**6, 10**6),
    )(both)


def per_device(
    normalized_input,
    frozen_queries,
    frozen_keys,
    frozen_values,
    output_gradient,
    adapter_down_maps,
    adapter_up_maps,
    shifted,
):
    tokens = normalized_input[0]
    spot = lax.dynamic_slice(jnp.asarray(SPOTS), (lax.axis_index("ulysses"), 0), (1, 8)).reshape(8)
    place = lax.axis_index("dp").reshape(1)
    up = adapter_up_maps.reshape(BOTH, WIDTH)
    down = adapter_down_maps.transpose(0, 2, 1).reshape(BOTH, WIDTH)

    sent_a, order = prepare_first(shifted.astype(jnp.int32), frozen_keys[0], output_gradient[0])
    keys_a = exchange(sent_a, "ulysses", PLAIN_GROUPS)
    sent_b, sent_c, sent_d, low = prepare_rest(
        order, tokens, down, frozen_queries[0], frozen_values[0], up, frozen_keys[0], output_gradient[0]
    )

    sent_b, keys_a, low, tokens = after((sent_b, keys_a, low, tokens))
    queries_b = exchange(sent_b, "ulysses", PLAIN_GROUPS)
    own = jnp.stack([low] + [lax.ppermute(low, "ulysses", y_shift(dy)) for dy in (1, 2, 3)])
    turned = turn(place, tokens)
    other = lax.ppermute(turned[1], "dp", CORE_SWAP)

    sent_c, keys_a, queries_b, own, turned, other = after((sent_c, keys_a, queries_b, own, turned, other))
    arrived_c = exchange(sent_c, "ulysses", SHIFT_GROUPS)
    later = lax.ppermute(own, "ulysses", z_shift(-1))
    earlier = lax.ppermute(own, "ulysses", z_shift(1))
    partial, grads_0 = attention_item(
        "first", 0, order, spot, [(queries_b, 0), (keys_a, 0), (queries_b, 1), (keys_a, 1)], up
    )
    mine, theirs, grads_1 = attention_item(
        "plain", 1, order, spot, [(queries_b, 2), (keys_a, 2), (queries_b, 3), (keys_a, 3)], up, partial
    )

    sent_d, arrived_c, later, earlier, theirs, turned, other = after(
        (sent_d, arrived_c, later, earlier, theirs, turned, other)
    )
    arrived_d = exchange(sent_d, "ulysses", SHIFT_GROUPS)
    theirs = lax.ppermute(theirs, "ulysses", PLAIN_SWAP)
    pieces = [jnp.stack([turned[0, dx], other[dx]]) for dx in range(XS)]
    pieces = pieces[:1] + [lax.ppermute(pieces[dx], "dp", x_shift(dx)) for dx in (1, 2, 3)]
    partial, grads_2 = attention_item("first", 2, order, spot, [(arrived_c, t) for t in range(4)], up)

    arrived_d, theirs, pieces = after((arrived_d, theirs, pieces), partial)
    partial, grads_3 = attention_item(
        "shifted", 3, order, spot, [(arrived_d, t) for t in range(4)], up, partial, mine, theirs
    )
    summed = exchange(partial.reshape(MEMBERS, ROWS, BOTH), "ulysses", SHIFT_GROUPS)
    ups = up_gradients(spot, own, later, earlier, (grads_0, grads_1, grads_2, grads_3))
    both = exchange(gather_parts(summed, ups), "dp")
    both = exchange(merge(order, spot, place, both, pieces), "ulysses")
    both = exchange(spread(both), "dp")
    grad_down, grad_up = finish(both)
    return (grad_down.transpose(0, 2, 1), grad_up)


def solution(mesh):
    rows = P("dp", "ulysses", None)
    in_specs = (rows, rows, rows, rows, rows, P(), P(), P())
    out_specs = (P(None, "ulysses", None), P(None, None, "ulysses"))
    return jax.shard_map(
        per_device, mesh=mesh, in_specs=in_specs, out_specs=out_specs, check_vma=False
    )
```

```python
import math

import jax
import jax.numpy as jnp
import numpy as np
from jax import lax
from jax.experimental import pallas as pl
from jax.experimental.pallas import tpu as pltpu
from jax.sharding import PartitionSpec as P

HEADS = 32
HD = 128
WIDTH = HEADS * HD
GROUP = 1024
PLANE = 512
RANK = 64
BOTH = 2 * RANK
ROWS = 128
ZS, YS = 8, 4
XS, CS = 4, 2
SLICES = XS * CS
MEMBERS = 8
PIECE = 16
RB = 256
BF16, F32 = jnp.bfloat16, jnp.float32

adapter_scale = 0.5

PLAIN_GROUPS = [[MEMBERS * g + i for i in range(MEMBERS)] for g in range(4)]
SHIFT_GROUPS = [[(MEMBERS * g + 4 + i) % HEADS for i in range(MEMBERS)] for g in range(4)]
PLAIN_SWAP = [(u, u ^ 4) for u in range(HEADS)]
CORE_SWAP = [(d, d ^ 1) for d in range(SLICES)]
ANYWHERE = pl.BlockSpec(memory_space=pltpu.HBM)
SCALARS = pl.BlockSpec(memory_space=pltpu.SMEM)

SPOTS = np.array(
    [[u % 4, u % 8, (u + 4) % 8, PLANE * (u // 4 % 2), PLANE * (1 - u // 4 % 2), 0, 0, 0] for u in range(HEADS)],
    np.int32,
)
SPOT_Y, SPOT_PLAIN, SPOT_SHIFT, SPOT_OWN_PLAIN, SPOT_OWN_SHIFT = range(5)


def z_shift(dz):
    return [(z * YS + y, ((z + dz) % ZS) * YS + y) for z in range(ZS) for y in range(YS)]


def y_shift(dy):
    return [(z * YS + y, z * YS + (y + dy) % YS) for z in range(ZS) for y in range(YS)]


def x_shift(dx):
    return [(x * CS + c, ((x + dx) % XS) * CS + c) for x in range(XS) for c in range(CS)]


def exchange(member, axis, groups=None):
    return lax.all_to_all(member, axis, 0, 0, tiled=True, axis_index_groups=groups)


def after(values, *others):
    return lax.optimization_barrier((values, others))[0]


def block(shape):
    return pl.BlockSpec(shape, lambda i, *s: (0,) * len(shape))


def dot_t(a, b):
    return lax.dot_general(a, b, (((1,), (1,)), ((), ())), preferred_element_type=F32)


def dot_0(a, b):
    return lax.dot_general(a, b, (((0,), (0,)), ((), ())), preferred_element_type=F32)


def call(kernel, name, scalars, in_specs, out_specs, out_shape, scratch, cost):
    return pl.pallas_call(
        kernel,
        name=name,
        out_shape=out_shape,
        grid_spec=pltpu.PrefetchScalarGridSpec(
            num_scalar_prefetch=scalars,
            grid=(1,),
            in_specs=in_specs,
            out_specs=out_specs,
            scratch_shapes=scratch,
        ),
        cost_estimate=pl.CostEstimate(flops=cost[0], bytes_accessed=cost[1], transcendentals=0),
    )


def order_heads(flags, order):
    def place(h, ones):
        flag = flags[h]
        order[jnp.where(flag > 0, HEADS // 2 + ones, h - ones)] = h
        return ones + jnp.where(flag > 0, 1, 0)

    lax.fori_loop(0, HEADS, place, 0, unroll=True)


def fetch_heads(first, order, fq_ref, fk_ref, fv_ref, go_ref, out_ref, q_in, v_in, sems):
    copies = []
    for p in range(2 * MEMBERS):
        item, seat = divmod(p, MEMBERS)
        cols = pl.ds(pl.multiple_of(order[first + p] * HD, HD), HD)
        places = (
            (fq_ref, q_in.at[p]),
            (fv_ref, v_in.at[p]),
            (fk_ref, out_ref.at[seat, :, pl.ds((4 * item + 1) * HD, HD)]),
            (go_ref, out_ref.at[seat, :, pl.ds((4 * item + 3) * HD, HD)]),
        )
        row = [
            pltpu.make_async_copy(ref.at[:, cols], spot, sems.at[p, t])
            for t, (ref, spot) in enumerate(places)
        ]
        for copy in row:
            copy.start()
        copies.append(row)
    return copies


def raise_heads(first, order, low, up_ref, copies, q_in, v_in, out_ref):
    for p in range(2 * MEMBERS):
        item, seat = divmod(p, MEMBERS)
        cols = pl.ds(pl.multiple_of(order[first + p] * HD, HD), HD)
        raised_q = jnp.dot(low[:, :RANK], up_ref[pl.ds(0, RANK), cols], preferred_element_type=F32)
        raised_v = jnp.dot(low[:, RANK:], up_ref[pl.ds(RANK, RANK), cols], preferred_element_type=F32)
        copies[p][0].wait()
        copies[p][1].wait()
        q = (q_in[p].astype(F32) + adapter_scale * raised_q).astype(BF16)
        v = (v_in[p].astype(F32) + adapter_scale * raised_v).astype(BF16)
        out_ref[seat, :, pl.ds(4 * item * HD, HD)] = q
        out_ref[seat, :, pl.ds((4 * item + 2) * HD, HD)] = v
    for row in copies:
        row[2].wait()
        row[3].wait()


def prepare_plain_kernel(flags, x_hbm, down_hbm, up_hbm, *refs):
    frozen, (out_ref, order, low_ref, x_in, down_in, up_in, q_in, v_in, sems, whole_sems) = refs[:4], refs[4:]
    wholes = [
        pltpu.make_async_copy(source, spot, whole_sems.at[t])
        for t, (source, spot) in enumerate(((x_hbm, x_in), (down_hbm, down_in), (up_hbm, up_in)))
    ]
    for copy in wholes:
        copy.start()
    order_heads(flags, order)
    copies = fetch_heads(0, order, *frozen, out_ref, q_in, v_in, sems)
    wholes[0].wait()
    wholes[1].wait()
    low = dot_t(x_in[...], down_in[...]).astype(BF16)
    low_ref[...] = low
    wholes[2].wait()
    raise_heads(0, order, low, up_in, copies, q_in, v_in, out_ref)


HEAD_SCRATCH = [pltpu.VMEM((2 * MEMBERS, ROWS, HD), BF16)] * 2 + [pltpu.SemaphoreType.DMA((2 * MEMBERS, 4))]


def prepare_plain(flags, x, down, up, frozen):
    return call(
        prepare_plain_kernel,
        "prepare_plain",
        1,
        [ANYWHERE] * 7,
        [block((MEMBERS, ROWS, 8 * HD)), SCALARS, block((ROWS, BOTH))],
        (
            jax.ShapeDtypeStruct((MEMBERS, ROWS, 8 * HD), BF16),
            jax.ShapeDtypeStruct((HEADS,), jnp.int32),
            jax.ShapeDtypeStruct((ROWS, BOTH), BF16),
        ),
        [pltpu.VMEM((ROWS, WIDTH), BF16), pltpu.VMEM((BOTH, WIDTH), BF16), pltpu.VMEM((BOTH, WIDTH), BF16)]
        + HEAD_SCRATCH
        + [pltpu.SemaphoreType.DMA((3,))],
        (10**9, 8 * 10**6),
    )(flags, x, down, up, *frozen)


def prepare_shifted_kernel(order, low_ref, up_ref, *refs):
    frozen, (out_ref, q_in, v_in, sems) = refs[:4], refs[4:]
    copies = fetch_heads(2 * MEMBERS, order, *frozen, out_ref, q_in, v_in, sems)
    raise_heads(2 * MEMBERS, order, low_ref[...], up_ref, copies, q_in, v_in, out_ref)


def prepare_shifted(order, low, up, frozen):
    return call(
        prepare_shifted_kernel,
        "prepare_shifted",
        1,
        [block((ROWS, BOTH)), block((BOTH, WIDTH))] + [ANYWHERE] * 4,
        block((MEMBERS, ROWS, 8 * HD)),
        jax.ShapeDtypeStruct((MEMBERS, ROWS, 8 * HD), BF16),
        HEAD_SCRATCH,
        (10**9, 8 * 10**6),
    )(order, low, up, *frozen)


def turn_kernel(spot, x_ref, out_ref):
    x, core = spot[0] // CS, spot[0] % CS
    for u in range(HEADS):
        turned = x_ref[:, pl.ds(u * HD, HD)].T
        for d in range(SLICES):
            other = (core + d) % CS
            step = (d // CS - x + XS) % XS
            out_ref[other, step, pl.ds(u * PIECE, PIECE), :] = turned[d * PIECE : (d + 1) * PIECE]


def turn(spot, x):
    shape = (CS, XS, HEADS * PIECE, ROWS)
    return call(
        turn_kernel,
        "turn_input",
        1,
        [block(x.shape)],
        block(shape),
        jax.ShapeDtypeStruct(shape, BF16),
        [],
        (10**9, 2 * 10**6),
    )(spot, x)


def attention_kernel(kind, order, spot, q_ref, k_ref, v_ref, g_ref, up_ref, *refs):
    if kind == "first":
        back_ref, grads_ref, dv_acc = refs
    elif kind == "plain":
        before_ref, mine_ref, theirs_ref, grads_ref, dv_acc, sum_ref = refs
    else:
        before_ref, mine_ref, theirs_ref, back_ref, grads_ref, dv_acc, sum_ref = refs
    factor = 1.0 / math.sqrt(HD)
    bend = factor * math.log2(math.e)
    row_ids = lax.broadcasted_iota(jnp.int32, (RB, RB), 0)
    column_ids = lax.broadcasted_iota(jnp.int32, (RB, RB), 1)
    keep = column_ids <= row_ids
    for i in range(GROUP // RB):
        n = (i + 1) * RB
        rows = pl.ds(i * RB, RB)
        q = q_ref[rows, :]
        g = g_ref[rows, :]
        k = k_ref[pl.ds(0, n), :]
        v = v_ref[pl.ds(0, n), :]
        scores = dot_t(q, k)
        last = jnp.where(keep, scores[:, i * RB :], -1e30)
        scores = last if i == 0 else jnp.concatenate([scores[:, : i * RB], last], axis=1)
        top = jnp.max(scores, axis=1, keepdims=True)
        weights = jnp.exp2((scores - top) * bend)
        total = jnp.sum(weights, axis=1, keepdims=True)
        attention = (weights * (1.0 / total)).astype(BF16)
        output = jnp.dot(attention, v, preferred_element_type=F32)
        grad_attention = dot_t(g, v)
        center = jnp.sum(g.astype(F32) * output, axis=1, keepdims=True)
        grad_scores = (attention.astype(F32) * (grad_attention - center)).astype(BF16)
        dq = jnp.dot(grad_scores, k, preferred_element_type=F32) * factor
        grads_ref[rows, pl.ds(0, HD)] = dq.astype(BF16)
        dv = dot_0(attention, g)
        if i:
            dv_acc[pl.ds(0, i * RB), :] += dv[: i * RB]
        dv_acc[rows, :] = dv[i * RB :]
    dq = grads_ref[:, pl.ds(0, HD)]
    dv = dv_acc[...].astype(BF16)
    grads_ref[:, pl.ds(HD, HD)] = dv
    up = up_ref[...]
    lanes = lax.broadcasted_iota(jnp.int32, (GROUP, BOTH), 1)
    back = jnp.where(lanes < RANK, dot_t(dq, up), dot_t(dv, up))
    if kind == "first":
        back_ref[...] = back
        return
    sum_ref[...] = back + before_ref[...]
    if kind == "plain":
        own = pl.multiple_of(spot[SPOT_OWN_PLAIN], PLANE)
        mine_ref[...] = sum_ref[pl.ds(own, PLANE), :]
        theirs_ref[...] = sum_ref[pl.ds(PLANE - own, PLANE), :].astype(BF16)
    else:
        own = pl.multiple_of(spot[SPOT_OWN_SHIFT], PLANE)
        sum_ref[pl.ds(own, PLANE), :] += mine_ref[...] + theirs_ref[...].astype(F32)
        back_ref[...] = sum_ref[...].astype(BF16)


def attention_item(kind, item, order, spot, members, up, *more):
    arrays = [array.reshape(GROUP, 8 * HD) for array, _ in members]
    columns = [pl.BlockSpec((GROUP, HD), lambda i, *s, column=column: (0, column)) for _, column in members]
    seat = SPOT_PLAIN if item < 2 else SPOT_SHIFT
    shapes = {
        "first": [((GROUP, BOTH), F32)],
        "plain": [((PLANE, BOTH), F32), ((PLANE, BOTH), BF16)],
        "shifted": [((GROUP, BOTH), BF16)],
    }[kind] + [((GROUP, 2 * HD), BF16)]
    scratch = [pltpu.VMEM((GROUP, HD), F32)]
    if kind != "first":
        scratch.append(pltpu.VMEM((GROUP, BOTH), F32))

    def body(*refs):
        attention_kernel(kind, *refs)

    return call(
        body,
        "attention_" + kind,
        2,
        columns
        + [pl.BlockSpec((BOTH, HD), lambda i, order, spot: (0, order[item * MEMBERS + spot[seat]]))]
        + [block(array.shape) for array in more],
        [block(shape) for shape, _ in shapes],
        [jax.ShapeDtypeStruct(*shape) for shape in shapes],
        scratch,
        (4 * 10**9, 3 * 10**6),
    )(order, spot, *arrays, up, *more)


def up_gradient_kernel(spot, own_ref, later_ref, earlier_ref, *refs):
    out_ref, low_a, low_b = refs[-3:]
    y = spot[SPOT_Y]

    def fill(low, first, second):
        for half, ref in enumerate((first, second)):
            for s in range(YS):
                low[pl.ds(half * PLANE + s * ROWS, ROWS), :] = ref[(y - s + YS) % YS]

    @pl.when(spot[SPOT_OWN_PLAIN] == 0)
    def _():
        fill(low_a, own_ref, later_ref)
        fill(low_b, earlier_ref, own_ref)

    @pl.when(spot[SPOT_OWN_PLAIN] != 0)
    def _():
        fill(low_a, earlier_ref, own_ref)
        fill(low_b, own_ref, later_ref)

    for item, grads in enumerate(refs[:4]):
        low = (low_a, low_b)[item // 2][...]
        for m in range(2):
            part = adapter_scale * dot_0(low[:, m * RANK : (m + 1) * RANK], grads[:, pl.ds(m * HD, HD)])
            part = part.astype(BF16)
            for e in range(RANK // PIECE):
                d = m * (RANK // PIECE) + e
                out_ref[d, pl.ds(item * PIECE, PIECE), :] = part[e * PIECE : (e + 1) * PIECE]


def up_gradients(spot, own, later, earlier, grads):
    shape = (SLICES, 4 * PIECE, HD)
    return call(
        up_gradient_kernel,
        "up_gradients",
        1,
        [block((YS, ROWS, BOTH))] * 3 + [block((GROUP, 2 * HD))] * 4,
        block(shape),
        jax.ShapeDtypeStruct(shape, BF16),
        [pltpu.VMEM((GROUP, BOTH), BF16)] * 2,
        (2 * 10**9, 3 * 10**6),
    )(spot, own, later, earlier, *grads)


def gather_kernel(summed_ref, ups_ref, out_ref):
    back = jnp.sum(summed_ref[...].astype(F32), axis=0).astype(BF16)
    for d in range(SLICES):
        out_ref[d, pl.ds(0, ROWS), :] = back
    out_ref[:, pl.ds(ROWS, 4 * PIECE), :] = ups_ref[...]


def gather_parts(summed, ups):
    shape = (SLICES, ROWS + 4 * PIECE, HD)
    return call(
        gather_kernel,
        "gather_parts",
        0,
        [block(summed.shape), block(ups.shape)],
        block(shape),
        jax.ShapeDtypeStruct(shape, BF16),
        [],
        (10**7, 10**6),
    )(summed, ups)


def merge_kernel(order, spot, place, both_ref, *refs):
    x_refs, out_ref = refs[:-1], refs[-1]
    x, core = place[0] // CS, place[0] % CS
    total = jnp.zeros((HEADS * PIECE, BOTH), F32)
    for dx in range(XS):
        for other in range(CS):
            s = (x - dx + XS) % XS * CS + (core + other) % CS
            back = both_ref[s, pl.ds(0, ROWS), :]
            total += jnp.dot(x_refs[dx][other], back, preferred_element_type=F32)
    total = (adapter_scale * total).astype(BF16)
    for u in range(HEADS):
        out_ref[u, pl.ds(0, PIECE), :] = total[u * PIECE : (u + 1) * PIECE]
        out_ref[u, pl.ds(PIECE, PIECE), :] = jnp.zeros((PIECE, HD), BF16)
    ups = jnp.sum(both_ref[:, pl.ds(ROWS, 4 * PIECE), :].astype(F32), axis=0).astype(BF16)
    for item in range(4):
        seat = spot[SPOT_PLAIN if item < 2 else SPOT_SHIFT]
        head = order[item * MEMBERS + seat]
        out_ref[head, pl.ds(PIECE, PIECE), :] = ups[item * PIECE : (item + 1) * PIECE]


def merge(order, spot, place, both, pieces):
    shape = (HEADS, 2 * PIECE, HD)
    return call(
        merge_kernel,
        "merge_gradients",
        3,
        [block(both.shape)] + [block(piece.shape) for piece in pieces],
        block(shape),
        jax.ShapeDtypeStruct(shape, BF16),
        [],
        (2 * 10**8, 2 * 10**6),
    )(order, spot, place, both, *pieces)


def spread_kernel(in_ref, out_ref):
    total = jnp.sum(in_ref[...].astype(F32), axis=0)
    for d in range(SLICES):
        out_ref[d] = total


def spread(both):
    shape = (SLICES, 2 * PIECE, HD)
    return call(
        spread_kernel,
        "spread_sums",
        0,
        [block(both.shape)],
        block(shape),
        jax.ShapeDtypeStruct(shape, F32),
        [],
        (10**6, 10**6),
    )(both)


def finish_kernel(in_ref, down_ref, up_ref):
    down = in_ref[:, pl.ds(0, PIECE), :].reshape(HD, BOTH).T
    up = in_ref[:, pl.ds(PIECE, PIECE), :].reshape(BOTH, HD)
    for m in range(2):
        down_ref[m] = down[m * RANK : (m + 1) * RANK]
        up_ref[m] = up[m * RANK : (m + 1) * RANK]


def finish(both):
    shape = (2, RANK, HD)
    return call(
        finish_kernel,
        "finish",
        0,
        [block(both.shape)],
        [block(shape)] * 2,
        [jax.ShapeDtypeStruct(shape, F32)] * 2,
        [],
        (10**6, 10**6),
    )(both)


def per_device(
    normalized_input,
    frozen_queries,
    frozen_keys,
    frozen_values,
    output_gradient,
    adapter_down_maps,
    adapter_up_maps,
    shifted,
):
    tokens = normalized_input[0]
    spot = lax.dynamic_slice(jnp.asarray(SPOTS), (lax.axis_index("ulysses"), 0), (1, 8)).reshape(8)
    place = lax.axis_index("dp").reshape(1)
    up = adapter_up_maps.reshape(BOTH, WIDTH)
    down = adapter_down_maps.transpose(0, 2, 1).reshape(BOTH, WIDTH)

    frozen = (frozen_queries[0], frozen_keys[0], frozen_values[0], output_gradient[0])
    sent, order, low = prepare_plain(shifted.astype(jnp.int32), tokens, down, up, frozen)
    plain = exchange(sent, "ulysses", PLAIN_GROUPS)
    sent = prepare_shifted(order, low, up, frozen)
    own = jnp.stack([low] + [lax.ppermute(low, "ulysses", y_shift(dy)) for dy in (1, 2, 3)])
    turned = turn(place, after(tokens, low))
    other = lax.ppermute(turned[1], "dp", CORE_SWAP)

    sent, plain, own, turned, other = after((sent, plain, own, turned, other))
    late = exchange(sent, "ulysses", SHIFT_GROUPS)
    later = lax.ppermute(own, "ulysses", z_shift(-1))
    earlier = lax.ppermute(own, "ulysses", z_shift(1))
    pieces = [jnp.stack([turned[0, dx], other[dx]]) for dx in range(XS)]
    pieces = pieces[:1] + [lax.ppermute(pieces[dx], "dp", x_shift(dx)) for dx in (1, 2, 3)]
    partial, grads_0 = attention_item("first", 0, order, spot, [(plain, t) for t in range(4)], up)
    mine, theirs, grads_1 = attention_item(
        "plain", 1, order, spot, [(plain, 4 + t) for t in range(4)], up, partial
    )
    theirs = lax.ppermute(theirs, "ulysses", PLAIN_SWAP)

    late, theirs, pieces, later, earlier = after((late, theirs, pieces, later, earlier))
    partial, grads_2 = attention_item("first", 2, order, spot, [(late, t) for t in range(4)], up)
    partial, grads_3 = attention_item(
        "shifted", 3, order, spot, [(late, 4 + t) for t in range(4)], up, partial, mine, theirs
    )
    summed = exchange(partial.reshape(MEMBERS, ROWS, BOTH), "ulysses", SHIFT_GROUPS)
    ups = up_gradients(spot, own, later, earlier, (grads_0, grads_1, grads_2, grads_3))
    both = exchange(gather_parts(summed, ups), "dp")
    both = exchange(merge(order, spot, place, both, pieces), "ulysses")
    both = exchange(spread(both), "dp")
    grad_down, grad_up = finish(both)
    return (grad_down.transpose(0, 2, 1), grad_up)


def solution(mesh):
    rows = P("dp", "ulysses", None)
    in_specs = (rows, rows, rows, rows, rows, P(), P(), P())
    out_specs = (P(None, "ulysses", None), P(None, None, "ulysses"))
    return jax.shard_map(
        per_device, mesh=mesh, in_specs=in_specs, out_specs=out_specs, check_vma=False
    )
```

```python
import math

import jax
import jax.numpy as jnp
import numpy as np
from jax import lax
from jax.experimental import pallas as pl
from jax.experimental.pallas import tpu as pltpu
from jax.sharding import PartitionSpec as P

HEADS = 32
HD = 128
WIDTH = HEADS * HD
GROUP = 1024
PLANE = 512
RANK = 64
BOTH = 2 * RANK
ROWS = 128
ZS, YS = 8, 4
XS, CS = 4, 2
SLICES = XS * CS
MEMBERS = 8
PIECE = 16
RB = 256
BF16, F32 = jnp.bfloat16, jnp.float32

adapter_scale = 0.5

PLAIN_GROUPS = [[MEMBERS * g + i for i in range(MEMBERS)] for g in range(4)]
SHIFT_GROUPS = [[(MEMBERS * g + 4 + i) % HEADS for i in range(MEMBERS)] for g in range(4)]
PLAIN_SWAP = [(u, u ^ 4) for u in range(HEADS)]
Y_GROUPS = [[YS * z + y for y in range(YS)] for z in range(ZS)]
SHIFT_SWAP = [(u, (((u + 4) % HEADS ^ 4) - 4) % HEADS) for u in range(HEADS)]
CORE_SWAP = [(d, d ^ 1) for d in range(SLICES)]
ANYWHERE = pl.BlockSpec(memory_space=pltpu.HBM)
SCALARS = pl.BlockSpec(memory_space=pltpu.SMEM)

SPOTS = np.array(
    [[u % 4, u % 8, (u + 4) % 8, PLANE * (u // 4 % 2), PLANE * (1 - u // 4 % 2), 0, 0, 0] for u in range(HEADS)],
    np.int32,
)
SPOT_Y, SPOT_PLAIN, SPOT_SHIFT, SPOT_OWN_PLAIN, SPOT_OWN_SHIFT = range(5)


def z_shift(dz):
    return [(z * YS + y, ((z + dz) % ZS) * YS + y) for z in range(ZS) for y in range(YS)]


def y_shift(dy):
    return [(z * YS + y, z * YS + (y + dy) % YS) for z in range(ZS) for y in range(YS)]


def x_shift(dx):
    return [(x * CS + c, ((x + dx) % XS) * CS + c) for x in range(XS) for c in range(CS)]


def exchange(member, axis, groups=None):
    return lax.all_to_all(member, axis, 0, 0, tiled=True, axis_index_groups=groups)


def after(values, *others):
    return lax.optimization_barrier((values, others))[0]


def block(shape):
    return pl.BlockSpec(shape, lambda i, *s: (0,) * len(shape))


def dot_t(a, b):
    return lax.dot_general(a, b, (((1,), (1,)), ((), ())), preferred_element_type=F32)


def dot_0(a, b):
    return lax.dot_general(a, b, (((0,), (0,)), ((), ())), preferred_element_type=F32)


def call(kernel, name, scalars, in_specs, out_specs, out_shape, scratch, cost, vmem=None):
    params = pltpu.CompilerParams(vmem_limit_bytes=vmem and vmem * 2**20)
    return pl.pallas_call(
        kernel,
        name=name,
        out_shape=out_shape,
        grid_spec=pltpu.PrefetchScalarGridSpec(
            num_scalar_prefetch=scalars,
            grid=(1,),
            in_specs=in_specs,
            out_specs=out_specs,
            scratch_shapes=scratch,
        ),
        compiler_params=params,
        cost_estimate=pl.CostEstimate(flops=cost[0], bytes_accessed=cost[1], transcendentals=0),
    )


def order_heads(flags, order):
    def place(h, ones):
        flag = flags[h]
        order[jnp.where(flag > 0, HEADS // 2 + ones, h - ones)] = h
        return ones + jnp.where(flag > 0, 1, 0)

    lax.fori_loop(0, HEADS, place, 0, unroll=True)


def fetch_heads(heads, places, fq_ref, fk_ref, fv_ref, go_ref, up_ref, q_in, v_in, up_in, sems):
    copies = []
    for p, (head, (buffer, entry)) in enumerate(zip(heads, places)):
        cols = pl.ds(pl.multiple_of(head * HD, HD), HD)
        own = pl.ds(p * HD, HD)
        spots = (
            (up_ref, up_in.at[:, own]),
            (fq_ref, q_in.at[:, own]),
            (fv_ref, v_in.at[:, own]),
            (fk_ref, buffer.at[(*entry[:-1], slice(None), pl.ds(entry[-1] + HD, HD))]),
            (go_ref, buffer.at[(*entry[:-1], slice(None), pl.ds(entry[-1] + 3 * HD, HD))]),
        )
        for t, (ref, spot) in enumerate(spots):
            copies.append(pltpu.make_async_copy(ref.at[:, cols], spot, sems.at[p, t]))
            copies[-1].start()
    return copies


def raise_heads(low, copies, places, q_in, v_in, up_in):
    lanes = lax.broadcasted_iota(jnp.int32, (ROWS, BOTH), 1)
    none = jnp.zeros_like(low)
    lows = jnp.concatenate([jnp.where(lanes < RANK, low, none), jnp.where(lanes < RANK, none, low)], axis=0)
    for copy in copies:
        copy.wait()
    raised = jnp.dot(lows, up_in[...], preferred_element_type=F32)
    for p, (buffer, entry) in enumerate(places):
        own = slice(p * HD, (p + 1) * HD)
        q = (q_in[:, own].astype(F32) + adapter_scale * raised[:ROWS, own]).astype(BF16)
        v = (v_in[:, own].astype(F32) + adapter_scale * raised[ROWS:, own]).astype(BF16)
        buffer[(*entry[:-1], slice(None), pl.ds(entry[-1], HD))] = q
        buffer[(*entry[:-1], slice(None), pl.ds(entry[-1] + 2 * HD, HD))] = v


HALF = HEADS // 2
HEAD_SCRATCH = [
    pltpu.VMEM((ROWS, HALF * HD), BF16),
    pltpu.VMEM((ROWS, HALF * HD), BF16),
    pltpu.VMEM((BOTH, HALF * HD), BF16),
    pltpu.SemaphoreType.DMA((HALF, 5)),
]


def prepare_plain_kernel(flags, x_hbm, down_hbm, *refs):
    frozen, (out_ref, order, low_ref, x_in, down_in, whole_sems, q_in, v_in, up_in, sems) = refs[:5], refs[5:]
    wholes = [
        pltpu.make_async_copy(x_hbm, x_in, whole_sems.at[0]),
        pltpu.make_async_copy(down_hbm, down_in, whole_sems.at[1]),
    ]
    for copy in wholes:
        copy.start()
    order_heads(flags, order)
    places = [(out_ref, (p % MEMBERS, p // MEMBERS * 4 * HD)) for p in range(HALF)]
    copies = fetch_heads([order[p] for p in range(HALF)], places, *frozen, q_in, v_in, up_in, sems)
    for copy in wholes:
        copy.wait()
    low = dot_t(x_in[...], down_in[...]).astype(BF16)
    low_ref[...] = low
    raise_heads(low, copies, places, q_in, v_in, up_in)


def prepare_plain(flags, x, down, frozen):
    return call(
        prepare_plain_kernel,
        "prepare_plain",
        1,
        [ANYWHERE] * 7,
        [block((MEMBERS, ROWS, 8 * HD)), SCALARS, block((ROWS, BOTH))],
        (
            jax.ShapeDtypeStruct((MEMBERS, ROWS, 8 * HD), BF16),
            jax.ShapeDtypeStruct((HEADS,), jnp.int32),
            jax.ShapeDtypeStruct((ROWS, BOTH), BF16),
        ),
        [pltpu.VMEM((ROWS, WIDTH), BF16), pltpu.VMEM((BOTH, WIDTH), BF16), pltpu.SemaphoreType.DMA((2,))]
        + HEAD_SCRATCH,
        (10**9, 8 * 10**6),
    )(flags, x, down, *frozen)


def prepare_shifted_kernel(order, spot, low_ref, *refs):
    frozen, outs, scratch = refs[:5], refs[5:9], refs[9:]
    y, own_half = spot[SPOT_Y], spot[SPOT_OWN_SHIFT] // PLANE
    heads, places = [], []
    for item in range(2):
        for other in range(2):
            for dy in range(YS):
                seat = (own_half + other) % 2 * YS + ((y + dy) % YS if item == 0 else dy)
                heads.append(order[HALF + item * MEMBERS + seat])
                places.append((outs[2 * item + other], (dy, 0)))
    copies = fetch_heads(heads, places, *frozen, *scratch)
    raise_heads(low_ref[...], copies, places, *scratch[:3])


def prepare_shifted(order, spot, low, frozen):
    return call(
        prepare_shifted_kernel,
        "prepare_shifted",
        2,
        [block((ROWS, BOTH))] + [ANYWHERE] * 5,
        [block((YS, ROWS, 4 * HD))] * 4,
        (jax.ShapeDtypeStruct((YS, ROWS, 4 * HD), BF16),) * 4,
        HEAD_SCRATCH,
        (10**9, 8 * 10**6),
    )(order, spot, low, *frozen)


def pack_kernel(low_ref, own_ref, other_ref, *out_refs):
    for dy, out_ref in enumerate(out_refs, 1):
        out_ref[:, pl.ds(0, 4 * HD)] = own_ref[dy]
        out_ref[:, pl.ds(4 * HD, 4 * HD)] = other_ref[dy]
        out_ref[:, pl.ds(8 * HD, BOTH)] = low_ref[...]


def pack(low, own, other):
    shape = (ROWS, 8 * HD + BOTH)
    return call(
        pack_kernel,
        "pack_first",
        0,
        [block(low.shape)] + [block(own.shape)] * 2,
        [block(shape)] * 3,
        (jax.ShapeDtypeStruct(shape, BF16),) * 3,
        [],
        (0, 4 * 10**6),
    )(low, own, other)


def turn_kernel(spot, x_ref, kept_ref, other_ref):
    x, core = spot[0] // CS, spot[0] % CS

    def fill(refs):
        for u in range(HEADS):
            turned = x_ref[:, pl.ds(u * HD, HD)].T
            for d in range(SLICES):
                step = (d // CS - x + XS) % XS
                refs[d % CS][step, pl.ds(u * PIECE, PIECE), :] = turned[d * PIECE : (d + 1) * PIECE]

    @pl.when(core == 0)
    def _():
        fill((kept_ref, other_ref))

    @pl.when(core != 0)
    def _():
        fill((other_ref, kept_ref))


def turn(place, x):
    shape = (XS, HEADS * PIECE, ROWS)
    return call(
        turn_kernel,
        "turn_input",
        1,
        [block(x.shape)],
        [block(shape)] * 2,
        (jax.ShapeDtypeStruct(shape, BF16),) * 2,
        [],
        (10**9, 2 * 10**6),
    )(place, x)


def attend(x_ref, up, grads_ref, column, dv_acc):
    factor = 1.0 / math.sqrt(HD)
    bend = factor * math.log2(math.e)
    row_ids = lax.broadcasted_iota(jnp.int32, (RB, RB), 0)
    column_ids = lax.broadcasted_iota(jnp.int32, (RB, RB), 1)
    keep = column_ids <= row_ids
    for i in range(GROUP // RB):
        n = (i + 1) * RB
        rows = pl.ds(i * RB, RB)
        q = x_ref[rows, pl.ds(0, HD)]
        g = x_ref[rows, pl.ds(3 * HD, HD)]
        k = x_ref[pl.ds(0, n), pl.ds(HD, HD)]
        v = x_ref[pl.ds(0, n), pl.ds(2 * HD, HD)]
        scores = dot_t(q, k)
        last = jnp.where(keep, scores[:, i * RB :], -1e30)
        scores = last if i == 0 else jnp.concatenate([scores[:, : i * RB], last], axis=1)
        top = jnp.max(scores, axis=1, keepdims=True)
        weights = jnp.exp2((scores - top) * bend)
        total = jnp.sum(weights, axis=1, keepdims=True)
        attention = (weights * (1.0 / total)).astype(BF16)
        output = jnp.dot(attention, v, preferred_element_type=F32)
        grad_attention = dot_t(g, v)
        center = jnp.sum(g.astype(F32) * output, axis=1, keepdims=True)
        grad_scores = (attention.astype(F32) * (grad_attention - center)).astype(BF16)
        dq = jnp.dot(grad_scores, k, preferred_element_type=F32) * factor
        grads_ref[rows, pl.ds(column, HD)] = dq.astype(BF16)
        dv = dot_0(attention, g)
        if i:
            dv_acc[pl.ds(0, i * RB), :] += dv[: i * RB]
        dv_acc[rows, :] = dv[i * RB :]
    dq = grads_ref[:, pl.ds(column, HD)]
    dv = dv_acc[...].astype(BF16)
    grads_ref[:, pl.ds(column + HD, HD)] = dv
    lanes = lax.broadcasted_iota(jnp.int32, (GROUP, BOTH), 1)
    return jnp.where(lanes < RANK, dot_t(dq, up), dot_t(dv, up))


def attention_plain_kernel(order, spot, arrived, up_a, up_b, mine_ref, theirs_ref, grads_ref, xs, dv_acc, total, sems):
    copies = []
    for item in range(2):
        source = arrived.at[:, pl.ds(item * 4 * HD, 4 * HD)]
        copies.append(pltpu.make_async_copy(source, xs.at[item], sems.at[item]))
        copies[-1].start()
    copies[0].wait()
    total[...] = attend(xs.at[0], up_a[...], grads_ref, 0, dv_acc)
    copies[1].wait()
    total[...] += attend(xs.at[1], up_b[...], grads_ref, 2 * HD, dv_acc)
    own = pl.multiple_of(spot[SPOT_OWN_PLAIN], PLANE)
    mine_ref[...] = total[pl.ds(own, PLANE), :]
    theirs_ref[...] = total[pl.ds(PLANE - own, PLANE), :].astype(BF16)


def up_columns(item):
    seat = SPOT_PLAIN if item < 2 else SPOT_SHIFT
    return pl.BlockSpec((BOTH, HD), lambda i, order, spot: (0, order[item * MEMBERS + spot[seat]]))


def attention_plain(order, spot, arrived, up):
    shapes = [((PLANE, BOTH), F32), ((PLANE, BOTH), BF16), ((GROUP, 4 * HD), BF16)]
    return call(
        attention_plain_kernel,
        "attention_plain",
        2,
        [ANYWHERE, up_columns(0), up_columns(1)],
        [block(shape) for shape, _ in shapes],
        [jax.ShapeDtypeStruct(*shape) for shape in shapes],
        [
            pltpu.VMEM((2, GROUP, 4 * HD), BF16),
            pltpu.VMEM((GROUP, HD), F32),
            pltpu.VMEM((GROUP, BOTH), F32),
            pltpu.SemaphoreType.DMA((2,)),
        ],
        (2 * 10**10, 4 * 10**6),
    )(order, spot, arrived.reshape(GROUP, 8 * HD), up, up)


def attention_shifted_kernel(last, order, spot, *refs):
    y, own = spot[SPOT_Y], spot[SPOT_OWN_SHIFT]
    if last:
        arrived, up, before_hbm, mine_hbm, theirs_hbm, back_ref, grads_hbm, x_in, dv_acc, sems = refs[:10]
        total, before_ref, mine_ref, theirs_ref, grads_ref, more_sems = refs[10:]
        blocks = [[arrived.at[s, half] for half in range(2)] for s in range(YS)]
        sources = range(YS)
    else:
        own_ref, other_ref, *pieces = refs[:5]
        up, back_ref, grads_ref, x_in, dv_acc, sems = refs[5:]
        blocks = [[own_ref.at[0], other_ref.at[0]]]
        for piece in pieces:
            blocks.append([piece.at[:, pl.ds(half * 4 * HD, 4 * HD)] for half in range(2)])
        sources = [(y - dy + YS) % YS for dy in range(YS)]
    copies = []
    for t, source in enumerate(sources):
        for half in range(2):
            start = (own if half == 0 else PLANE - own) + source * ROWS
            rows = pl.ds(pl.multiple_of(start, ROWS), ROWS)
            copies.append(pltpu.make_async_copy(blocks[t][half], x_in.at[rows, :], sems.at[t, half]))
            copies[-1].start()
    if last:
        pairs = ((before_hbm, before_ref), (mine_hbm, mine_ref), (theirs_hbm, theirs_ref))
        others = [pltpu.make_async_copy(*pair, more_sems.at[t]) for t, pair in enumerate(pairs)]
        for copy in others:
            copy.start()
    for copy in copies:
        copy.wait()
    back = attend(x_in, up[...], grads_ref, 0, dv_acc)
    if not last:
        back_ref[...] = back
        return
    save = pltpu.make_async_copy(grads_ref, grads_hbm, more_sems.at[3])
    save.start()
    for copy in others:
        copy.wait()
    total[...] = back + before_ref[...]
    mine_rows = pl.ds(pl.multiple_of(own, PLANE), PLANE)
    total[mine_rows, :] += mine_ref[...] + theirs_ref[...].astype(F32)
    back_ref[...] = total[...].astype(BF16)
    save.wait()


LAST_SCRATCH = [
    pltpu.VMEM((GROUP, BOTH), F32),
    pltpu.VMEM((GROUP, BOTH), F32),
    pltpu.VMEM((PLANE, BOTH), F32),
    pltpu.VMEM((PLANE, BOTH), BF16),
    pltpu.VMEM((GROUP, 2 * HD), BF16),
    pltpu.SemaphoreType.DMA((4,)),
]


def attention_shifted(item, order, spot, arrived, up, *more):
    last = len(more) > 0
    shapes = [((GROUP, BOTH), BF16 if last else F32), ((GROUP, 2 * HD), BF16)]

    def body(*refs):
        attention_shifted_kernel(last, *refs)

    return call(
        body,
        "attention_last" if last else "attention_third",
        2,
        [pl.BlockSpec(memory_space=pl.ANY) if last else ANYWHERE] * len(arrived)
        + [up_columns(item)]
        + [ANYWHERE] * len(more),
        [block(shapes[0][0]), ANYWHERE if last else block(shapes[1][0])],
        [jax.ShapeDtypeStruct(*shape) for shape in shapes],
        [pltpu.VMEM((GROUP, 4 * HD), BF16), pltpu.VMEM((GROUP, HD), F32), pltpu.SemaphoreType.DMA((YS, 2))]
        + LAST_SCRATCH * last,
        (4 * 10**9, 3 * 10**6) if last else (10**6, 10**4),
    )(order, spot, *arrived, up, *more)


def up_gradient_kernel(spot, own_ref, later_ref, earlier_ref, *refs):
    out_ref, low_a, low_b = refs[-3:]
    y = spot[SPOT_Y]

    def fill(low, first, second):
        for half, ref in enumerate((first, second)):
            for s in range(YS):
                low[pl.ds(half * PLANE + s * ROWS, ROWS), :] = ref[(y - s + YS) % YS]

    @pl.when(spot[SPOT_OWN_PLAIN] == 0)
    def _():
        fill(low_a, own_ref, later_ref)
        fill(low_b, earlier_ref, own_ref)

    @pl.when(spot[SPOT_OWN_PLAIN] != 0)
    def _():
        fill(low_a, earlier_ref, own_ref)
        fill(low_b, own_ref, later_ref)

    for item in range(4):
        low = (low_a, low_b)[item // 2][...]
        grads, column = ((refs[0], 0), (refs[0], 2 * HD), (refs[1], 0), (refs[2], 0))[item]
        for m in range(2):
            columns = pl.ds(column + m * HD, HD)
            part = adapter_scale * dot_0(low[:, m * RANK : (m + 1) * RANK], grads[:, columns])
            part = part.astype(BF16)
            for e in range(RANK // PIECE):
                d = m * (RANK // PIECE) + e
                out_ref[d, pl.ds(item * PIECE, PIECE), :] = part[e * PIECE : (e + 1) * PIECE]


def up_gradients(spot, own, later, earlier, grads):
    shape = (SLICES, 4 * PIECE, HD)
    return call(
        up_gradient_kernel,
        "up_gradients",
        1,
        [block((YS, ROWS, BOTH))] * 3 + [block(array.shape) for array in grads],
        block(shape),
        jax.ShapeDtypeStruct(shape, BF16),
        [pltpu.VMEM((GROUP, BOTH), BF16)] * 2,
        (2 * 10**9, 3 * 10**6),
        16,
    )(spot, own, later, earlier, *grads)


def gather_kernel(summed_ref, ups_ref, out_ref):
    back = jnp.sum(summed_ref[...].astype(F32), axis=0).astype(BF16)
    for d in range(SLICES):
        out_ref[d, pl.ds(0, ROWS), :] = back
    out_ref[:, pl.ds(ROWS, 4 * PIECE), :] = ups_ref[...]


def gather_parts(summed, ups):
    shape = (SLICES, ROWS + 4 * PIECE, HD)
    return call(
        gather_kernel,
        "gather_parts",
        0,
        [block(summed.shape), block(ups.shape)],
        block(shape),
        jax.ShapeDtypeStruct(shape, BF16),
        [],
        (10**7, 10**6),
        16,
    )(summed, ups)


def merge_kernel(order, spot, place, both_ref, *refs):
    x_refs, out_ref = refs[:-1], refs[-1]
    x, core = place[0] // CS, place[0] % CS
    total = jnp.zeros((HEADS * PIECE, BOTH), F32)
    for dx in range(XS):
        for other in range(CS):
            s = (x - dx + XS) % XS * CS + (core + other) % CS
            back = both_ref[s, pl.ds(0, ROWS), :]
            total += jnp.dot(x_refs[dx][other], back, preferred_element_type=F32)
    total = (adapter_scale * total).astype(BF16)
    for u in range(HEADS):
        out_ref[u, pl.ds(0, PIECE), :] = total[u * PIECE : (u + 1) * PIECE]
        out_ref[u, pl.ds(PIECE, PIECE), :] = jnp.zeros((PIECE, HD), BF16)
    ups = jnp.sum(both_ref[:, pl.ds(ROWS, 4 * PIECE), :].astype(F32), axis=0).astype(BF16)
    for item in range(4):
        seat = spot[SPOT_PLAIN if item < 2 else SPOT_SHIFT]
        head = order[item * MEMBERS + seat]
        out_ref[head, pl.ds(PIECE, PIECE), :] = ups[item * PIECE : (item + 1) * PIECE]


def merge(order, spot, place, both, pieces):
    shape = (HEADS, 2 * PIECE, HD)
    return call(
        merge_kernel,
        "merge_gradients",
        3,
        [block(both.shape)] + [block(piece.shape) for piece in pieces],
        block(shape),
        jax.ShapeDtypeStruct(shape, BF16),
        [],
        (2 * 10**8, 2 * 10**6),
        16,
    )(order, spot, place, both, *pieces)


def spread_kernel(in_ref, out_ref):
    total = jnp.sum(in_ref[...].astype(F32), axis=0)
    for d in range(SLICES):
        out_ref[d] = total


def spread(both):
    shape = (SLICES, 2 * PIECE, HD)
    return call(
        spread_kernel,
        "spread_sums",
        0,
        [block(both.shape)],
        block(shape),
        jax.ShapeDtypeStruct(shape, F32),
        [],
        (10**6, 10**6),
        16,
    )(both)


def finish_kernel(in_ref, down_ref, up_ref):
    down = in_ref[:, pl.ds(0, PIECE), :].reshape(HD, BOTH).T
    up = in_ref[:, pl.ds(PIECE, PIECE), :].reshape(BOTH, HD)
    for m in range(2):
        down_ref[m] = down[m * RANK : (m + 1) * RANK]
        up_ref[m] = up[m * RANK : (m + 1) * RANK]


def finish(both):
    shape = (2, RANK, HD)
    return call(
        finish_kernel,
        "finish",
        0,
        [block(both.shape)],
        [block(shape)] * 2,
        [jax.ShapeDtypeStruct(shape, F32)] * 2,
        [],
        (10**6, 10**6),
        16,
    )(both)


def per_device(
    normalized_input,
    frozen_queries,
    frozen_keys,
    frozen_values,
    output_gradient,
    adapter_down_maps,
    adapter_up_maps,
    shifted,
):
    tokens = normalized_input[0]
    spot = lax.dynamic_slice(jnp.asarray(SPOTS), (lax.axis_index("ulysses"), 0), (1, 8)).reshape(8)
    place = lax.axis_index("dp").reshape(1)
    up = adapter_up_maps.reshape(BOTH, WIDTH)
    down = adapter_down_maps.transpose(0, 2, 1).reshape(BOTH, WIDTH)

    frozen = (frozen_queries[0], frozen_keys[0], frozen_values[0], output_gradient[0], up)
    sent, order, low = prepare_plain(shifted.astype(jnp.int32), tokens, down, frozen)
    plain = exchange(sent, "ulysses", PLAIN_GROUPS)
    own_c, other_c, own_d, other_d = prepare_shifted(order, spot, low, frozen)
    other_c = lax.ppermute(other_c, "ulysses", SHIFT_SWAP)
    other_d = lax.ppermute(other_d, "ulysses", SHIFT_SWAP)
    kept, other = turn(place, after(tokens, own_c))
    other = lax.ppermute(other, "dp", CORE_SWAP)
    pieces = [jnp.stack([kept[dx], other[dx]]) for dx in range(XS)]
    pieces = pieces[:1] + [lax.ppermute(pieces[dx], "dp", x_shift(dx)) for dx in (1, 2, 3)]

    packed = pack(low, own_c, other_c)
    arrived_c = [lax.ppermute(packed[dy - 1], "ulysses", y_shift(dy)) for dy in (1, 2, 3)]
    sent = jnp.stack([own_d, other_d], axis=1)
    plain, pieces, sent = after((plain, pieces, sent), packed)

    arrived_d = exchange(sent, "ulysses", Y_GROUPS)
    mine, theirs, grads_plain = attention_plain(order, spot, plain, up)
    theirs = lax.ppermute(theirs, "ulysses", PLAIN_SWAP)
    arrived_c = after(arrived_c, grads_plain, sent)
    partial, grads_c = attention_shifted(2, order, spot, [own_c, other_c, *arrived_c], up)
    own = jnp.stack([low] + [array[:, 8 * HD :] for array in arrived_c])
    later = lax.ppermute(own, "ulysses", z_shift(-1))
    earlier = lax.ppermute(own, "ulysses", z_shift(1))

    arrived_d, theirs, later, earlier = after((arrived_d, theirs, later, earlier), partial)
    partial, grads_d = attention_shifted(
        3, order, spot, [arrived_d], up, partial, mine, theirs
    )
    summed = exchange(partial.reshape(MEMBERS, ROWS, BOTH), "ulysses", SHIFT_GROUPS)
    ups = up_gradients(spot, own, later, earlier, (grads_plain, grads_c, grads_d))
    both = exchange(gather_parts(summed, ups), "dp")
    both = exchange(merge(order, spot, place, both, pieces), "ulysses")
    both = exchange(spread(both), "dp")
    grad_down, grad_up = finish(both)
    return (grad_down.transpose(0, 2, 1), grad_up)


def solution(mesh):
    rows = P("dp", "ulysses", None)
    in_specs = (rows, rows, rows, rows, rows, P(), P(), P())
    out_specs = (P(None, "ulysses", None), P(None, None, "ulysses"))
    return jax.shard_map(
        per_device, mesh=mesh, in_specs=in_specs, out_specs=out_specs, check_vma=False
    )
```

```python
import math

import jax
import jax.numpy as jnp
from jax import lax
from jax.experimental import pallas as pl
from jax.experimental.pallas import tpu as pltpu
from jax.sharding import PartitionSpec as P

HEADS = 32
HD = 128
WIDTH = HEADS * HD
GROUP = 1024
PLANE = 512
RANK = 64
BOTH = 2 * RANK
ROWS = 128
ZS, YS = 8, 4
XS, CS = 4, 2
SLICES = XS * CS
MEMBERS = 8
PIECE = 16
RB = 256
BF16, F32 = jnp.bfloat16, jnp.float32

adapter_scale = 0.5

PLAIN_GROUPS = [[MEMBERS * g + i for i in range(MEMBERS)] for g in range(4)]
SHIFT_GROUPS = [[(MEMBERS * g + 4 + i) % HEADS for i in range(MEMBERS)] for g in range(4)]
PLAIN_SWAP = [(u, u ^ 4) for u in range(HEADS)]
Y_GROUPS = [[YS * z + y for y in range(YS)] for z in range(ZS)]
SHIFT_SWAP = [(u, (((u + 4) % HEADS ^ 4) - 4) % HEADS) for u in range(HEADS)]
CORE_SWAP = [(d, d ^ 1) for d in range(SLICES)]
ANYWHERE = pl.BlockSpec(memory_space=pltpu.HBM)
SCALARS = pl.BlockSpec(memory_space=pltpu.SMEM)

SPOT_Y, SPOT_PLAIN, SPOT_SHIFT, SPOT_OWN_PLAIN, SPOT_OWN_SHIFT = range(5)


def z_shift(dz):
    return [(z * YS + y, ((z + dz) % ZS) * YS + y) for z in range(ZS) for y in range(YS)]


def y_shift(dy):
    return [(z * YS + y, z * YS + (y + dy) % YS) for z in range(ZS) for y in range(YS)]


def x_shift(dx):
    return [(x * CS + c, ((x + dx) % XS) * CS + c) for x in range(XS) for c in range(CS)]


def exchange(member, axis, groups=None):
    return lax.all_to_all(member, axis, 0, 0, tiled=True, axis_index_groups=groups)


def after(values, *others):
    return lax.optimization_barrier((values, others))[0]


def block(shape):
    return pl.BlockSpec(shape, lambda i, *s: (0,) * len(shape))


def dot_t(a, b):
    return lax.dot_general(a, b, (((1,), (1,)), ((), ())), preferred_element_type=F32)


def dot_0(a, b):
    return lax.dot_general(a, b, (((0,), (0,)), ((), ())), preferred_element_type=F32)


def call(kernel, name, scalars, in_specs, out_specs, out_shape, scratch, cost, vmem=None):
    params = pltpu.CompilerParams(vmem_limit_bytes=vmem and vmem * 2**20)
    return pl.pallas_call(
        kernel,
        name=name,
        out_shape=out_shape,
        grid_spec=pltpu.PrefetchScalarGridSpec(
            num_scalar_prefetch=scalars,
            grid=(1,),
            in_specs=in_specs,
            out_specs=out_specs,
            scratch_shapes=scratch,
        ),
        compiler_params=params,
        cost_estimate=pl.CostEstimate(flops=cost[0], bytes_accessed=cost[1], transcendentals=0),
    )


def order_heads(flags, order):
    def place(h, ones):
        flag = flags[h]
        order[jnp.where(flag > 0, HEADS // 2 + ones, h - ones)] = h
        return ones + jnp.where(flag > 0, 1, 0)

    lax.fori_loop(0, HEADS, place, 0, unroll=True)


def fetch_heads(heads, places, fq_ref, fk_ref, fv_ref, go_ref, up_ref, q_in, v_in, up_in, sems):
    copies = []
    for p, (head, (buffer, entry)) in enumerate(zip(heads, places)):
        cols = pl.ds(pl.multiple_of(head * HD, HD), HD)
        own = pl.ds(p * HD, HD)
        spots = (
            (up_ref, up_in.at[:, own]),
            (fq_ref, q_in.at[:, own]),
            (fv_ref, v_in.at[:, own]),
            (fk_ref, buffer.at[(*entry[:-1], slice(None), pl.ds(entry[-1] + HD, HD))]),
            (go_ref, buffer.at[(*entry[:-1], slice(None), pl.ds(entry[-1] + 3 * HD, HD))]),
        )
        for t, (ref, spot) in enumerate(spots):
            copies.append(pltpu.make_async_copy(ref.at[:, cols], spot, sems.at[p, t]))
            copies[-1].start()
    return copies


def raise_heads(low, copies, places, q_in, v_in, up_in):
    lanes = lax.broadcasted_iota(jnp.int32, (ROWS, BOTH), 1)
    none = jnp.zeros_like(low)
    lows = jnp.concatenate([jnp.where(lanes < RANK, low, none), jnp.where(lanes < RANK, none, low)], axis=0)
    for copy in copies:
        copy.wait()
    raised = jnp.dot(lows, up_in[...], preferred_element_type=F32)
    for p, (buffer, entry) in enumerate(places):
        own = slice(p * HD, (p + 1) * HD)
        q = (q_in[:, own].astype(F32) + adapter_scale * raised[:ROWS, own]).astype(BF16)
        v = (v_in[:, own].astype(F32) + adapter_scale * raised[ROWS:, own]).astype(BF16)
        buffer[(*entry[:-1], slice(None), pl.ds(entry[-1], HD))] = q
        buffer[(*entry[:-1], slice(None), pl.ds(entry[-1] + 2 * HD, HD))] = v


HALF = HEADS // 2


def head_scratch(count):
    return [
        pltpu.VMEM((ROWS, count * HD), BF16),
        pltpu.VMEM((ROWS, count * HD), BF16),
        pltpu.VMEM((BOTH, count * HD), BF16),
        pltpu.SemaphoreType.DMA((count, 5)),
    ]


def prepare_plain_kernel(flags, x_hbm, down_hbm, *refs):
    frozen, (out_ref, order, spot, low_ref, x_in, down_in, whole_sems, q_in, v_in, up_in, sems) = refs[:5], refs[5:]
    wholes = [
        pltpu.make_async_copy(x_hbm, x_in, whole_sems.at[0]),
        pltpu.make_async_copy(down_hbm, down_in, whole_sems.at[1]),
    ]
    for copy in wholes:
        copy.start()
    order_heads(flags, order)
    me = lax.axis_index("ulysses")
    spot[SPOT_Y] = me % YS
    spot[SPOT_PLAIN] = me % MEMBERS
    spot[SPOT_SHIFT] = (me + YS) % MEMBERS
    spot[SPOT_OWN_PLAIN] = me // YS % 2 * PLANE
    spot[SPOT_OWN_SHIFT] = (1 - me // YS % 2) * PLANE
    places = [(out_ref, (p % MEMBERS, p // MEMBERS * 4 * HD)) for p in range(HALF)]
    copies = fetch_heads([order[p] for p in range(HALF)], places, *frozen, q_in, v_in, up_in, sems)
    for copy in wholes:
        copy.wait()
    low = dot_t(x_in[...], down_in[...]).astype(BF16)
    low_ref[...] = low
    raise_heads(low, copies, places, q_in, v_in, up_in)


def prepare_plain(flags, x, down, frozen):
    return call(
        prepare_plain_kernel,
        "prepare_plain",
        1,
        [ANYWHERE] * 7,
        [block((MEMBERS, ROWS, 8 * HD)), SCALARS, SCALARS, block((ROWS, BOTH))],
        (
            jax.ShapeDtypeStruct((MEMBERS, ROWS, 8 * HD), BF16),
            jax.ShapeDtypeStruct((HEADS,), jnp.int32),
            jax.ShapeDtypeStruct((MEMBERS,), jnp.int32),
            jax.ShapeDtypeStruct((ROWS, BOTH), BF16),
        ),
        [pltpu.VMEM((ROWS, WIDTH), BF16), pltpu.VMEM((BOTH, WIDTH), BF16), pltpu.SemaphoreType.DMA((2,))]
        + head_scratch(HALF),
        (10**9, 8 * 10**6),
    )(flags, x, down, *frozen)


def prepare_shifted_kernel(item, order, spot, low_ref, *refs):
    frozen, outs, scratch = refs[:5], refs[5:7], refs[7:]
    y, own_half = spot[SPOT_Y], spot[SPOT_OWN_SHIFT] // PLANE
    heads, places = [], []
    for other in range(2):
        for step in range(YS):
            seat = (own_half + other) % 2 * YS + ((y + step) % YS if item == 2 else step)
            heads.append(order[item * MEMBERS + seat])
            places.append((outs[other], (step, 0)))
    copies = fetch_heads(heads, places, *frozen, *scratch)
    raise_heads(low_ref[...], copies, places, *scratch[:3])


def prepare_shifted(item, order, spot, low, frozen):
    def body(*refs):
        prepare_shifted_kernel(item, *refs)

    return call(
        body,
        "prepare_third" if item == 2 else "prepare_last",
        2,
        [block((ROWS, BOTH))] + [ANYWHERE] * 5,
        [block((YS, ROWS, 4 * HD))] * 2,
        (jax.ShapeDtypeStruct((YS, ROWS, 4 * HD), BF16),) * 2,
        head_scratch(MEMBERS),
        (10**9, 8 * 10**6),
    )(order, spot, low, *frozen)


def pack_kernel(low_ref, own_ref, other_ref, *out_refs):
    for dy, out_ref in enumerate(out_refs, 1):
        out_ref[:, pl.ds(0, 4 * HD)] = own_ref[dy]
        out_ref[:, pl.ds(4 * HD, 4 * HD)] = other_ref[dy]
        out_ref[:, pl.ds(8 * HD, BOTH)] = low_ref[...]


def pack(low, own, other):
    shape = (ROWS, 8 * HD + BOTH)
    return call(
        pack_kernel,
        "pack_first",
        0,
        [block(low.shape)] + [block(own.shape)] * 2,
        [block(shape)] * 3,
        (jax.ShapeDtypeStruct(shape, BF16),) * 3,
        [],
        (0, 4 * 10**6),
    )(low, own, other)


def turn_kernel(spot, x_ref, *out_refs):
    x, core = spot[0] // CS, spot[0] % CS
    *out_refs, stage = out_refs
    for u in range(HEADS):
        stage[pl.ds(u * HD, HD), :] = x_ref[:, pl.ds(u * HD, HD)].T
    for step, out_ref in enumerate(out_refs):
        for other in range(CS):
            d = (x + step) % XS * CS + (core + other) % CS
            for u in range(HEADS):
                rows = pl.ds(pl.multiple_of(u * HD + d * PIECE, PIECE), PIECE)
                out_ref[other, pl.ds(u * PIECE, PIECE), :] = stage[rows, :]


def turn(place, x):
    shape = (CS, HEADS * PIECE, ROWS)
    return call(
        turn_kernel,
        "turn_input",
        1,
        [block(x.shape)],
        [block(shape)] * XS,
        (jax.ShapeDtypeStruct(shape, BF16),) * XS,
        [pltpu.VMEM((WIDTH, ROWS), BF16)],
        (10**9, 2 * 10**6),
    )(place, x)


def attend(x_ref, up, grads_ref, column, dv_acc, arrive):
    factor = 1.0 / math.sqrt(HD)
    bend = factor * math.log2(math.e)
    row_ids = lax.broadcasted_iota(jnp.int32, (RB, RB), 0)
    column_ids = lax.broadcasted_iota(jnp.int32, (RB, RB), 1)
    keep = column_ids <= row_ids
    for i in range(GROUP // RB):
        arrive(i)
        n = (i + 1) * RB
        rows = pl.ds(i * RB, RB)
        q = x_ref[rows, pl.ds(0, HD)]
        g = x_ref[rows, pl.ds(3 * HD, HD)]
        k = x_ref[pl.ds(0, n), pl.ds(HD, HD)]
        v = x_ref[pl.ds(0, n), pl.ds(2 * HD, HD)]
        scores = dot_t(q, k)
        last = jnp.where(keep, scores[:, i * RB :], -1e30)
        scores = last if i == 0 else jnp.concatenate([scores[:, : i * RB], last], axis=1)
        top = jnp.max(scores, axis=1, keepdims=True)
        weights = jnp.exp2((scores - top) * bend)
        total = jnp.sum(weights, axis=1, keepdims=True)
        attention = (weights * (1.0 / total)).astype(BF16)
        output = jnp.dot(attention, v, preferred_element_type=F32)
        grad_attention = dot_t(g, v)
        center = jnp.sum(g.astype(F32) * output, axis=1, keepdims=True)
        grad_scores = (attention.astype(F32) * (grad_attention - center)).astype(BF16)
        dq = jnp.dot(grad_scores, k, preferred_element_type=F32) * factor
        grads_ref[rows, pl.ds(column, HD)] = dq.astype(BF16)
        dv = dot_0(attention, g)
        if i:
            dv_acc[pl.ds(0, i * RB), :] += dv[: i * RB]
        dv_acc[rows, :] = dv[i * RB :]
    dq = grads_ref[:, pl.ds(column, HD)]
    dv = dv_acc[...].astype(BF16)
    grads_ref[:, pl.ds(column + HD, HD)] = dv
    lanes = lax.broadcasted_iota(jnp.int32, (GROUP, BOTH), 1)
    return jnp.where(lanes < RANK, dot_t(dq, up), dot_t(dv, up))


def attention_plain_kernel(order, spot, arrived, up_a, up_b, mine_ref, theirs_ref, grads_ref, xs, dv_acc, total, sems):
    copies = []
    for item in range(2):
        for i in range(GROUP // RB):
            rows = pl.ds(i * RB, RB)
            source = arrived.at[rows, pl.ds(item * 4 * HD, 4 * HD)]
            copies.append(pltpu.make_async_copy(source, xs.at[item, rows, :], sems.at[item, i]))
            copies[-1].start()
    arrive = lambda i: copies[i].wait()
    total[...] = attend(xs.at[0], up_a[...], grads_ref, 0, dv_acc, arrive)
    arrive = lambda i: copies[GROUP // RB + i].wait()
    total[...] += attend(xs.at[1], up_b[...], grads_ref, 2 * HD, dv_acc, arrive)
    own = pl.multiple_of(spot[SPOT_OWN_PLAIN], PLANE)
    mine_ref[...] = total[pl.ds(own, PLANE), :]
    theirs_ref[...] = total[pl.ds(PLANE - own, PLANE), :].astype(BF16)


def up_columns(item):
    seat = SPOT_PLAIN if item < 2 else SPOT_SHIFT
    return pl.BlockSpec((BOTH, HD), lambda i, order, spot: (0, order[item * MEMBERS + spot[seat]]))


def attention_plain(order, spot, arrived, up):
    shapes = [((PLANE, BOTH), F32), ((PLANE, BOTH), BF16), ((GROUP, 4 * HD), BF16)]
    return call(
        attention_plain_kernel,
        "attention_plain",
        2,
        [ANYWHERE, up_columns(0), up_columns(1)],
        [block(shape) for shape, _ in shapes],
        [jax.ShapeDtypeStruct(*shape) for shape in shapes],
        [
            pltpu.VMEM((2, GROUP, 4 * HD), BF16),
            pltpu.VMEM((GROUP, HD), F32),
            pltpu.VMEM((GROUP, BOTH), F32),
            pltpu.SemaphoreType.DMA((2, GROUP // RB)),
        ],
        (2 * 10**10, 4 * 10**6),
    )(order, spot, arrived.reshape(GROUP, 8 * HD), up, up)


def attention_shifted_kernel(last, order, spot, *refs):
    y, own = spot[SPOT_Y], spot[SPOT_OWN_SHIFT]
    if last:
        arrived, up, before_hbm, mine_hbm, theirs_hbm, back_ref, grads_hbm, x_in, dv_acc, sems = refs[:10]
        total, before_ref, mine_ref, theirs_ref, grads_ref, more_sems = refs[10:]
        blocks = [[arrived.at[s, half] for half in range(2)] for s in range(YS)]
        sources = range(YS)
    else:
        low_ref, own_ref, other_ref, *pieces = refs[:6]
        up, back_ref, grads_ref, lows_ref, x_in, dv_acc, sems = refs[6:]
        blocks = [[own_ref.at[0], other_ref.at[0]]]
        for piece in pieces:
            blocks.append([piece.at[:, pl.ds(half * 4 * HD, 4 * HD)] for half in range(2)])
        sources = [(y - dy + YS) % YS for dy in range(YS)]
    for t, source in enumerate(sources):
        for half in range(2):
            at = (own if half == 0 else PLANE - own) // ROWS + source
            rows = pl.ds(pl.multiple_of(at * ROWS, ROWS), ROWS)
            pltpu.make_async_copy(blocks[t][half], x_in.at[rows, :], sems.at[at]).start()

    def arrive(i):
        for at in range(i * RB // ROWS, (i + 1) * RB // ROWS):
            pltpu.make_async_copy(blocks[0][0], x_in.at[pl.ds(at * ROWS, ROWS), :], sems.at[at]).wait()

    if last:
        pairs = ((before_hbm, before_ref), (mine_hbm, mine_ref), (theirs_hbm, theirs_ref))
        others = [pltpu.make_async_copy(*pair, more_sems.at[t]) for t, pair in enumerate(pairs)]
        for copy in others:
            copy.start()
    else:
        sources = [low_ref] + [piece.at[:, pl.ds(8 * HD, BOTH)] for piece in pieces]
        others = [
            pltpu.make_async_copy(source, lows_ref.at[dy], sems.at[MEMBERS + dy])
            for dy, source in enumerate(sources)
        ]
        for copy in others:
            copy.start()
    back = attend(x_in, up[...], grads_ref, 0, dv_acc, arrive)
    if not last:
        back_ref[...] = back
        for copy in others:
            copy.wait()
        return
    save = pltpu.make_async_copy(grads_ref, grads_hbm, more_sems.at[3])
    save.start()
    for copy in others:
        copy.wait()
    total[...] = back + before_ref[...]
    mine_rows = pl.ds(pl.multiple_of(own, PLANE), PLANE)
    total[mine_rows, :] += mine_ref[...] + theirs_ref[...].astype(F32)
    back_ref[...] = total[...].astype(BF16)
    save.wait()


LAST_SCRATCH = [
    pltpu.VMEM((GROUP, BOTH), F32),
    pltpu.VMEM((GROUP, BOTH), F32),
    pltpu.VMEM((PLANE, BOTH), F32),
    pltpu.VMEM((PLANE, BOTH), BF16),
    pltpu.VMEM((GROUP, 2 * HD), BF16),
    pltpu.SemaphoreType.DMA((4,)),
]


def attention_shifted(item, order, spot, arrived, up, *more):
    last = len(more) > 0
    shapes = [((GROUP, BOTH), BF16 if last else F32), ((GROUP, 2 * HD), BF16)]
    if not last:
        shapes.append(((YS, ROWS, BOTH), BF16))

    def body(*refs):
        attention_shifted_kernel(last, *refs)

    return call(
        body,
        "attention_last" if last else "attention_third",
        2,
        [pl.BlockSpec(memory_space=pl.ANY) if last else ANYWHERE] * len(arrived)
        + [up_columns(item)]
        + [ANYWHERE] * len(more),
        [block(shapes[0][0]), ANYWHERE] if last else [block(shape) for shape, _ in shapes],
        [jax.ShapeDtypeStruct(*shape) for shape in shapes],
        [pltpu.VMEM((GROUP, 4 * HD), BF16), pltpu.VMEM((GROUP, HD), F32), pltpu.SemaphoreType.DMA((3 * YS,))]
        + LAST_SCRATCH * last,
        (4 * 10**9, 3 * 10**6) if last else (10**6, 10**4),
    )(order, spot, *arrived, up, *more)


def up_gradient_kernel(spot, own_ref, later_ref, earlier_ref, *refs):
    out_ref, low_a, low_b = refs[-3:]
    y = spot[SPOT_Y]

    def fill(low, first, second):
        for half, ref in enumerate((first, second)):
            for s in range(YS):
                low[pl.ds(half * PLANE + s * ROWS, ROWS), :] = ref[(y - s + YS) % YS]

    @pl.when(spot[SPOT_OWN_PLAIN] == 0)
    def _():
        fill(low_a, own_ref, later_ref)
        fill(low_b, earlier_ref, own_ref)

    @pl.when(spot[SPOT_OWN_PLAIN] != 0)
    def _():
        fill(low_a, earlier_ref, own_ref)
        fill(low_b, own_ref, later_ref)

    for item in range(4):
        low = (low_a, low_b)[item // 2][...]
        grads, column = ((refs[0], 0), (refs[0], 2 * HD), (refs[1], 0), (refs[2], 0))[item]
        for m in range(2):
            columns = pl.ds(column + m * HD, HD)
            part = adapter_scale * dot_0(low[:, m * RANK : (m + 1) * RANK], grads[:, columns])
            part = part.astype(BF16)
            for e in range(RANK // PIECE):
                d = m * (RANK // PIECE) + e
                out_ref[d, pl.ds(item * PIECE, PIECE), :] = part[e * PIECE : (e + 1) * PIECE]


def up_gradients(spot, own, later, earlier, grads):
    shape = (SLICES, 4 * PIECE, HD)
    return call(
        up_gradient_kernel,
        "up_gradients",
        1,
        [block((YS, ROWS, BOTH))] * 3 + [block(array.shape) for array in grads],
        block(shape),
        jax.ShapeDtypeStruct(shape, BF16),
        [pltpu.VMEM((GROUP, BOTH), BF16)] * 2,
        (2 * 10**9, 3 * 10**6),
        16,
    )(spot, own, later, earlier, *grads)


def gather_kernel(summed_ref, ups_ref, out_ref):
    back = jnp.sum(summed_ref[...].astype(F32), axis=0).astype(BF16)
    for d in range(SLICES):
        out_ref[d, pl.ds(0, ROWS), :] = back
    out_ref[:, pl.ds(ROWS, 4 * PIECE), :] = ups_ref[...]


def gather_parts(summed, ups):
    shape = (SLICES, ROWS + 4 * PIECE, HD)
    return call(
        gather_kernel,
        "gather_parts",
        0,
        [block(summed.shape), block(ups.shape)],
        block(shape),
        jax.ShapeDtypeStruct(shape, BF16),
        [],
        (10**7, 10**6),
        16,
    )(summed, ups)


def merge_kernel(order, spot, place, both_ref, *refs):
    x_refs, crossed_ref, out_ref = refs[:-2], refs[-2], refs[-1]
    x, core = place[0] // CS, place[0] % CS
    total = jnp.zeros((HEADS * PIECE, BOTH), F32)
    for dx in range(XS):
        for other in range(CS):
            s = (x - dx + XS) % XS * CS + (core + other) % CS
            back = both_ref[s, pl.ds(0, ROWS), :]
            part = x_refs[dx][0] if other == 0 else crossed_ref[dx]
            total += jnp.dot(part, back, preferred_element_type=F32)
    total = (adapter_scale * total).astype(BF16)
    for u in range(HEADS):
        out_ref[u, pl.ds(0, PIECE), :] = total[u * PIECE : (u + 1) * PIECE]
        out_ref[u, pl.ds(PIECE, PIECE), :] = jnp.zeros((PIECE, HD), BF16)
    ups = jnp.sum(both_ref[:, pl.ds(ROWS, 4 * PIECE), :].astype(F32), axis=0).astype(BF16)
    for item in range(4):
        seat = spot[SPOT_PLAIN if item < 2 else SPOT_SHIFT]
        head = order[item * MEMBERS + seat]
        out_ref[head, pl.ds(PIECE, PIECE), :] = ups[item * PIECE : (item + 1) * PIECE]


def merge(order, spot, place, both, pieces, crossed):
    shape = (HEADS, 2 * PIECE, HD)
    return call(
        merge_kernel,
        "merge_gradients",
        3,
        [block(both.shape)] + [block((1, *piece.shape[1:])) for piece in pieces] + [block(crossed.shape)],
        block(shape),
        jax.ShapeDtypeStruct(shape, BF16),
        [],
        (2 * 10**8, 2 * 10**6),
        16,
    )(order, spot, place, both, *pieces, crossed)


def spread_kernel(in_ref, out_ref):
    total = jnp.sum(in_ref[...].astype(F32), axis=0)
    for d in range(SLICES):
        out_ref[d] = total


def spread(both):
    shape = (SLICES, 2 * PIECE, HD)
    return call(
        spread_kernel,
        "spread_sums",
        0,
        [block(both.shape)],
        block(shape),
        jax.ShapeDtypeStruct(shape, F32),
        [],
        (10**6, 10**6),
        16,
    )(both)


def finish_kernel(in_ref, down_ref, up_ref):
    down = in_ref[:, pl.ds(0, PIECE), :].reshape(HD, BOTH).T
    up = in_ref[:, pl.ds(PIECE, PIECE), :].reshape(BOTH, HD)
    for m in range(2):
        down_ref[m] = down[m * RANK : (m + 1) * RANK]
        up_ref[m] = up[m * RANK : (m + 1) * RANK]


def finish(both):
    shape = (2, RANK, HD)
    return call(
        finish_kernel,
        "finish",
        0,
        [block(both.shape)],
        [block(shape)] * 2,
        [jax.ShapeDtypeStruct(shape, F32)] * 2,
        [],
        (10**6, 10**6),
        16,
    )(both)


def per_device(
    normalized_input,
    frozen_queries,
    frozen_keys,
    frozen_values,
    output_gradient,
    adapter_down_maps,
    adapter_up_maps,
    shifted,
):
    tokens = normalized_input[0]
    place = lax.axis_index("dp").reshape(1)
    up = adapter_up_maps.reshape(BOTH, WIDTH)
    down = adapter_down_maps.transpose(0, 2, 1).reshape(BOTH, WIDTH)

    frozen = (frozen_queries[0], frozen_keys[0], frozen_values[0], output_gradient[0], up)
    sent, order, spot, low = prepare_plain(shifted.astype(jnp.int32), tokens, down, frozen)
    plain = exchange(sent, "ulysses", PLAIN_GROUPS)
    own_c, other_c = prepare_shifted(2, order, spot, low, frozen)
    other_c = lax.ppermute(other_c, "ulysses", SHIFT_SWAP)
    own_d, other_d = prepare_shifted(3, order, spot, after(low, own_c), frozen)
    turned = turn(place, after(tokens, own_d))
    pieces = [turned[0]] + [lax.ppermute(turned[dx], "dp", x_shift(dx)) for dx in (1, 2, 3)]
    other_d, other_c = after((other_d, other_c), turned)
    other_d = lax.ppermute(other_d, "ulysses", SHIFT_SWAP)

    packed = pack(low, own_c, other_c)
    arrived_c = [lax.ppermute(packed[dy - 1], "ulysses", y_shift(dy)) for dy in (1, 2, 3)]
    sent = jnp.stack([own_d, other_d], axis=1)
    crossed = jnp.stack([piece[1] for piece in pieces])
    plain, pieces, sent, crossed = after((plain, pieces, sent, crossed), packed)

    arrived_d = exchange(sent, "ulysses", Y_GROUPS)
    crossed = lax.ppermute(crossed, "dp", CORE_SWAP)
    mine, theirs, grads_plain = attention_plain(order, spot, plain, up)
    theirs = lax.ppermute(theirs, "ulysses", PLAIN_SWAP)
    arrived_c = after(arrived_c, grads_plain, sent)
    partial, grads_c, own = attention_shifted(2, order, spot, [low, own_c, other_c, *arrived_c], up)
    later = lax.ppermute(own, "ulysses", z_shift(-1))
    earlier = lax.ppermute(own, "ulysses", z_shift(1))

    arrived_d, theirs, crossed = after((arrived_d, theirs, crossed), partial)
    partial, grads_d = attention_shifted(3, order, spot, [arrived_d], up, partial, mine, theirs)
    summed = exchange(partial.reshape(MEMBERS, ROWS, BOTH), "ulysses", SHIFT_GROUPS)
    ups = up_gradients(spot, own, later, earlier, (grads_plain, grads_c, grads_d))
    both = exchange(gather_parts(summed, ups), "dp")
    both = exchange(merge(order, spot, place, both, pieces, crossed), "ulysses")
    both = exchange(spread(both), "dp")
    grad_down, grad_up = finish(both)
    return (grad_down.transpose(0, 2, 1), grad_up)


def solution(mesh):
    rows = P("dp", "ulysses", None)
    in_specs = (rows, rows, rows, rows, rows, P(), P(), P())
    out_specs = (P(None, "ulysses", None), P(None, None, "ulysses"))
    return jax.shard_map(
        per_device, mesh=mesh, in_specs=in_specs, out_specs=out_specs, check_vma=False
    )
```

```python
import math

import jax
import jax.numpy as jnp
from jax import lax
from jax.experimental import pallas as pl
from jax.experimental.pallas import tpu as pltpu
from jax.sharding import PartitionSpec as P

HEADS = 32
HD = 128
WIDTH = HEADS * HD
GROUP = 1024
PLANE = 512
RANK = 64
BOTH = 2 * RANK
ROWS = 128
ZS, YS = 8, 4
XS, CS = 4, 2
SLICES = XS * CS
MEMBERS = 8
PIECE = 16
RB = 256
BF16, F32 = jnp.bfloat16, jnp.float32

adapter_scale = 0.5

PLAIN_GROUPS = [[MEMBERS * g + i for i in range(MEMBERS)] for g in range(4)]
SHIFT_GROUPS = [[(MEMBERS * g + 4 + i) % HEADS for i in range(MEMBERS)] for g in range(4)]
PLAIN_SWAP = [(u, u ^ 4) for u in range(HEADS)]
SHIFT_SWAP = [(u, (((u + 4) % HEADS ^ 4) - 4) % HEADS) for u in range(HEADS)]
CORE_SWAP = [(d, d ^ 1) for d in range(SLICES)]
ANYWHERE = pl.BlockSpec(memory_space=pltpu.HBM)
SCALARS = pl.BlockSpec(memory_space=pltpu.SMEM)

SPOT_Y, SPOT_PLAIN, SPOT_SHIFT, SPOT_OWN_PLAIN, SPOT_OWN_SHIFT = range(5)


def z_shift(dz):
    return [(z * YS + y, ((z + dz) % ZS) * YS + y) for z in range(ZS) for y in range(YS)]


def y_shift(dy):
    return [(z * YS + y, z * YS + (y + dy) % YS) for z in range(ZS) for y in range(YS)]


def x_shift(dx):
    return [(x * CS + c, ((x + dx) % XS) * CS + c) for x in range(XS) for c in range(CS)]


def exchange(member, axis, groups=None):
    return lax.all_to_all(member, axis, 0, 0, tiled=True, axis_index_groups=groups)


def after(values, *others):
    return lax.optimization_barrier((values, others))[0]


def block(shape):
    return pl.BlockSpec(shape, lambda i, *s: (0,) * len(shape))


def dot_t(a, b):
    return lax.dot_general(a, b, (((1,), (1,)), ((), ())), preferred_element_type=F32)


def dot_0(a, b):
    return lax.dot_general(a, b, (((0,), (0,)), ((), ())), preferred_element_type=F32)


def call(kernel, name, scalars, in_specs, out_specs, out_shape, scratch, cost, vmem=None):
    params = pltpu.CompilerParams(vmem_limit_bytes=vmem and vmem * 2**20)
    return pl.pallas_call(
        kernel,
        name=name,
        out_shape=out_shape,
        grid_spec=pltpu.PrefetchScalarGridSpec(
            num_scalar_prefetch=scalars,
            grid=(1,),
            in_specs=in_specs,
            out_specs=out_specs,
            scratch_shapes=scratch,
        ),
        compiler_params=params,
        cost_estimate=pl.CostEstimate(flops=cost[0], bytes_accessed=cost[1], transcendentals=0),
    )


def order_heads(flags, order):
    def place(h, ones):
        flag = flags[h]
        order[jnp.where(flag > 0, HEADS // 2 + ones, h - ones)] = h
        return ones + jnp.where(flag > 0, 1, 0)

    lax.fori_loop(0, HEADS, place, 0, unroll=True)


def fetch_heads(heads, places, fq_ref, fk_ref, fv_ref, go_ref, up_ref, q_in, v_in, up_in, sems):
    copies = []
    for p, (head, (buffer, entry)) in enumerate(zip(heads, places)):
        cols = pl.ds(pl.multiple_of(head * HD, HD), HD)
        own = pl.ds(p * HD, HD)
        spots = (
            (up_ref, up_in.at[:, own]),
            (fq_ref, q_in.at[:, own]),
            (fv_ref, v_in.at[:, own]),
            (fk_ref, buffer.at[(*entry[:-1], slice(None), pl.ds(entry[-1] + HD, HD))]),
            (go_ref, buffer.at[(*entry[:-1], slice(None), pl.ds(entry[-1] + 3 * HD, HD))]),
        )
        for t, (ref, spot) in enumerate(spots):
            copies.append(pltpu.make_async_copy(ref.at[:, cols], spot, sems.at[p, t]))
            copies[-1].start()
    return copies


def raise_heads(low, copies, places, q_in, v_in, up_in):
    lanes = lax.broadcasted_iota(jnp.int32, (ROWS, BOTH), 1)
    none = jnp.zeros_like(low)
    lows = jnp.concatenate([jnp.where(lanes < RANK, low, none), jnp.where(lanes < RANK, none, low)], axis=0)
    for copy in copies:
        copy.wait()
    raised = jnp.dot(lows, up_in[...], preferred_element_type=F32)
    for p, (buffer, entry) in enumerate(places):
        own = slice(p * HD, (p + 1) * HD)
        q = (q_in[:, own].astype(F32) + adapter_scale * raised[:ROWS, own]).astype(BF16)
        v = (v_in[:, own].astype(F32) + adapter_scale * raised[ROWS:, own]).astype(BF16)
        buffer[(*entry[:-1], slice(None), pl.ds(entry[-1], HD))] = q
        buffer[(*entry[:-1], slice(None), pl.ds(entry[-1] + 2 * HD, HD))] = v


HALF = HEADS // 2


def head_scratch(count):
    return [
        pltpu.VMEM((ROWS, count * HD), BF16),
        pltpu.VMEM((ROWS, count * HD), BF16),
        pltpu.VMEM((BOTH, count * HD), BF16),
        pltpu.SemaphoreType.DMA((count, 5)),
    ]


def prepare_plain_kernel(flags, x_hbm, down_hbm, *refs):
    frozen, (out_ref, order, spot, low_ref, x_in, down_in, whole_sems, q_in, v_in, up_in, sems) = refs[:5], refs[5:]
    wholes = [
        pltpu.make_async_copy(x_hbm, x_in, whole_sems.at[0]),
        pltpu.make_async_copy(down_hbm, down_in, whole_sems.at[1]),
    ]
    for copy in wholes:
        copy.start()
    order_heads(flags, order)
    me = lax.axis_index("ulysses")
    spot[SPOT_Y] = me % YS
    spot[SPOT_PLAIN] = me % MEMBERS
    spot[SPOT_SHIFT] = (me + YS) % MEMBERS
    spot[SPOT_OWN_PLAIN] = me // YS % 2 * PLANE
    spot[SPOT_OWN_SHIFT] = (1 - me // YS % 2) * PLANE
    places = [(out_ref, (p % MEMBERS, p // MEMBERS * 4 * HD)) for p in range(HALF)]
    copies = fetch_heads([order[p] for p in range(HALF)], places, *frozen, q_in, v_in, up_in, sems)
    for copy in wholes:
        copy.wait()
    low = dot_t(x_in[...], down_in[...]).astype(BF16)
    low_ref[...] = low
    raise_heads(low, copies, places, q_in, v_in, up_in)


def prepare_plain(flags, x, down, frozen):
    return call(
        prepare_plain_kernel,
        "prepare_plain",
        1,
        [ANYWHERE] * 7,
        [block((MEMBERS, ROWS, 8 * HD)), SCALARS, SCALARS, block((ROWS, BOTH))],
        (
            jax.ShapeDtypeStruct((MEMBERS, ROWS, 8 * HD), BF16),
            jax.ShapeDtypeStruct((HEADS,), jnp.int32),
            jax.ShapeDtypeStruct((MEMBERS,), jnp.int32),
            jax.ShapeDtypeStruct((ROWS, BOTH), BF16),
        ),
        [pltpu.VMEM((ROWS, WIDTH), BF16), pltpu.VMEM((BOTH, WIDTH), BF16), pltpu.SemaphoreType.DMA((2,))]
        + head_scratch(HALF),
        (10**9, 8 * 10**6),
    )(flags, x, down, *frozen)


def prepare_third_kernel(order, spot, low_ref, *refs):
    frozen, outs, scratch = refs[:5], refs[5:7], refs[7:]
    y, own_half = spot[SPOT_Y], spot[SPOT_OWN_SHIFT] // PLANE
    heads, places = [], []
    for other in range(2):
        for dy in range(YS):
            seat = (own_half + other) % 2 * YS + (y + dy) % YS
            heads.append(order[2 * MEMBERS + seat])
            places.append((outs[other], (dy, 0)))
    copies = fetch_heads(heads, places, *frozen, *scratch)
    raise_heads(low_ref[...], copies, places, *scratch[:3])


def prepare_last_kernel(order, spot, low_ref, *refs):
    frozen, out_ref, scratch = refs[:5], refs[5], refs[6:]
    heads = [order[3 * MEMBERS + seat] for seat in range(MEMBERS)]
    places = [(out_ref, (seat, 0)) for seat in range(MEMBERS)]
    copies = fetch_heads(heads, places, *frozen, *scratch)
    raise_heads(low_ref[...], copies, places, *scratch[:3])


def prepare_shifted(item, order, spot, low, frozen):
    shapes = [(YS, ROWS, 4 * HD)] * 2 if item == 2 else [(MEMBERS, ROWS, 4 * HD)]
    return call(
        prepare_third_kernel if item == 2 else prepare_last_kernel,
        "prepare_third" if item == 2 else "prepare_last",
        2,
        [block((ROWS, BOTH))] + [ANYWHERE] * 5,
        [block(shape) for shape in shapes],
        [jax.ShapeDtypeStruct(shape, BF16) for shape in shapes],
        head_scratch(MEMBERS),
        (10**9, 8 * 10**6),
    )(order, spot, low, *frozen)


def pack_kernel(low_ref, own_ref, other_ref, *out_refs):
    for dy, out_ref in enumerate(out_refs, 1):
        out_ref[:, pl.ds(0, 4 * HD)] = own_ref[dy]
        out_ref[:, pl.ds(4 * HD, 4 * HD)] = other_ref[dy]
        out_ref[:, pl.ds(8 * HD, BOTH)] = low_ref[...]


def pack(low, own, other):
    shape = (ROWS, 8 * HD + BOTH)
    return call(
        pack_kernel,
        "pack_first",
        0,
        [block(low.shape)] + [block(own.shape)] * 2,
        [block(shape)] * 3,
        (jax.ShapeDtypeStruct(shape, BF16),) * 3,
        [],
        (0, 4 * 10**6),
    )(low, own, other)


def turn_kernel(spot, x_ref, *out_refs):
    x, core = spot[0] // CS, spot[0] % CS
    *out_refs, stage = out_refs
    for u in range(HEADS):
        stage[pl.ds(u * HD, HD), :] = x_ref[:, pl.ds(u * HD, HD)].T
    for step, out_ref in enumerate(out_refs):
        for other in range(CS):
            d = (x + step) % XS * CS + (core + other) % CS
            for u in range(HEADS):
                rows = pl.ds(pl.multiple_of(u * HD + d * PIECE, PIECE), PIECE)
                out_ref[other, pl.ds(u * PIECE, PIECE), :] = stage[rows, :]


def turn(place, x):
    shape = (CS, HEADS * PIECE, ROWS)
    return call(
        turn_kernel,
        "turn_input",
        1,
        [block(x.shape)],
        [block(shape)] * XS,
        (jax.ShapeDtypeStruct(shape, BF16),) * XS,
        [pltpu.VMEM((WIDTH, ROWS), BF16)],
        (10**9, 2 * 10**6),
    )(place, x)


def attend(x_ref, up, grads_ref, column, dv_acc):
    factor = 1.0 / math.sqrt(HD)
    bend = factor * math.log2(math.e)
    row_ids = lax.broadcasted_iota(jnp.int32, (RB, RB), 0)
    column_ids = lax.broadcasted_iota(jnp.int32, (RB, RB), 1)
    keep = column_ids <= row_ids
    for i in range(GROUP // RB):
        n = (i + 1) * RB
        rows = pl.ds(i * RB, RB)
        q = x_ref[rows, pl.ds(0, HD)]
        g = x_ref[rows, pl.ds(3 * HD, HD)]
        k = x_ref[pl.ds(0, n), pl.ds(HD, HD)]
        v = x_ref[pl.ds(0, n), pl.ds(2 * HD, HD)]
        scores = dot_t(q, k)
        last = jnp.where(keep, scores[:, i * RB :], -1e30)
        scores = last if i == 0 else jnp.concatenate([scores[:, : i * RB], last], axis=1)
        top = jnp.max(scores, axis=1, keepdims=True)
        weights = jnp.exp2((scores - top) * bend)
        total = jnp.sum(weights, axis=1, keepdims=True)
        attention = (weights * (1.0 / total)).astype(BF16)
        grad_attention = dot_t(g, v)
        center = jnp.sum(attention.astype(F32) * grad_attention, axis=1, keepdims=True)
        grad_scores = (attention.astype(F32) * (grad_attention - center)).astype(BF16)
        dq = jnp.dot(grad_scores, k, preferred_element_type=F32) * factor
        grads_ref[rows, pl.ds(column, HD)] = dq.astype(BF16)
        dv = dot_0(g, attention)
        if i:
            dv_acc[:, pl.ds(0, i * RB)] += dv[:, : i * RB]
        dv_acc[:, rows] = dv[:, i * RB :]
    dq = grads_ref[:, pl.ds(column, HD)]
    dv = dv_acc[...].T.astype(BF16)
    grads_ref[:, pl.ds(column + HD, HD)] = dv
    lanes = lax.broadcasted_iota(jnp.int32, (GROUP, BOTH), 1)
    return jnp.where(lanes < RANK, dot_t(dq, up), dot_t(dv, up))


def attention_plain_kernel(order, spot, arrived, up_a, up_b, mine_ref, theirs_ref, grads_ref, xs, dv_acc, total, sems):
    copies = []
    for item in range(2):
        source = arrived.at[:, pl.ds(item * 4 * HD, 4 * HD)]
        copies.append(pltpu.make_async_copy(source, xs.at[item], sems.at[item]))
        copies[-1].start()
    copies[0].wait()
    total[...] = attend(xs.at[0], up_a[...], grads_ref, 0, dv_acc)
    copies[1].wait()
    total[...] += attend(xs.at[1], up_b[...], grads_ref, 2 * HD, dv_acc)
    own = pl.multiple_of(spot[SPOT_OWN_PLAIN], PLANE)
    mine_ref[...] = total[pl.ds(own, PLANE), :]
    theirs_ref[...] = total[pl.ds(PLANE - own, PLANE), :].astype(BF16)


def up_columns(item):
    seat = SPOT_PLAIN if item < 2 else SPOT_SHIFT
    return pl.BlockSpec((BOTH, HD), lambda i, order, spot: (0, order[item * MEMBERS + spot[seat]]))


def attention_plain(order, spot, arrived, up):
    shapes = [((PLANE, BOTH), F32), ((PLANE, BOTH), BF16), ((GROUP, 4 * HD), BF16)]
    return call(
        attention_plain_kernel,
        "attention_plain",
        2,
        [ANYWHERE, up_columns(0), up_columns(1)],
        [block(shape) for shape, _ in shapes],
        [jax.ShapeDtypeStruct(*shape) for shape in shapes],
        [
            pltpu.VMEM((2, GROUP, 4 * HD), BF16),
            pltpu.VMEM((HD, GROUP), F32),
            pltpu.VMEM((GROUP, BOTH), F32),
            pltpu.SemaphoreType.DMA((2,)),
        ],
        (2 * 10**10, 4 * 10**6),
    )(order, spot, arrived.reshape(GROUP, 8 * HD), up, up)


def attention_shifted_kernel(last, order, spot, *refs):
    y, own = spot[SPOT_Y], spot[SPOT_OWN_SHIFT]
    if last:
        arrived, up, before_hbm, mine_hbm, theirs_hbm, back_ref, grads_hbm, x_in, dv_acc, sems = refs[:10]
        total, before_ref, mine_ref, theirs_ref, grads_ref, more_sems = refs[10:]
        pltpu.make_async_copy(arrived, x_in, sems.at[0]).start()
    else:
        low_ref, own_ref, other_ref, *pieces = refs[:6]
        up, back_ref, grads_ref, lows_ref, x_in, dv_acc, sems = refs[6:]
        for dy in range(YS):
            for half in range(2):
                at = (own if half == 0 else PLANE - own) // ROWS + (y - dy + YS) % YS
                rows = pl.ds(pl.multiple_of(at * ROWS, ROWS), ROWS)
                if dy == 0:
                    source = (own_ref, other_ref)[half].at[0]
                else:
                    source = pieces[dy - 1].at[:, pl.ds(half * 4 * HD, 4 * HD)]
                pltpu.make_async_copy(source, x_in.at[rows, :], sems.at[2 * dy + half]).start()
    if last:
        pairs = ((before_hbm, before_ref), (mine_hbm, mine_ref), (theirs_hbm, theirs_ref))
        others = [pltpu.make_async_copy(*pair, more_sems.at[t]) for t, pair in enumerate(pairs)]
        for copy in others:
            copy.start()
    else:
        sources = [low_ref] + [piece.at[:, pl.ds(8 * HD, BOTH)] for piece in pieces]
        others = [
            pltpu.make_async_copy(source, lows_ref.at[dy], sems.at[MEMBERS + dy])
            for dy, source in enumerate(sources)
        ]
        for copy in others:
            copy.start()
    if last:
        pltpu.make_async_copy(arrived, x_in, sems.at[0]).wait()
    else:
        for t in range(MEMBERS):
            pltpu.make_async_copy(own_ref.at[0], x_in.at[pl.ds(t * ROWS, ROWS), :], sems.at[t]).wait()
    back = attend(x_in, up[...], grads_ref, 0, dv_acc)
    if not last:
        back_ref[...] = back
        for copy in others:
            copy.wait()
        return
    save = pltpu.make_async_copy(grads_ref, grads_hbm, more_sems.at[3])
    save.start()
    for copy in others:
        copy.wait()
    total[...] = back + before_ref[...]
    mine_rows = pl.ds(pl.multiple_of(own, PLANE), PLANE)
    total[mine_rows, :] += mine_ref[...] + theirs_ref[...].astype(F32)
    back_ref[...] = total[...].astype(BF16)
    save.wait()


LAST_SCRATCH = [
    pltpu.VMEM((GROUP, BOTH), F32),
    pltpu.VMEM((GROUP, BOTH), F32),
    pltpu.VMEM((PLANE, BOTH), F32),
    pltpu.VMEM((PLANE, BOTH), BF16),
    pltpu.VMEM((GROUP, 2 * HD), BF16),
    pltpu.SemaphoreType.DMA((4,)),
]


def attention_shifted(item, order, spot, arrived, up, *more):
    last = len(more) > 0
    shapes = [((GROUP, BOTH), BF16 if last else F32), ((GROUP, 2 * HD), BF16)]
    if not last:
        shapes.append(((YS, ROWS, BOTH), BF16))

    def body(*refs):
        attention_shifted_kernel(last, *refs)

    return call(
        body,
        "attention_last" if last else "attention_third",
        2,
        [pl.BlockSpec(memory_space=pl.ANY) if last else ANYWHERE] * len(arrived)
        + [up_columns(item)]
        + [ANYWHERE] * len(more),
        [block(shapes[0][0]), ANYWHERE] if last else [block(shape) for shape, _ in shapes],
        [jax.ShapeDtypeStruct(*shape) for shape in shapes],
        [pltpu.VMEM((GROUP, 4 * HD), BF16), pltpu.VMEM((HD, GROUP), F32), pltpu.SemaphoreType.DMA((3 * YS,))]
        + LAST_SCRATCH * last,
        (4 * 10**9, 3 * 10**6) if last else (10**6, 10**4),
    )(order, spot, *arrived, up, *more)


def up_gradient_kernel(spot, own_ref, later_ref, earlier_ref, *refs):
    out_ref, low_a, low_b = refs[-3:]
    y = spot[SPOT_Y]

    def fill(low, first, second):
        for half, ref in enumerate((first, second)):
            for s in range(YS):
                low[pl.ds(half * PLANE + s * ROWS, ROWS), :] = ref[(y - s + YS) % YS]

    @pl.when(spot[SPOT_OWN_PLAIN] == 0)
    def _():
        fill(low_a, own_ref, later_ref)
        fill(low_b, earlier_ref, own_ref)

    @pl.when(spot[SPOT_OWN_PLAIN] != 0)
    def _():
        fill(low_a, earlier_ref, own_ref)
        fill(low_b, own_ref, later_ref)

    for item in range(4):
        low = (low_a, low_b)[item // 2][...]
        grads, column = ((refs[0], 0), (refs[0], 2 * HD), (refs[1], 0), (refs[2], 0))[item]
        for m in range(2):
            columns = pl.ds(column + m * HD, HD)
            part = adapter_scale * dot_0(low[:, m * RANK : (m + 1) * RANK], grads[:, columns])
            part = part.astype(BF16)
            for e in range(RANK // PIECE):
                d = m * (RANK // PIECE) + e
                out_ref[d, pl.ds(item * PIECE, PIECE), :] = part[e * PIECE : (e + 1) * PIECE]


def up_gradients(spot, own, later, earlier, grads):
    shape = (SLICES, 4 * PIECE, HD)
    return call(
        up_gradient_kernel,
        "up_gradients",
        1,
        [block((YS, ROWS, BOTH))] * 3 + [block(array.shape) for array in grads],
        block(shape),
        jax.ShapeDtypeStruct(shape, BF16),
        [pltpu.VMEM((GROUP, BOTH), BF16)] * 2,
        (2 * 10**9, 3 * 10**6),
        16,
    )(spot, own, later, earlier, *grads)


def gather_kernel(summed_ref, ups_ref, out_ref):
    back = jnp.sum(summed_ref[...].astype(F32), axis=0).astype(BF16)
    for d in range(SLICES):
        out_ref[d, pl.ds(0, ROWS), :] = back
    out_ref[:, pl.ds(ROWS, 4 * PIECE), :] = ups_ref[...]


def gather_parts(summed, ups):
    shape = (SLICES, ROWS + 4 * PIECE, HD)
    return call(
        gather_kernel,
        "gather_parts",
        0,
        [block(summed.shape), block(ups.shape)],
        block(shape),
        jax.ShapeDtypeStruct(shape, BF16),
        [],
        (10**7, 10**6),
        16,
    )(summed, ups)


def merge_kernel(order, spot, place, both_ref, *refs):
    x_refs, crossed_ref, out_ref = refs[:-2], refs[-2], refs[-1]
    x, core = place[0] // CS, place[0] % CS
    total = jnp.zeros((HEADS * PIECE, BOTH), F32)
    for dx in range(XS):
        for other in range(CS):
            s = (x - dx + XS) % XS * CS + (core + other) % CS
            back = both_ref[s, pl.ds(0, ROWS), :]
            part = x_refs[dx][0] if other == 0 else crossed_ref[dx]
            total += jnp.dot(part, back, preferred_element_type=F32)
    total = (adapter_scale * total).astype(BF16)
    for u in range(HEADS):
        out_ref[u, pl.ds(0, PIECE), :] = total[u * PIECE : (u + 1) * PIECE]
        out_ref[u, pl.ds(PIECE, PIECE), :] = jnp.zeros((PIECE, HD), BF16)
    ups = jnp.sum(both_ref[:, pl.ds(ROWS, 4 * PIECE), :].astype(F32), axis=0).astype(BF16)
    for item in range(4):
        seat = spot[SPOT_PLAIN if item < 2 else SPOT_SHIFT]
        head = order[item * MEMBERS + seat]
        out_ref[head, pl.ds(PIECE, PIECE), :] = ups[item * PIECE : (item + 1) * PIECE]


def merge(order, spot, place, both, pieces, crossed):
    shape = (HEADS, 2 * PIECE, HD)
    return call(
        merge_kernel,
        "merge_gradients",
        3,
        [block(both.shape)] + [block((1, *piece.shape[1:])) for piece in pieces] + [block(crossed.shape)],
        block(shape),
        jax.ShapeDtypeStruct(shape, BF16),
        [],
        (2 * 10**8, 2 * 10**6),
        16,
    )(order, spot, place, both, *pieces, crossed)


def spread_kernel(in_ref, out_ref):
    total = jnp.sum(in_ref[...].astype(F32), axis=0)
    for d in range(SLICES):
        out_ref[d] = total


def spread(both):
    shape = (SLICES, 2 * PIECE, HD)
    return call(
        spread_kernel,
        "spread_sums",
        0,
        [block(both.shape)],
        block(shape),
        jax.ShapeDtypeStruct(shape, F32),
        [],
        (10**6, 10**6),
        16,
    )(both)


def finish_kernel(in_ref, down_ref, up_ref):
    down = in_ref[:, pl.ds(0, PIECE), :].reshape(HD, BOTH).T
    up = in_ref[:, pl.ds(PIECE, PIECE), :].reshape(BOTH, HD)
    for m in range(2):
        down_ref[m] = down[m * RANK : (m + 1) * RANK]
        up_ref[m] = up[m * RANK : (m + 1) * RANK]


def finish(both):
    shape = (2, RANK, HD)
    return call(
        finish_kernel,
        "finish",
        0,
        [block(both.shape)],
        [block(shape)] * 2,
        [jax.ShapeDtypeStruct(shape, F32)] * 2,
        [],
        (10**6, 10**6),
        16,
    )(both)


def per_device(
    normalized_input,
    frozen_queries,
    frozen_keys,
    frozen_values,
    output_gradient,
    adapter_down_maps,
    adapter_up_maps,
    shifted,
):
    tokens = normalized_input[0]
    place = lax.axis_index("dp").reshape(1)
    up = adapter_up_maps.reshape(BOTH, WIDTH)
    down = adapter_down_maps.transpose(0, 2, 1).reshape(BOTH, WIDTH)

    frozen = (frozen_queries[0], frozen_keys[0], frozen_values[0], output_gradient[0], up)
    sent, order, spot, low = prepare_plain(shifted.astype(jnp.int32), tokens, down, frozen)
    plain = exchange(sent, "ulysses", PLAIN_GROUPS)
    own_c, other_c = prepare_shifted(2, order, spot, low, frozen)
    other_c = lax.ppermute(other_c, "ulysses", SHIFT_SWAP)
    turned = turn(place, after(tokens, own_c))
    pieces = [turned[0]] + [lax.ppermute(turned[dx], "dp", x_shift(dx)) for dx in (1, 2, 3)]
    (sent,) = prepare_shifted(3, order, spot, after(low, turned), frozen)

    packed = pack(after(low, pieces, sent), own_c, other_c)
    arrived_c = [lax.ppermute(packed[dy - 1], "ulysses", y_shift(dy)) for dy in (1, 2, 3)]
    plain, pieces, sent = after((plain, pieces, sent), packed)

    arrived_d = exchange(sent, "ulysses", SHIFT_GROUPS).reshape(GROUP, 4 * HD)
    crossed = lax.ppermute(jnp.stack([piece[1] for piece in pieces]), "dp", CORE_SWAP)
    mine, theirs, grads_plain = attention_plain(order, spot, plain, up)
    theirs = lax.ppermute(theirs, "ulysses", PLAIN_SWAP)
    arrived_c = after(arrived_c, grads_plain, sent)
    partial, grads_c, own = attention_shifted(2, order, spot, [low, own_c, other_c, *arrived_c], up)
    later = lax.ppermute(own, "ulysses", z_shift(-1))
    earlier = lax.ppermute(own, "ulysses", z_shift(1))

    arrived_d, theirs, crossed, later, earlier = after((arrived_d, theirs, crossed, later, earlier), partial)
    partial, grads_d = attention_shifted(3, order, spot, [arrived_d], up, partial, mine, theirs)
    summed = exchange(partial.reshape(MEMBERS, ROWS, BOTH), "ulysses", SHIFT_GROUPS)
    ups = up_gradients(spot, own, later, earlier, (grads_plain, grads_c, grads_d))
    both = exchange(gather_parts(summed, ups), "dp")
    both = exchange(merge(order, spot, place, both, pieces, crossed), "ulysses")
    both = exchange(spread(both), "dp")
    grad_down, grad_up = finish(both)
    return (grad_down.transpose(0, 2, 1), grad_up)


def solution(mesh):
    rows = P("dp", "ulysses", None)
    in_specs = (rows, rows, rows, rows, rows, P(), P(), P())
    out_specs = (P(None, "ulysses", None), P(None, None, "ulysses"))
    return jax.shard_map(
        per_device, mesh=mesh, in_specs=in_specs, out_specs=out_specs, check_vma=False
    )
```

```python
import math

import jax
import jax.numpy as jnp
from jax import lax
from jax.experimental import pallas as pl
from jax.experimental.pallas import tpu as pltpu
from jax.sharding import PartitionSpec as P

HEADS = 32
HD = 128
WIDTH = HEADS * HD
GROUP = 1024
PLANE = 512
RANK = 64
BOTH = 2 * RANK
ROWS = 128
ZS, YS = 8, 4
XS, CS = 4, 2
SLICES = XS * CS
MEMBERS = 8
PIECE = 16
RB = 256
BF16, F32 = jnp.bfloat16, jnp.float32

adapter_scale = 0.5

PLAIN_GROUPS = [[MEMBERS * g + i for i in range(MEMBERS)] for g in range(4)]
SHIFT_GROUPS = [[(MEMBERS * g + 4 + i) % HEADS for i in range(MEMBERS)] for g in range(4)]
PLAIN_SWAP = [(u, u ^ 4) for u in range(HEADS)]
SHIFT_SWAP = [(u, (((u + 4) % HEADS ^ 4) - 4) % HEADS) for u in range(HEADS)]
CORE_SWAP = [(d, d ^ 1) for d in range(SLICES)]
ANYWHERE = pl.BlockSpec(memory_space=pltpu.HBM)
SCALARS = pl.BlockSpec(memory_space=pltpu.SMEM)

SPOT_Y, SPOT_PLAIN, SPOT_SHIFT, SPOT_OWN_PLAIN, SPOT_OWN_SHIFT = range(5)


def y_shift(dy):
    return [(z * YS + y, z * YS + (y + dy) % YS) for z in range(ZS) for y in range(YS)]


def x_shift(dx):
    return [(x * CS + c, ((x + dx) % XS) * CS + c) for x in range(XS) for c in range(CS)]


def exchange(member, axis, groups=None):
    return lax.all_to_all(member, axis, 0, 0, tiled=True, axis_index_groups=groups)


def after(values, *others):
    return lax.optimization_barrier((values, others))[0]


def block(shape):
    return pl.BlockSpec(shape, lambda i, *s: (0,) * len(shape))


def dot_t(a, b):
    return lax.dot_general(a, b, (((1,), (1,)), ((), ())), preferred_element_type=F32)


def dot_0(a, b):
    return lax.dot_general(a, b, (((0,), (0,)), ((), ())), preferred_element_type=F32)


def call(kernel, name, scalars, in_specs, out_specs, out_shape, scratch, cost, vmem=None):
    params = pltpu.CompilerParams(vmem_limit_bytes=vmem and vmem * 2**20)
    return pl.pallas_call(
        kernel,
        name=name,
        out_shape=out_shape,
        grid_spec=pltpu.PrefetchScalarGridSpec(
            num_scalar_prefetch=scalars,
            grid=(1,),
            in_specs=in_specs,
            out_specs=out_specs,
            scratch_shapes=scratch,
        ),
        compiler_params=params,
        cost_estimate=pl.CostEstimate(flops=cost[0], bytes_accessed=cost[1], transcendentals=0),
    )


def order_heads(flags, order):
    def place(h, ones):
        flag = flags[h]
        order[jnp.where(flag > 0, HEADS // 2 + ones, h - ones)] = h
        return ones + jnp.where(flag > 0, 1, 0)

    lax.fori_loop(0, HEADS, place, 0, unroll=True)


def fetch_heads(heads, places, fq_ref, fk_ref, fv_ref, go_ref, up_ref, q_in, v_in, up_in, sems):
    copies = []
    for p, (head, (buffer, entry)) in enumerate(zip(heads, places)):
        cols = pl.ds(pl.multiple_of(head * HD, HD), HD)
        own = pl.ds(p * HD, HD)
        spots = (
            (up_ref, up_in.at[:, own]),
            (fq_ref, q_in.at[:, own]),
            (fv_ref, v_in.at[:, own]),
            (fk_ref, buffer.at[(*entry[:-1], slice(None), pl.ds(entry[-1] + HD, HD))]),
            (go_ref, buffer.at[(*entry[:-1], slice(None), pl.ds(entry[-1] + 3 * HD, HD))]),
        )
        for t, (ref, spot) in enumerate(spots):
            copies.append(pltpu.make_async_copy(ref.at[:, cols], spot, sems.at[p, t]))
            copies[-1].start()
    return copies


def raise_heads(low, copies, places, q_in, v_in, up_in):
    lanes = lax.broadcasted_iota(jnp.int32, (ROWS, BOTH), 1)
    none = jnp.zeros_like(low)
    lows = jnp.concatenate([jnp.where(lanes < RANK, low, none), jnp.where(lanes < RANK, none, low)], axis=0)
    for copy in copies:
        copy.wait()
    raised = jnp.dot(lows, up_in[...], preferred_element_type=F32)
    for p, (buffer, entry) in enumerate(places):
        own = slice(p * HD, (p + 1) * HD)
        q = (q_in[:, own].astype(F32) + adapter_scale * raised[:ROWS, own]).astype(BF16)
        v = (v_in[:, own].astype(F32) + adapter_scale * raised[ROWS:, own]).astype(BF16)
        buffer[(*entry[:-1], slice(None), pl.ds(entry[-1], HD))] = q
        buffer[(*entry[:-1], slice(None), pl.ds(entry[-1] + 2 * HD, HD))] = v


HALF = HEADS // 2


def head_scratch(count):
    return [
        pltpu.VMEM((ROWS, count * HD), BF16),
        pltpu.VMEM((ROWS, count * HD), BF16),
        pltpu.VMEM((BOTH, count * HD), BF16),
        pltpu.SemaphoreType.DMA((count, 5)),
    ]


def prepare_plain_kernel(flags, x_hbm, down_hbm, *refs):
    frozen, (out_ref, order, spot, low_ref, x_in, down_in, whole_sems, q_in, v_in, up_in, sems) = refs[:5], refs[5:]
    wholes = [
        pltpu.make_async_copy(x_hbm, x_in, whole_sems.at[0]),
        pltpu.make_async_copy(down_hbm, down_in, whole_sems.at[1]),
    ]
    for copy in wholes:
        copy.start()
    order_heads(flags, order)
    me = lax.axis_index("ulysses")
    spot[SPOT_Y] = me % YS
    spot[SPOT_PLAIN] = me % MEMBERS
    spot[SPOT_SHIFT] = (me + YS) % MEMBERS
    spot[SPOT_OWN_PLAIN] = me // YS % 2 * PLANE
    spot[SPOT_OWN_SHIFT] = (1 - me // YS % 2) * PLANE
    places = [(out_ref, (p % MEMBERS, p // MEMBERS * 4 * HD)) for p in range(HALF)]
    copies = fetch_heads([order[p] for p in range(HALF)], places, *frozen, q_in, v_in, up_in, sems)
    for copy in wholes:
        copy.wait()
    low = dot_t(x_in[...], down_in[...]).astype(BF16)
    low_ref[...] = low
    for seat in range(MEMBERS):
        out_ref[seat, :, pl.ds(8 * HD, BOTH)] = low
    raise_heads(low, copies, places, q_in, v_in, up_in)


def prepare_plain(flags, x, down, frozen):
    return call(
        prepare_plain_kernel,
        "prepare_plain",
        1,
        [ANYWHERE] * 7,
        [block((MEMBERS, ROWS, 8 * HD + BOTH)), SCALARS, SCALARS, block((ROWS, BOTH))],
        (
            jax.ShapeDtypeStruct((MEMBERS, ROWS, 8 * HD + BOTH), BF16),
            jax.ShapeDtypeStruct((HEADS,), jnp.int32),
            jax.ShapeDtypeStruct((MEMBERS,), jnp.int32),
            jax.ShapeDtypeStruct((ROWS, BOTH), BF16),
        ),
        [pltpu.VMEM((ROWS, WIDTH), BF16), pltpu.VMEM((BOTH, WIDTH), BF16), pltpu.SemaphoreType.DMA((2,))]
        + head_scratch(HALF),
        (10**9, 8 * 10**6),
    )(flags, x, down, *frozen)


def prepare_third_kernel(order, spot, low_ref, *refs):
    frozen, outs, scratch = refs[:5], refs[5:7], refs[7:]
    y, own_half = spot[SPOT_Y], spot[SPOT_OWN_SHIFT] // PLANE
    heads, places = [], []
    for other in range(2):
        for dy in range(YS):
            seat = (own_half + other) % 2 * YS + (y + dy) % YS
            heads.append(order[2 * MEMBERS + seat])
            places.append((outs[other], (dy, 0)))
    copies = fetch_heads(heads, places, *frozen, *scratch)
    raise_heads(low_ref[...], copies, places, *scratch[:3])


def prepare_last_kernel(order, spot, low_ref, *refs):
    frozen, out_ref, scratch = refs[:5], refs[5], refs[6:]
    heads = [order[3 * MEMBERS + seat] for seat in range(MEMBERS)]
    places = [(out_ref, (seat, 0)) for seat in range(MEMBERS)]
    for seat in range(MEMBERS):
        out_ref[seat, :, pl.ds(4 * HD, BOTH)] = low_ref[...]
    copies = fetch_heads(heads, places, *frozen, *scratch)
    raise_heads(low_ref[...], copies, places, *scratch[:3])


def prepare_shifted(item, order, spot, low, frozen):
    shapes = [(YS, ROWS, 4 * HD)] * 2 if item == 2 else [(MEMBERS, ROWS, 4 * HD + BOTH)]
    return call(
        prepare_third_kernel if item == 2 else prepare_last_kernel,
        "prepare_third" if item == 2 else "prepare_last",
        2,
        [block((ROWS, BOTH))] + [ANYWHERE] * 5,
        [block(shape) for shape in shapes],
        [jax.ShapeDtypeStruct(shape, BF16) for shape in shapes],
        head_scratch(MEMBERS),
        (10**9, 8 * 10**6),
    )(order, spot, low, *frozen)


def pack_kernel(own_ref, other_ref, *out_refs):
    for dy, out_ref in enumerate(out_refs, 1):
        out_ref[:, pl.ds(0, 4 * HD)] = own_ref[dy]
        out_ref[:, pl.ds(4 * HD, 4 * HD)] = other_ref[dy]


def pack(own, other):
    shape = (ROWS, 8 * HD)
    return call(
        pack_kernel,
        "pack_third",
        0,
        [block(own.shape)] * 2,
        [block(shape)] * 3,
        (jax.ShapeDtypeStruct(shape, BF16),) * 3,
        [],
        (0, 4 * 10**6),
    )(own, other)


def turn_kernel(spot, x_ref, *out_refs):
    x, core = spot[0] // CS, spot[0] % CS
    *out_refs, stage = out_refs
    for u in range(HEADS):
        stage[pl.ds(u * HD, HD), :] = x_ref[:, pl.ds(u * HD, HD)].T
    for step, out_ref in enumerate(out_refs):
        for other in range(CS):
            d = (x + step) % XS * CS + (core + other) % CS
            for u in range(HEADS):
                rows = pl.ds(pl.multiple_of(u * HD + d * PIECE, PIECE), PIECE)
                out_ref[other, pl.ds(u * PIECE, PIECE), :] = stage[rows, :]


def turn(place, x):
    shape = (CS, HEADS * PIECE, ROWS)
    return call(
        turn_kernel,
        "turn_input",
        1,
        [block(x.shape)],
        [block(shape)] * XS,
        (jax.ShapeDtypeStruct(shape, BF16),) * XS,
        [pltpu.VMEM((WIDTH, ROWS), BF16)],
        (10**9, 2 * 10**6),
    )(place, x)


def attend(x_ref, up, grads_ref, column, dv_acc):
    factor = 1.0 / math.sqrt(HD)
    bend = factor * math.log2(math.e)
    row_ids = lax.broadcasted_iota(jnp.int32, (RB, RB), 0)
    column_ids = lax.broadcasted_iota(jnp.int32, (RB, RB), 1)
    keep = column_ids <= row_ids
    for i in range(GROUP // RB):
        n = (i + 1) * RB
        rows = pl.ds(i * RB, RB)
        q = x_ref[rows, pl.ds(0, HD)]
        g = x_ref[rows, pl.ds(3 * HD, HD)]
        k = x_ref[pl.ds(0, n), pl.ds(HD, HD)]
        v = x_ref[pl.ds(0, n), pl.ds(2 * HD, HD)]
        scores = dot_t(q, k)
        last = jnp.where(keep, scores[:, i * RB :], -1e30)
        scores = last if i == 0 else jnp.concatenate([scores[:, : i * RB], last], axis=1)
        top = jnp.max(scores, axis=1, keepdims=True)
        weights = jnp.exp2((scores - top) * bend)
        total = jnp.sum(weights, axis=1, keepdims=True)
        attention = (weights * (1.0 / total)).astype(BF16)
        grad_attention = dot_t(g, v)
        center = jnp.sum(attention.astype(F32) * grad_attention, axis=1, keepdims=True)
        grad_scores = (attention.astype(F32) * (grad_attention - center)).astype(BF16)
        dq = jnp.dot(grad_scores, k, preferred_element_type=F32) * factor
        grads_ref[rows, pl.ds(column, HD)] = dq.astype(BF16)
        dv = dot_0(g, attention)
        if i:
            dv_acc[:, pl.ds(0, i * RB)] += dv[:, : i * RB]
        dv_acc[:, rows] = dv[:, i * RB :]
    dq = grads_ref[:, pl.ds(column, HD)]
    dv = dv_acc[...].T.astype(BF16)
    grads_ref[:, pl.ds(column + HD, HD)] = dv
    lanes = lax.broadcasted_iota(jnp.int32, (GROUP, BOTH), 1)
    return jnp.where(lanes < RANK, dot_t(dq, up), dot_t(dv, up))


def attention_plain_kernel(order, spot, arrived, up_a, up_b, mine_ref, theirs_ref, grads_ref, xs, dv_acc, total, sems):
    copies = []
    for item in range(2):
        source = arrived.at[:, pl.ds(item * 4 * HD, 4 * HD)]
        copies.append(pltpu.make_async_copy(source, xs.at[item], sems.at[item]))
        copies[-1].start()
    copies[0].wait()
    total[...] = attend(xs.at[0], up_a[...], grads_ref, 0, dv_acc)
    copies[1].wait()
    total[...] += attend(xs.at[1], up_b[...], grads_ref, 2 * HD, dv_acc)
    own = pl.multiple_of(spot[SPOT_OWN_PLAIN], PLANE)
    mine_ref[...] = total[pl.ds(own, PLANE), :]
    theirs_ref[...] = total[pl.ds(PLANE - own, PLANE), :].astype(BF16)


def up_columns(item):
    seat = SPOT_PLAIN if item < 2 else SPOT_SHIFT
    return pl.BlockSpec((BOTH, HD), lambda i, order, spot: (0, order[item * MEMBERS + spot[seat]]))


def attention_plain(order, spot, arrived, up):
    shapes = [((PLANE, BOTH), F32), ((PLANE, BOTH), BF16), ((GROUP, 4 * HD), BF16)]
    return call(
        attention_plain_kernel,
        "attention_plain",
        2,
        [ANYWHERE, up_columns(0), up_columns(1)],
        [block(shape) for shape, _ in shapes],
        [jax.ShapeDtypeStruct(*shape) for shape in shapes],
        [
            pltpu.VMEM((2, GROUP, 4 * HD), BF16),
            pltpu.VMEM((HD, GROUP), F32),
            pltpu.VMEM((GROUP, BOTH), F32),
            pltpu.SemaphoreType.DMA((2,)),
        ],
        (2 * 10**10, 4 * 10**6),
    )(order, spot, arrived, up, up)


def attention_shifted_kernel(last, order, spot, *refs):
    y, own = spot[SPOT_Y], spot[SPOT_OWN_SHIFT]
    if last:
        own_ref, other_ref, *pieces = refs[:5]
        up, before_hbm, mine_hbm, theirs_hbm, back_ref, grads_hbm, x_in, dv_acc, sems = refs[5:14]
        total, before_ref, mine_ref, theirs_ref, grads_ref, more_sems = refs[14:]
        for dy in range(YS):
            for half in range(2):
                at = (own if half == 0 else PLANE - own) // ROWS + (y - dy + YS) % YS
                rows = pl.ds(pl.multiple_of(at * ROWS, ROWS), ROWS)
                if dy == 0:
                    source = (own_ref, other_ref)[half].at[0]
                else:
                    source = pieces[dy - 1].at[:, pl.ds(half * 4 * HD, 4 * HD)]
                pltpu.make_async_copy(source, x_in.at[rows, :], sems.at[2 * dy + half]).start()
    else:
        arrived, up, back_ref, grads_ref, x_in, dv_acc, sems = refs
        pltpu.make_async_copy(arrived.at[:, pl.ds(0, 4 * HD)], x_in, sems.at[0]).start()
    if last:
        pairs = ((before_hbm, before_ref), (mine_hbm, mine_ref), (theirs_hbm, theirs_ref))
        others = [pltpu.make_async_copy(*pair, more_sems.at[t]) for t, pair in enumerate(pairs)]
        for copy in others:
            copy.start()
    if last:
        for t in range(MEMBERS):
            pltpu.make_async_copy(own_ref.at[0], x_in.at[pl.ds(t * ROWS, ROWS), :], sems.at[t]).wait()
    else:
        pltpu.make_async_copy(arrived.at[:, pl.ds(0, 4 * HD)], x_in, sems.at[0]).wait()
    back = attend(x_in, up[...], grads_ref, 0, dv_acc)
    if not last:
        back_ref[...] = back
        return
    save = pltpu.make_async_copy(grads_ref, grads_hbm, more_sems.at[3])
    save.start()
    for copy in others:
        copy.wait()
    total[...] = back + before_ref[...]
    mine_rows = pl.ds(pl.multiple_of(own, PLANE), PLANE)
    total[mine_rows, :] += mine_ref[...] + theirs_ref[...].astype(F32)
    back_ref[...] = total[...].astype(BF16)
    save.wait()


LAST_SCRATCH = [
    pltpu.VMEM((GROUP, BOTH), F32),
    pltpu.VMEM((GROUP, BOTH), F32),
    pltpu.VMEM((PLANE, BOTH), F32),
    pltpu.VMEM((PLANE, BOTH), BF16),
    pltpu.VMEM((GROUP, 2 * HD), BF16),
    pltpu.SemaphoreType.DMA((4,)),
]


def attention_shifted(item, order, spot, arrived, up, *more):
    last = len(more) > 0
    shapes = [((GROUP, BOTH), BF16 if last else F32), ((GROUP, 2 * HD), BF16)]

    def body(*refs):
        attention_shifted_kernel(last, *refs)

    return call(
        body,
        "attention_last" if last else "attention_third",
        2,
        [pl.BlockSpec(memory_space=pl.ANY) if last else ANYWHERE] * len(arrived)
        + [up_columns(item)]
        + [ANYWHERE] * len(more),
        [block(shapes[0][0]), ANYWHERE] if last else [block(shape) for shape, _ in shapes],
        [jax.ShapeDtypeStruct(*shape) for shape in shapes],
        [pltpu.VMEM((GROUP, 4 * HD), BF16), pltpu.VMEM((HD, GROUP), F32), pltpu.SemaphoreType.DMA((2 * YS,))]
        + LAST_SCRATCH * last,
        (4 * 10**9, 3 * 10**6) if last else (10**6, 10**4),
    )(order, spot, *arrived, up, *more)


def up_gradient_kernel(low_a, low_b, *refs):
    out_ref = refs[-1]
    for item in range(4):
        low = (low_a, low_b)[item // 2][...]
        grads, column = ((refs[0], 0), (refs[0], 2 * HD), (refs[1], 0), (refs[2], 0))[item]
        for m in range(2):
            columns = pl.ds(column + m * HD, HD)
            part = adapter_scale * dot_0(low[:, m * RANK : (m + 1) * RANK], grads[:, columns])
            part = part.astype(BF16)
            for e in range(RANK // PIECE):
                d = m * (RANK // PIECE) + e
                out_ref[d, pl.ds(item * PIECE, PIECE), :] = part[e * PIECE : (e + 1) * PIECE]


def up_gradients(plain, late, grads):
    shape = (SLICES, 4 * PIECE, HD)
    lows = [pl.BlockSpec((GROUP, BOTH), lambda i, column=column: (0, column)) for column in (8, 4)]
    return call(
        up_gradient_kernel,
        "up_gradients",
        0,
        lows + [block(array.shape) for array in grads],
        block(shape),
        jax.ShapeDtypeStruct(shape, BF16),
        [],
        (2 * 10**9, 3 * 10**6),
    )(plain, late, *grads)


def gather_kernel(summed_ref, ups_ref, out_ref):
    back = jnp.sum(summed_ref[...].astype(F32), axis=0).astype(BF16)
    for d in range(SLICES):
        out_ref[d, pl.ds(0, ROWS), :] = back
    out_ref[:, pl.ds(ROWS, 4 * PIECE), :] = ups_ref[...]


def gather_parts(summed, ups):
    shape = (SLICES, ROWS + 4 * PIECE, HD)
    return call(
        gather_kernel,
        "gather_parts",
        0,
        [block(summed.shape), block(ups.shape)],
        block(shape),
        jax.ShapeDtypeStruct(shape, BF16),
        [],
        (10**7, 10**6),
        16,
    )(summed, ups)


def merge_kernel(order, spot, place, both_ref, *refs):
    x_refs, crossed_refs, out_ref = refs[:XS], refs[XS:-1], refs[-1]
    x, core = place[0] // CS, place[0] % CS
    total = jnp.zeros((HEADS * PIECE, BOTH), F32)
    for dx in range(XS):
        for other in range(CS):
            s = (x - dx + XS) % XS * CS + (core + other) % CS
            back = both_ref[s, pl.ds(0, ROWS), :]
            part = (x_refs, crossed_refs)[other][dx][0]
            total += jnp.dot(part, back, preferred_element_type=F32)
    total = (adapter_scale * total).astype(BF16)
    for u in range(HEADS):
        out_ref[u, pl.ds(0, PIECE), :] = total[u * PIECE : (u + 1) * PIECE]
        out_ref[u, pl.ds(PIECE, PIECE), :] = jnp.zeros((PIECE, HD), BF16)
    ups = jnp.sum(both_ref[:, pl.ds(ROWS, 4 * PIECE), :].astype(F32), axis=0).astype(BF16)
    for item in range(4):
        seat = spot[SPOT_PLAIN if item < 2 else SPOT_SHIFT]
        head = order[item * MEMBERS + seat]
        out_ref[head, pl.ds(PIECE, PIECE), :] = ups[item * PIECE : (item + 1) * PIECE]


def merge(order, spot, place, both, pieces, crossed):
    shape = (HEADS, 2 * PIECE, HD)
    return call(
        merge_kernel,
        "merge_gradients",
        3,
        [block(both.shape)]
        + [
            pl.BlockSpec((1, *piece.shape[1:]), lambda i, *s, half=half: (half, 0, 0))
            for half in range(2)
            for piece in (pieces, crossed)[half]
        ],
        block(shape),
        jax.ShapeDtypeStruct(shape, BF16),
        [],
        (2 * 10**8, 2 * 10**6),
        16,
    )(order, spot, place, both, *pieces, *crossed)


def spread_kernel(in_ref, out_ref):
    total = jnp.sum(in_ref[...].astype(F32), axis=0)
    for d in range(SLICES):
        out_ref[d] = total


def spread(both):
    shape = (SLICES, 2 * PIECE, HD)
    return call(
        spread_kernel,
        "spread_sums",
        0,
        [block(both.shape)],
        block(shape),
        jax.ShapeDtypeStruct(shape, F32),
        [],
        (10**6, 10**6),
        16,
    )(both)


def finish_kernel(in_ref, down_ref, up_ref):
    down = in_ref[:, pl.ds(0, PIECE), :].reshape(HD, BOTH).T
    up = in_ref[:, pl.ds(PIECE, PIECE), :].reshape(BOTH, HD)
    for m in range(2):
        down_ref[m] = down[m * RANK : (m + 1) * RANK]
        up_ref[m] = up[m * RANK : (m + 1) * RANK]


def finish(both):
    shape = (2, RANK, HD)
    return call(
        finish_kernel,
        "finish",
        0,
        [block(both.shape)],
        [block(shape)] * 2,
        [jax.ShapeDtypeStruct(shape, F32)] * 2,
        [],
        (10**6, 10**6),
        16,
    )(both)


def per_device(
    normalized_input,
    frozen_queries,
    frozen_keys,
    frozen_values,
    output_gradient,
    adapter_down_maps,
    adapter_up_maps,
    shifted,
):
    tokens = normalized_input[0]
    place = lax.axis_index("dp").reshape(1)
    up = adapter_up_maps.reshape(BOTH, WIDTH)
    down = adapter_down_maps.transpose(0, 2, 1).reshape(BOTH, WIDTH)

    frozen = (frozen_queries[0], frozen_keys[0], frozen_values[0], output_gradient[0], up)
    sent, order, spot, low = prepare_plain(shifted.astype(jnp.int32), tokens, down, frozen)
    plain = exchange(sent, "ulysses", PLAIN_GROUPS).reshape(GROUP, 8 * HD + BOTH)
    own_c, other_c = prepare_shifted(2, order, spot, low, frozen)
    other_c = lax.ppermute(other_c, "ulysses", SHIFT_SWAP)
    turned = turn(place, after(tokens, own_c))
    pieces = [turned[0]] + [lax.ppermute(turned[dx], "dp", x_shift(dx)) for dx in (1, 2, 3)]
    (sent,) = prepare_shifted(3, order, spot, after(low, turned), frozen)

    packed = pack(after(own_c, pieces, sent), other_c)
    plain, pieces, sent, packed = after((plain, pieces, sent, packed))
    arrived_d = exchange(sent, "ulysses", SHIFT_GROUPS).reshape(GROUP, 4 * HD + BOTH)
    arrived_c = [lax.ppermute(packed[dy - 1], "ulysses", y_shift(dy)) for dy in (1, 2, 3)]
    mine, theirs, grads_plain = attention_plain(order, spot, plain, up)
    theirs = lax.ppermute(theirs, "ulysses", PLAIN_SWAP)
    arrived_d = after(arrived_d, grads_plain)
    partial, grads_d = attention_shifted(3, order, spot, [arrived_d], up)

    arrived_c, theirs = after((arrived_c, theirs), partial)
    partial, grads_c = attention_shifted(2, order, spot, [own_c, other_c, *arrived_c], up, partial, mine, theirs)
    crossed = [lax.ppermute(piece, "dp", CORE_SWAP) for piece in after(pieces, partial)]
    summed = exchange(partial.reshape(MEMBERS, ROWS, BOTH), "ulysses", SHIFT_GROUPS)
    ups = up_gradients(plain, arrived_d, (grads_plain, grads_c, grads_d))

    both = exchange(gather_parts(summed, ups), "dp")
    both = exchange(merge(order, spot, place, both, pieces, crossed), "ulysses")
    both = exchange(spread(both), "dp")
    grad_down, grad_up = finish(both)
    return (grad_down.transpose(0, 2, 1), grad_up)


def solution(mesh):
    rows = P("dp", "ulysses", None)
    in_specs = (rows, rows, rows, rows, rows, P(), P(), P())
    out_specs = (P(None, "ulysses", None), P(None, None, "ulysses"))
    return jax.shard_map(
        per_device, mesh=mesh, in_specs=in_specs, out_specs=out_specs, check_vma=False
    )
```

```python
import math

import jax
import jax.numpy as jnp
from jax import lax
from jax.experimental import pallas as pl
from jax.experimental.pallas import tpu as pltpu
from jax.sharding import PartitionSpec as P

HEADS = 32
HD = 128
WIDTH = HEADS * HD
GROUP = 1024
PLANE = 512
RANK = 64
BOTH = 2 * RANK
ROWS = 128
ZS, YS = 8, 4
XS, CS = 4, 2
SLICES = XS * CS
MEMBERS = 8
PIECE = 16
RB = 256
BF16, F32 = jnp.bfloat16, jnp.float32

adapter_scale = 0.5

PLAIN_GROUPS = [[MEMBERS * g + i for i in range(MEMBERS)] for g in range(4)]
SHIFT_GROUPS = [[(MEMBERS * g + 4 + i) % HEADS for i in range(MEMBERS)] for g in range(4)]
PLAIN_SWAP = [(u, u ^ 4) for u in range(HEADS)]
SHIFT_SWAP = [(u, (((u + 4) % HEADS ^ 4) - 4) % HEADS) for u in range(HEADS)]
CORE_SWAP = [(d, d ^ 1) for d in range(SLICES)]
ANYWHERE = pl.BlockSpec(memory_space=pltpu.HBM)
SCALARS = pl.BlockSpec(memory_space=pltpu.SMEM)

SPOT_Y, SPOT_PLAIN, SPOT_SHIFT, SPOT_OWN_PLAIN, SPOT_OWN_SHIFT = range(5)


def y_shift(dy):
    return [(z * YS + y, z * YS + (y + dy) % YS) for z in range(ZS) for y in range(YS)]


def x_shift(dx):
    return [(x * CS + c, ((x + dx) % XS) * CS + c) for x in range(XS) for c in range(CS)]


def exchange(member, axis, groups=None):
    return lax.all_to_all(member, axis, 0, 0, tiled=True, axis_index_groups=groups)


def after(values, *others):
    return lax.optimization_barrier((values, others))[0]


def block(shape):
    return pl.BlockSpec(shape, lambda i, *s: (0,) * len(shape))


def dot_t(a, b):
    return lax.dot_general(a, b, (((1,), (1,)), ((), ())), preferred_element_type=F32)


def dot_0(a, b):
    return lax.dot_general(a, b, (((0,), (0,)), ((), ())), preferred_element_type=F32)


def call(kernel, name, scalars, in_specs, out_specs, out_shape, scratch, cost, vmem=None):
    params = pltpu.CompilerParams(vmem_limit_bytes=vmem and vmem * 2**20)
    return pl.pallas_call(
        kernel,
        name=name,
        out_shape=out_shape,
        grid_spec=pltpu.PrefetchScalarGridSpec(
            num_scalar_prefetch=scalars,
            grid=(1,),
            in_specs=in_specs,
            out_specs=out_specs,
            scratch_shapes=scratch,
        ),
        compiler_params=params,
        cost_estimate=pl.CostEstimate(flops=cost[0], bytes_accessed=cost[1], transcendentals=0),
    )


def order_heads(flags, order):
    def place(h, ones):
        flag = flags[h]
        order[jnp.where(flag > 0, HEADS // 2 + ones, h - ones)] = h
        return ones + jnp.where(flag > 0, 1, 0)

    lax.fori_loop(0, HEADS, place, 0, unroll=True)


def fetch_heads(heads, places, fq_ref, fk_ref, fv_ref, go_ref, up_ref, q_in, v_in, up_in, sems):
    copies = []
    for p, (head, (buffer, entry)) in enumerate(zip(heads, places)):
        cols = pl.ds(pl.multiple_of(head * HD, HD), HD)
        own = pl.ds(p * HD, HD)
        spots = (
            (up_ref, up_in.at[:, own]),
            (fq_ref, q_in.at[:, own]),
            (fv_ref, v_in.at[:, own]),
            (fk_ref, buffer.at[(*entry[:-1], slice(None), pl.ds(entry[-1] + HD, HD))]),
            (go_ref, buffer.at[(*entry[:-1], slice(None), pl.ds(entry[-1] + 3 * HD, HD))]),
        )
        for t, (ref, spot) in enumerate(spots):
            copies.append(pltpu.make_async_copy(ref.at[:, cols], spot, sems.at[p, t]))
            copies[-1].start()
    return copies


def raise_heads(low, copies, places, q_in, v_in, up_in):
    lanes = lax.broadcasted_iota(jnp.int32, (ROWS, BOTH), 1)
    none = jnp.zeros_like(low)
    lows = jnp.concatenate([jnp.where(lanes < RANK, low, none), jnp.where(lanes < RANK, none, low)], axis=0)
    for copy in copies:
        copy.wait()
    raised = jnp.dot(lows, up_in[...], preferred_element_type=F32)
    for p, (buffer, entry) in enumerate(places):
        own = slice(p * HD, (p + 1) * HD)
        q = (q_in[:, own].astype(F32) + adapter_scale * raised[:ROWS, own]).astype(BF16)
        v = (v_in[:, own].astype(F32) + adapter_scale * raised[ROWS:, own]).astype(BF16)
        buffer[(*entry[:-1], slice(None), pl.ds(entry[-1], HD))] = q
        buffer[(*entry[:-1], slice(None), pl.ds(entry[-1] + 2 * HD, HD))] = v


HALF = HEADS // 2


def head_scratch(count):
    return [
        pltpu.VMEM((ROWS, count * HD), BF16),
        pltpu.VMEM((ROWS, count * HD), BF16),
        pltpu.VMEM((BOTH, count * HD), BF16),
        pltpu.SemaphoreType.DMA((count, 5)),
    ]


def prepare_plain_kernel(flags, x_hbm, down_hbm, *refs):
    frozen, (out_ref, order, spot, low_ref, x_in, down_in, whole_sems, q_in, v_in, up_in, sems) = refs[:5], refs[5:]
    wholes = [
        pltpu.make_async_copy(x_hbm, x_in, whole_sems.at[0]),
        pltpu.make_async_copy(down_hbm, down_in, whole_sems.at[1]),
    ]
    for copy in wholes:
        copy.start()
    order_heads(flags, order)
    me = lax.axis_index("ulysses")
    spot[SPOT_Y] = me % YS
    spot[SPOT_PLAIN] = me % MEMBERS
    spot[SPOT_SHIFT] = (me + YS) % MEMBERS
    spot[SPOT_OWN_PLAIN] = me // YS % 2 * PLANE
    spot[SPOT_OWN_SHIFT] = (1 - me // YS % 2) * PLANE
    places = [(out_ref, (p % MEMBERS, p // MEMBERS * 4 * HD)) for p in range(HALF)]
    copies = fetch_heads([order[p] for p in range(HALF)], places, *frozen, q_in, v_in, up_in, sems)
    for copy in wholes:
        copy.wait()
    low = dot_t(x_in[...], down_in[...]).astype(BF16)
    low_ref[...] = low
    for seat in range(MEMBERS):
        out_ref[seat, :, pl.ds(8 * HD, BOTH)] = low
    raise_heads(low, copies, places, q_in, v_in, up_in)


def prepare_plain(flags, x, down, frozen):
    return call(
        prepare_plain_kernel,
        "prepare_plain",
        1,
        [ANYWHERE] * 7,
        [block((MEMBERS, ROWS, 8 * HD + BOTH)), SCALARS, SCALARS, block((ROWS, BOTH))],
        (
            jax.ShapeDtypeStruct((MEMBERS, ROWS, 8 * HD + BOTH), BF16),
            jax.ShapeDtypeStruct((HEADS,), jnp.int32),
            jax.ShapeDtypeStruct((MEMBERS,), jnp.int32),
            jax.ShapeDtypeStruct((ROWS, BOTH), BF16),
        ),
        [pltpu.VMEM((ROWS, WIDTH), BF16), pltpu.VMEM((BOTH, WIDTH), BF16), pltpu.SemaphoreType.DMA((2,))]
        + head_scratch(HALF),
        (10**9, 8 * 10**6),
    )(flags, x, down, *frozen)


def prepare_third_kernel(order, spot, low_ref, *refs):
    frozen, outs, scratch = refs[:5], refs[5:7], refs[7:]
    y, own_half = spot[SPOT_Y], spot[SPOT_OWN_SHIFT] // PLANE
    heads, places = [], []
    for other in range(2):
        for dy in range(YS):
            seat = (own_half + other) % 2 * YS + (y + dy) % YS
            heads.append(order[2 * MEMBERS + seat])
            places.append((outs[other], (dy, 0)))
    copies = fetch_heads(heads, places, *frozen, *scratch)
    raise_heads(low_ref[...], copies, places, *scratch[:3])


def prepare_last_kernel(order, spot, low_ref, *refs):
    frozen, out_ref, scratch = refs[:5], refs[5], refs[6:]
    heads = [order[3 * MEMBERS + seat] for seat in range(MEMBERS)]
    places = [(out_ref, (seat, 0)) for seat in range(MEMBERS)]
    for seat in range(MEMBERS):
        out_ref[seat, :, pl.ds(4 * HD, BOTH)] = low_ref[...]
    copies = fetch_heads(heads, places, *frozen, *scratch)
    raise_heads(low_ref[...], copies, places, *scratch[:3])


def prepare_shifted(item, order, spot, low, frozen):
    shapes = [(YS, ROWS, 4 * HD)] * 2 if item == 2 else [(MEMBERS, ROWS, 4 * HD + BOTH)]
    return call(
        prepare_third_kernel if item == 2 else prepare_last_kernel,
        "prepare_third" if item == 2 else "prepare_last",
        2,
        [block((ROWS, BOTH))] + [ANYWHERE] * 5,
        [block(shape) for shape in shapes],
        [jax.ShapeDtypeStruct(shape, BF16) for shape in shapes],
        head_scratch(MEMBERS),
        (10**9, 8 * 10**6),
    )(order, spot, low, *frozen)


def pack_kernel(own_ref, other_ref, *out_refs):
    for dy, out_ref in enumerate(out_refs, 1):
        out_ref[:, pl.ds(0, 4 * HD)] = own_ref[dy]
        out_ref[:, pl.ds(4 * HD, 4 * HD)] = other_ref[dy]


def pack(own, other):
    shape = (ROWS, 8 * HD)
    return call(
        pack_kernel,
        "pack_third",
        0,
        [block(own.shape)] * 2,
        [block(shape)] * 3,
        (jax.ShapeDtypeStruct(shape, BF16),) * 3,
        [],
        (0, 4 * 10**6),
    )(own, other)


def turn_kernel(spot, x_ref, *out_refs):
    x, core = spot[0] // CS, spot[0] % CS
    *out_refs, stage = out_refs
    for u in range(HEADS):
        stage[pl.ds(u * HD, HD), :] = x_ref[:, pl.ds(u * HD, HD)].T
    for step, out_ref in enumerate(out_refs):
        for other in range(CS):
            d = (x + step) % XS * CS + (core + other) % CS
            for u in range(HEADS):
                rows = pl.ds(pl.multiple_of(u * HD + d * PIECE, PIECE), PIECE)
                out_ref[other, pl.ds(u * PIECE, PIECE), :] = stage[rows, :]


def turn(place, x):
    shape = (CS, HEADS * PIECE, ROWS)
    return call(
        turn_kernel,
        "turn_input",
        1,
        [block(x.shape)],
        [block(shape)] * XS,
        (jax.ShapeDtypeStruct(shape, BF16),) * XS,
        [pltpu.VMEM((WIDTH, ROWS), BF16)],
        (10**9, 2 * 10**6),
    )(place, x)


def attend(x_ref, up, grads_ref, column, dv_acc):
    factor = 1.0 / math.sqrt(HD)
    bend = factor * math.log2(math.e)
    row_ids = lax.broadcasted_iota(jnp.int32, (RB, RB), 0)
    column_ids = lax.broadcasted_iota(jnp.int32, (RB, RB), 1)
    keep = column_ids <= row_ids
    for i in range(GROUP // RB):
        n = (i + 1) * RB
        rows = pl.ds(i * RB, RB)
        q = x_ref[rows, pl.ds(0, HD)]
        g = x_ref[rows, pl.ds(3 * HD, HD)]
        k = x_ref[pl.ds(0, n), pl.ds(HD, HD)]
        v = x_ref[pl.ds(0, n), pl.ds(2 * HD, HD)]
        scores = dot_t(q, k)
        last = jnp.where(keep, scores[:, i * RB :], -1e30)
        scores = last if i == 0 else jnp.concatenate([scores[:, : i * RB], last], axis=1)
        top = jnp.max(scores, axis=1, keepdims=True)
        weights = jnp.exp2((scores - top) * bend)
        total = jnp.sum(weights, axis=1, keepdims=True)
        attention = (weights * (1.0 / total)).astype(BF16)
        grad_attention = dot_t(g, v)
        center = jnp.sum(attention.astype(F32) * grad_attention, axis=1, keepdims=True)
        grad_scores = (attention.astype(F32) * (grad_attention - center)).astype(BF16)
        dq = jnp.dot(grad_scores, k, preferred_element_type=F32) * factor
        grads_ref[rows, pl.ds(column, HD)] = dq.astype(BF16)
        dv = dot_0(g, attention)
        if i:
            dv_acc[:, pl.ds(0, i * RB)] += dv[:, : i * RB]
        dv_acc[:, rows] = dv[:, i * RB :]
    dq = grads_ref[:, pl.ds(column, HD)]
    dv = dv_acc[...].T.astype(BF16)
    grads_ref[:, pl.ds(column + HD, HD)] = dv
    lanes = lax.broadcasted_iota(jnp.int32, (GROUP, BOTH), 1)
    return jnp.where(lanes < RANK, dot_t(dq, up), dot_t(dv, up))


def attention_plain_kernel(order, spot, arrived, up_a, up_b, mine_ref, theirs_ref, grads_ref, xs, dv_acc, total, sems):
    copies = []
    for item in range(2):
        source = arrived.at[:, pl.ds(item * 4 * HD, 4 * HD)]
        copies.append(pltpu.make_async_copy(source, xs.at[item], sems.at[item]))
        copies[-1].start()
    copies[0].wait()
    total[...] = attend(xs.at[0], up_a[...], grads_ref, 0, dv_acc)
    copies[1].wait()
    total[...] += attend(xs.at[1], up_b[...], grads_ref, 2 * HD, dv_acc)
    own = pl.multiple_of(spot[SPOT_OWN_PLAIN], PLANE)
    mine_ref[...] = total[pl.ds(own, PLANE), :]
    theirs_ref[...] = total[pl.ds(PLANE - own, PLANE), :].astype(BF16)


def up_columns(item):
    seat = SPOT_PLAIN if item < 2 else SPOT_SHIFT
    return pl.BlockSpec((BOTH, HD), lambda i, order, spot: (0, order[item * MEMBERS + spot[seat]]))


def attention_plain(order, spot, arrived, up):
    shapes = [((PLANE, BOTH), F32), ((PLANE, BOTH), BF16), ((GROUP, 4 * HD), BF16)]
    return call(
        attention_plain_kernel,
        "attention_plain",
        2,
        [ANYWHERE, up_columns(0), up_columns(1)],
        [block(shape) for shape, _ in shapes],
        [jax.ShapeDtypeStruct(*shape) for shape in shapes],
        [
            pltpu.VMEM((2, GROUP, 4 * HD), BF16),
            pltpu.VMEM((HD, GROUP), F32),
            pltpu.VMEM((GROUP, BOTH), F32),
            pltpu.SemaphoreType.DMA((2,)),
        ],
        (2 * 10**10, 4 * 10**6),
    )(order, spot, arrived, up, up)


def attention_shifted_kernel(last, order, spot, *refs):
    y, own = spot[SPOT_Y], spot[SPOT_OWN_SHIFT]
    if last:
        arrived, up, before_hbm, mine_hbm, theirs_hbm, back_ref, grads_hbm, x_in, dv_acc, sems = refs[:10]
        total, before_ref, mine_ref, theirs_ref, grads_ref, more_sems = refs[10:]
        pltpu.make_async_copy(arrived.at[:, pl.ds(0, 4 * HD)], x_in, sems.at[0]).start()
    else:
        own_ref, other_ref, *pieces = refs[:5]
        up, back_ref, grads_ref, x_in, dv_acc, sems = refs[5:]
        for dy in range(YS):
            for half in range(2):
                at = (own if half == 0 else PLANE - own) // ROWS + (y - dy + YS) % YS
                rows = pl.ds(pl.multiple_of(at * ROWS, ROWS), ROWS)
                if dy == 0:
                    source = (own_ref, other_ref)[half].at[0]
                else:
                    source = pieces[dy - 1].at[:, pl.ds(half * 4 * HD, 4 * HD)]
                pltpu.make_async_copy(source, x_in.at[rows, :], sems.at[2 * dy + half]).start()
    if last:
        pairs = ((before_hbm, before_ref), (mine_hbm, mine_ref), (theirs_hbm, theirs_ref))
        others = [pltpu.make_async_copy(*pair, more_sems.at[t]) for t, pair in enumerate(pairs)]
        for copy in others:
            copy.start()
    if last:
        pltpu.make_async_copy(arrived.at[:, pl.ds(0, 4 * HD)], x_in, sems.at[0]).wait()
    else:
        for t in range(MEMBERS):
            pltpu.make_async_copy(own_ref.at[0], x_in.at[pl.ds(t * ROWS, ROWS), :], sems.at[t]).wait()
    back = attend(x_in, up[...], grads_ref, 0, dv_acc)
    if not last:
        back_ref[...] = back
        return
    save = pltpu.make_async_copy(grads_ref, grads_hbm, more_sems.at[3])
    save.start()
    for copy in others:
        copy.wait()
    total[...] = back + before_ref[...]
    mine_rows = pl.ds(pl.multiple_of(own, PLANE), PLANE)
    total[mine_rows, :] += mine_ref[...] + theirs_ref[...].astype(F32)
    back_ref[...] = total[...].astype(BF16)
    save.wait()


LAST_SCRATCH = [
    pltpu.VMEM((GROUP, BOTH), F32),
    pltpu.VMEM((GROUP, BOTH), F32),
    pltpu.VMEM((PLANE, BOTH), F32),
    pltpu.VMEM((PLANE, BOTH), BF16),
    pltpu.VMEM((GROUP, 2 * HD), BF16),
    pltpu.SemaphoreType.DMA((4,)),
]


def attention_shifted(item, order, spot, arrived, up, *more):
    last = len(more) > 0
    shapes = [((GROUP, BOTH), BF16 if last else F32), ((GROUP, 2 * HD), BF16)]

    def body(*refs):
        attention_shifted_kernel(last, *refs)

    return call(
        body,
        "attention_last" if last else "attention_third",
        2,
        [pl.BlockSpec(memory_space=pl.ANY) if last else ANYWHERE] * len(arrived)
        + [up_columns(item)]
        + [ANYWHERE] * len(more),
        [block(shapes[0][0]), ANYWHERE] if last else [block(shape) for shape, _ in shapes],
        [jax.ShapeDtypeStruct(*shape) for shape in shapes],
        [pltpu.VMEM((GROUP, 4 * HD), BF16), pltpu.VMEM((HD, GROUP), F32), pltpu.SemaphoreType.DMA((2 * YS,))]
        + LAST_SCRATCH * last,
        (4 * 10**9, 3 * 10**6) if last else (10**10, 10**4),
    )(order, spot, *arrived, up, *more)


def up_gradient_kernel(low_a, low_b, *refs):
    out_ref = refs[-1]
    for item in range(4):
        low = (low_a, low_b)[item // 2][...]
        grads, column = ((refs[0], 0), (refs[0], 2 * HD), (refs[1], 0), (refs[2], 0))[item]
        for m in range(2):
            columns = pl.ds(column + m * HD, HD)
            part = adapter_scale * dot_0(low[:, m * RANK : (m + 1) * RANK], grads[:, columns])
            part = part.astype(BF16)
            for e in range(RANK // PIECE):
                d = m * (RANK // PIECE) + e
                out_ref[d, pl.ds(item * PIECE, PIECE), :] = part[e * PIECE : (e + 1) * PIECE]


def up_gradients(plain, late, grads):
    shape = (SLICES, 4 * PIECE, HD)
    lows = [pl.BlockSpec((GROUP, BOTH), lambda i, column=column: (0, column)) for column in (8, 4)]
    return call(
        up_gradient_kernel,
        "up_gradients",
        0,
        lows + [block(array.shape) for array in grads],
        block(shape),
        jax.ShapeDtypeStruct(shape, BF16),
        [],
        (2 * 10**9, 3 * 10**6),
    )(plain, late, *grads)


def gather_kernel(summed_ref, ups_ref, out_ref):
    back = jnp.sum(summed_ref[...].astype(F32), axis=0).astype(BF16)
    for d in range(SLICES):
        out_ref[d, pl.ds(0, ROWS), :] = back
    out_ref[:, pl.ds(ROWS, 4 * PIECE), :] = ups_ref[...]


def gather_parts(summed, ups):
    shape = (SLICES, ROWS + 4 * PIECE, HD)
    return call(
        gather_kernel,
        "gather_parts",
        0,
        [block(summed.shape), block(ups.shape)],
        block(shape),
        jax.ShapeDtypeStruct(shape, BF16),
        [],
        (10**7, 10**6),
        16,
    )(summed, ups)


def merge_kernel(order, spot, place, both_ref, *refs):
    x_refs, crossed_ref, out_ref = refs[:-2], refs[-2], refs[-1]
    x, core = place[0] // CS, place[0] % CS
    total = jnp.zeros((HEADS * PIECE, BOTH), F32)
    for dx in range(XS):
        for other in range(CS):
            s = (x - dx + XS) % XS * CS + (core + other) % CS
            back = both_ref[s, pl.ds(0, ROWS), :]
            part = x_refs[dx][0] if other == 0 else crossed_ref[dx]
            total += jnp.dot(part, back, preferred_element_type=F32)
    total = (adapter_scale * total).astype(BF16)
    for u in range(HEADS):
        out_ref[u, pl.ds(0, PIECE), :] = total[u * PIECE : (u + 1) * PIECE]
        out_ref[u, pl.ds(PIECE, PIECE), :] = jnp.zeros((PIECE, HD), BF16)
    ups = jnp.sum(both_ref[:, pl.ds(ROWS, 4 * PIECE), :].astype(F32), axis=0).astype(BF16)
    for item in range(4):
        seat = spot[SPOT_PLAIN if item < 2 else SPOT_SHIFT]
        head = order[item * MEMBERS + seat]
        out_ref[head, pl.ds(PIECE, PIECE), :] = ups[item * PIECE : (item + 1) * PIECE]


def merge(order, spot, place, both, pieces, crossed):
    shape = (HEADS, 2 * PIECE, HD)
    return call(
        merge_kernel,
        "merge_gradients",
        3,
        [block(both.shape)] + [block((1, *piece.shape[1:])) for piece in pieces] + [block(crossed.shape)],
        block(shape),
        jax.ShapeDtypeStruct(shape, BF16),
        [],
        (2 * 10**8, 2 * 10**6),
        16,
    )(order, spot, place, both, *pieces, crossed)


def spread_kernel(in_ref, out_ref):
    total = jnp.sum(in_ref[...].astype(F32), axis=0)
    for d in range(SLICES):
        out_ref[d] = total


def spread(both):
    shape = (SLICES, 2 * PIECE, HD)
    return call(
        spread_kernel,
        "spread_sums",
        0,
        [block(both.shape)],
        block(shape),
        jax.ShapeDtypeStruct(shape, F32),
        [],
        (10**6, 10**6),
        16,
    )(both)


def finish_kernel(in_ref, down_ref, up_ref):
    down = in_ref[:, pl.ds(0, PIECE), :].reshape(HD, BOTH).T
    up = in_ref[:, pl.ds(PIECE, PIECE), :].reshape(BOTH, HD)
    for m in range(2):
        down_ref[m] = down[m * RANK : (m + 1) * RANK]
        up_ref[m] = up[m * RANK : (m + 1) * RANK]


def finish(both):
    shape = (2, RANK, HD)
    return call(
        finish_kernel,
        "finish",
        0,
        [block(both.shape)],
        [block(shape)] * 2,
        [jax.ShapeDtypeStruct(shape, F32)] * 2,
        [],
        (10**6, 10**6),
        16,
    )(both)


def per_device(
    normalized_input,
    frozen_queries,
    frozen_keys,
    frozen_values,
    output_gradient,
    adapter_down_maps,
    adapter_up_maps,
    shifted,
):
    tokens = normalized_input[0]
    place = lax.axis_index("dp").reshape(1)
    up = adapter_up_maps.reshape(BOTH, WIDTH)
    down = adapter_down_maps.transpose(0, 2, 1).reshape(BOTH, WIDTH)

    frozen = (frozen_queries[0], frozen_keys[0], frozen_values[0], output_gradient[0], up)
    sent, order, spot, low = prepare_plain(shifted.astype(jnp.int32), tokens, down, frozen)
    plain = exchange(sent, "ulysses", PLAIN_GROUPS).reshape(GROUP, 8 * HD + BOTH)
    own_c, other_c = prepare_shifted(2, order, spot, low, frozen)
    other_c = lax.ppermute(other_c, "ulysses", SHIFT_SWAP)
    turned = turn(place, after(tokens, own_c))
    pieces = [turned[0]] + [lax.ppermute(turned[dx], "dp", x_shift(dx)) for dx in (1, 2, 3)]
    (sent,) = prepare_shifted(3, order, spot, after(low, turned), frozen)

    packed = pack(after(own_c, pieces[0], sent), other_c)
    arrived_c = [lax.ppermute(packed[dy - 1], "ulysses", y_shift(dy)) for dy in (1, 2, 3)]
    plain, pieces, sent = after((plain, pieces, sent), packed)

    arrived_d = exchange(sent, "ulysses", SHIFT_GROUPS).reshape(GROUP, 4 * HD + BOTH)
    crossed = lax.ppermute(jnp.stack([piece[1] for piece in pieces]), "dp", CORE_SWAP)
    mine, theirs, grads_plain = attention_plain(order, spot, plain, up)
    theirs = lax.ppermute(theirs, "ulysses", PLAIN_SWAP)
    arrived_c = after(arrived_c, grads_plain, sent)
    partial, grads_c = attention_shifted(2, order, spot, [own_c, other_c, *arrived_c], up)

    arrived_d, theirs, crossed = after((arrived_d, theirs, crossed), partial)
    partial, grads_d = attention_shifted(3, order, spot, [arrived_d], up, partial, mine, theirs)
    summed = exchange(partial.reshape(MEMBERS, ROWS, BOTH), "ulysses", SHIFT_GROUPS)
    ups = up_gradients(plain, arrived_d, (grads_plain, grads_c, grads_d))

    both = exchange(gather_parts(summed, ups), "dp")
    both = exchange(merge(order, spot, place, both, pieces, crossed), "ulysses")
    both = exchange(spread(both), "dp")
    grad_down, grad_up = finish(both)
    return (grad_down.transpose(0, 2, 1), grad_up)


def solution(mesh):
    rows = P("dp", "ulysses", None)
    in_specs = (rows, rows, rows, rows, rows, P(), P(), P())
    out_specs = (P(None, "ulysses", None), P(None, None, "ulysses"))
    return jax.shard_map(
        per_device, mesh=mesh, in_specs=in_specs, out_specs=out_specs, check_vma=False
    )
```

```python
import math

import jax
import jax.numpy as jnp
from jax import lax
from jax.experimental import pallas as pl
from jax.experimental.pallas import tpu as pltpu
from jax.sharding import PartitionSpec as P

HEADS = 32
HD = 128
WIDTH = HEADS * HD
GROUP = 1024
PLANE = 512
RANK = 64
BOTH = 2 * RANK
ROWS = 128
ZS, YS = 8, 4
XS, CS = 4, 2
SLICES = XS * CS
MEMBERS = 8
PIECE = 16
RB = 256
BF16, F32 = jnp.bfloat16, jnp.float32

adapter_scale = 0.5

PLAIN_GROUPS = [[MEMBERS * g + i for i in range(MEMBERS)] for g in range(4)]
SHIFT_GROUPS = [[(MEMBERS * g + 4 + i) % HEADS for i in range(MEMBERS)] for g in range(4)]
PLAIN_SWAP = [(u, u ^ 4) for u in range(HEADS)]
SHIFT_SWAP = [(u, (((u + 4) % HEADS ^ 4) - 4) % HEADS) for u in range(HEADS)]
CORE_SWAP = [(d, d ^ 1) for d in range(SLICES)]
ANYWHERE = pl.BlockSpec(memory_space=pltpu.HBM)
SCALARS = pl.BlockSpec(memory_space=pltpu.SMEM)

SPOT_Y, SPOT_PLAIN, SPOT_SHIFT, SPOT_OWN_PLAIN, SPOT_OWN_SHIFT = range(5)


def y_shift(dy):
    return [(z * YS + y, z * YS + (y + dy) % YS) for z in range(ZS) for y in range(YS)]


def x_shift(dx):
    return [(x * CS + c, ((x + dx) % XS) * CS + c) for x in range(XS) for c in range(CS)]


def exchange(member, axis, groups=None):
    return lax.all_to_all(member, axis, 0, 0, tiled=True, axis_index_groups=groups)


def after(values, *others):
    return lax.optimization_barrier((values, others))[0]


def block(shape):
    return pl.BlockSpec(shape, lambda i, *s: (0,) * len(shape))


def dot_t(a, b):
    return lax.dot_general(a, b, (((1,), (1,)), ((), ())), preferred_element_type=F32)


def dot_0(a, b):
    return lax.dot_general(a, b, (((0,), (0,)), ((), ())), preferred_element_type=F32)


def call(kernel, name, scalars, in_specs, out_specs, out_shape, scratch, cost, vmem=None):
    params = pltpu.CompilerParams(vmem_limit_bytes=vmem and vmem * 2**20)
    return pl.pallas_call(
        kernel,
        name=name,
        out_shape=out_shape,
        grid_spec=pltpu.PrefetchScalarGridSpec(
            num_scalar_prefetch=scalars,
            grid=(1,),
            in_specs=in_specs,
            out_specs=out_specs,
            scratch_shapes=scratch,
        ),
        compiler_params=params,
        cost_estimate=pl.CostEstimate(flops=cost[0], bytes_accessed=cost[1], transcendentals=0),
    )


def order_heads(flags, order):
    def place(h, ones):
        flag = flags[h]
        order[jnp.where(flag > 0, HEADS // 2 + ones, h - ones)] = h
        return ones + jnp.where(flag > 0, 1, 0)

    lax.fori_loop(0, HEADS, place, 0, unroll=True)


def fetch_heads(heads, places, fq_ref, fk_ref, fv_ref, go_ref, up_ref, q_in, v_in, up_in, sems):
    copies = []
    for p, (head, (buffer, entry)) in enumerate(zip(heads, places)):
        cols = pl.ds(pl.multiple_of(head * HD, HD), HD)
        own = pl.ds(p * HD, HD)
        spots = (
            (up_ref, up_in.at[:, own]),
            (fq_ref, q_in.at[:, own]),
            (fv_ref, v_in.at[:, own]),
            (fk_ref, buffer.at[(*entry[:-1], slice(None), pl.ds(entry[-1] + HD, HD))]),
            (go_ref, buffer.at[(*entry[:-1], slice(None), pl.ds(entry[-1] + 3 * HD, HD))]),
        )
        for t, (ref, spot) in enumerate(spots):
            copies.append(pltpu.make_async_copy(ref.at[:, cols], spot, sems.at[p, t]))
            copies[-1].start()
    return copies


def raise_heads(low, copies, places, q_in, v_in, up_in, turns=None, done=None):
    lanes = lax.broadcasted_iota(jnp.int32, (ROWS, BOTH), 1)
    none = jnp.zeros_like(low)
    lows = jnp.concatenate([jnp.where(lanes < RANK, low, none), jnp.where(lanes < RANK, none, low)], axis=0)
    for copy in copies:
        copy.wait()
    raised = jnp.dot(lows, up_in[...], preferred_element_type=F32)
    for t, p in enumerate(turns or range(len(places))):
        buffer, entry = places[p]
        own = slice(p * HD, (p + 1) * HD)
        q = (q_in[:, own].astype(F32) + adapter_scale * raised[:ROWS, own]).astype(BF16)
        v = (v_in[:, own].astype(F32) + adapter_scale * raised[ROWS:, own]).astype(BF16)
        buffer[(*entry[:-1], slice(None), pl.ds(entry[-1], HD))] = q
        buffer[(*entry[:-1], slice(None), pl.ds(entry[-1] + 2 * HD, HD))] = v
        if done is not None:
            done(t)


HALF = HEADS // 2


def head_scratch(count):
    return [
        pltpu.VMEM((ROWS, count * HD), BF16),
        pltpu.VMEM((ROWS, count * HD), BF16),
        pltpu.VMEM((BOTH, count * HD), BF16),
        pltpu.SemaphoreType.DMA((count, 5)),
    ]


def prepare_plain_kernel(flags, x_hbm, down_hbm, *refs):
    frozen, (out_hbm, order, spot, low_ref, out_ref, out_sems, *refs) = refs[:5], refs[5:]
    x_in, down_in, whole_sems, q_in, v_in, up_in, sems = refs
    wholes = [
        pltpu.make_async_copy(x_hbm, x_in, whole_sems.at[0]),
        pltpu.make_async_copy(down_hbm, down_in, whole_sems.at[1]),
    ]
    for copy in wholes:
        copy.start()
    order_heads(flags, order)
    me = lax.axis_index("ulysses")
    spot[SPOT_Y] = me % YS
    spot[SPOT_PLAIN] = me % MEMBERS
    spot[SPOT_SHIFT] = (me + YS) % MEMBERS
    spot[SPOT_OWN_PLAIN] = me // YS % 2 * PLANE
    spot[SPOT_OWN_SHIFT] = (1 - me // YS % 2) * PLANE
    places = [(out_ref, (p % MEMBERS, p // MEMBERS * 4 * HD)) for p in range(HALF)]
    copies = fetch_heads([order[p] for p in range(HALF)], places, *frozen, q_in, v_in, up_in, sems)
    for copy in wholes:
        copy.wait()
    low = dot_t(x_in[...], down_in[...]).astype(BF16)
    low_ref[...] = low
    for seat in range(MEMBERS):
        out_ref[seat, :, pl.ds(8 * HD, BOTH)] = low
    sends = [
        pltpu.make_async_copy(out_ref.at[seat], out_hbm.at[seat], out_sems.at[seat]) for seat in range(MEMBERS)
    ]

    def done(t):
        if t % 2 == 1 and t > 1:
            sends[t // 2 - 1].start()

    turns = [seat + half * MEMBERS for seat in range(MEMBERS) for half in range(2)]
    raise_heads(low, copies, places, q_in, v_in, up_in, turns, done)
    sends[-1].start()
    for send in sends:
        send.wait()


def prepare_plain(flags, x, down, frozen):
    return call(
        prepare_plain_kernel,
        "prepare_plain",
        1,
        [ANYWHERE] * 7,
        [ANYWHERE, SCALARS, SCALARS, block((ROWS, BOTH))],
        (
            jax.ShapeDtypeStruct((MEMBERS, ROWS, 8 * HD + BOTH), BF16),
            jax.ShapeDtypeStruct((HEADS,), jnp.int32),
            jax.ShapeDtypeStruct((MEMBERS,), jnp.int32),
            jax.ShapeDtypeStruct((ROWS, BOTH), BF16),
        ),
        [pltpu.VMEM((MEMBERS, ROWS, 8 * HD + BOTH), BF16), pltpu.SemaphoreType.DMA((MEMBERS,))]
        + [pltpu.VMEM((ROWS, WIDTH), BF16), pltpu.VMEM((BOTH, WIDTH), BF16), pltpu.SemaphoreType.DMA((2,))]
        + head_scratch(HALF),
        (10**9, 8 * 10**6),
    )(flags, x, down, *frozen)


def prepare_third_kernel(order, spot, low_ref, *refs):
    frozen, outs, scratch = refs[:5], refs[5:7], refs[7:]
    y, own_half = spot[SPOT_Y], spot[SPOT_OWN_SHIFT] // PLANE
    heads, places = [], []
    for other in range(2):
        for dy in range(YS):
            seat = (own_half + other) % 2 * YS + (y + dy) % YS
            heads.append(order[2 * MEMBERS + seat])
            places.append((outs[other], (dy, 0)))
    copies = fetch_heads(heads, places, *frozen, *scratch)
    raise_heads(low_ref[...], copies, places, *scratch[:3])


def prepare_last_kernel(order, spot, low_ref, *refs):
    frozen, out_ref, scratch = refs[:5], refs[5], refs[6:]
    heads = [order[3 * MEMBERS + seat] for seat in range(MEMBERS)]
    places = [(out_ref, (seat, 0)) for seat in range(MEMBERS)]
    for seat in range(MEMBERS):
        out_ref[seat, :, pl.ds(4 * HD, BOTH)] = low_ref[...]
    copies = fetch_heads(heads, places, *frozen, *scratch)
    raise_heads(low_ref[...], copies, places, *scratch[:3])


def prepare_shifted(item, order, spot, low, frozen):
    shapes = [(YS, ROWS, 4 * HD)] * 2 if item == 2 else [(MEMBERS, ROWS, 4 * HD + BOTH)]
    return call(
        prepare_third_kernel if item == 2 else prepare_last_kernel,
        "prepare_third" if item == 2 else "prepare_last",
        2,
        [block((ROWS, BOTH))] + [ANYWHERE] * 5,
        [block(shape) for shape in shapes],
        [jax.ShapeDtypeStruct(shape, BF16) for shape in shapes],
        head_scratch(MEMBERS),
        (10**9, 8 * 10**6),
    )(order, spot, low, *frozen)


def pack_kernel(own_ref, other_ref, *out_refs):
    for dy, out_ref in enumerate(out_refs, 1):
        out_ref[:, pl.ds(0, 4 * HD)] = own_ref[dy]
        out_ref[:, pl.ds(4 * HD, 4 * HD)] = other_ref[dy]


def pack(own, other):
    shape = (ROWS, 8 * HD)
    return call(
        pack_kernel,
        "pack_third",
        0,
        [block(own.shape)] * 2,
        [block(shape)] * 3,
        (jax.ShapeDtypeStruct(shape, BF16),) * 3,
        [],
        (0, 4 * 10**6),
    )(own, other)


def turn_kernel(spot, x_ref, *out_refs):
    x, core = spot[0] // CS, spot[0] % CS
    *out_refs, stage = out_refs
    for u in range(HEADS):
        stage[pl.ds(u * HD, HD), :] = x_ref[:, pl.ds(u * HD, HD)].T
    for step, out_ref in enumerate(out_refs):
        for other in range(CS):
            d = (x + step) % XS * CS + (core + other) % CS
            for u in range(HEADS):
                rows = pl.ds(pl.multiple_of(u * HD + d * PIECE, PIECE), PIECE)
                out_ref[other, pl.ds(u * PIECE, PIECE), :] = stage[rows, :]


def turn(place, x):
    shape = (CS, HEADS * PIECE, ROWS)
    return call(
        turn_kernel,
        "turn_input",
        1,
        [block(x.shape)],
        [block(shape)] * XS,
        (jax.ShapeDtypeStruct(shape, BF16),) * XS,
        [pltpu.VMEM((WIDTH, ROWS), BF16)],
        (10**9, 2 * 10**6),
    )(place, x)


def attend(x_ref, up_of, grads_ref, column, dv_acc):
    factor = 1.0 / math.sqrt(HD)
    bend = factor * math.log2(math.e)
    row_ids = lax.broadcasted_iota(jnp.int32, (RB, RB), 0)
    column_ids = lax.broadcasted_iota(jnp.int32, (RB, RB), 1)
    keep = column_ids <= row_ids
    for i in range(GROUP // RB):
        n = (i + 1) * RB
        rows = pl.ds(i * RB, RB)
        q = x_ref[rows, pl.ds(0, HD)]
        g = x_ref[rows, pl.ds(3 * HD, HD)]
        k = x_ref[pl.ds(0, n), pl.ds(HD, HD)]
        v = x_ref[pl.ds(0, n), pl.ds(2 * HD, HD)]
        scores = dot_t(q, k)
        last = jnp.where(keep, scores[:, i * RB :], -1e30)
        scores = last if i == 0 else jnp.concatenate([scores[:, : i * RB], last], axis=1)
        top = jnp.max(scores, axis=1, keepdims=True)
        weights = jnp.exp2((scores - top) * bend)
        total = jnp.sum(weights, axis=1, keepdims=True)
        attention = (weights * (1.0 / total)).astype(BF16)
        grad_attention = dot_t(g, v)
        center = jnp.sum(attention.astype(F32) * grad_attention, axis=1, keepdims=True)
        grad_scores = (attention.astype(F32) * (grad_attention - center)).astype(BF16)
        dq = jnp.dot(grad_scores, k, preferred_element_type=F32) * factor
        grads_ref[rows, pl.ds(column, HD)] = dq.astype(BF16)
        dv = dot_0(g, attention)
        if i:
            dv_acc[:, pl.ds(0, i * RB)] += dv[:, : i * RB]
        dv_acc[:, rows] = dv[:, i * RB :]
    dq = grads_ref[:, pl.ds(column, HD)]
    dv = dv_acc[...].T.astype(BF16)
    grads_ref[:, pl.ds(column + HD, HD)] = dv
    lanes = lax.broadcasted_iota(jnp.int32, (GROUP, BOTH), 1)
    up = up_of()
    return jnp.where(lanes < RANK, dot_t(dq, up), dot_t(dv, up))


def attention_plain_kernel(order, spot, arrived, up_hbm, mine_ref, theirs_ref, grads_ref, xs, dv_acc, total, sems, *ups):
    up_in, up_sems = ups
    copies = []
    for item in range(2):
        source = arrived.at[:, pl.ds(item * 4 * HD, 4 * HD)]
        copies.append(pltpu.make_async_copy(source, xs.at[item], sems.at[item]))
        copies[-1].start()
    up_of = [fetch_up(item, order, spot, up_hbm, up_in.at[item], up_sems.at[item]) for item in range(2)]
    copies[0].wait()
    total[...] = attend(xs.at[0], up_of[0], grads_ref, 0, dv_acc)
    copies[1].wait()
    total[...] += attend(xs.at[1], up_of[1], grads_ref, 2 * HD, dv_acc)
    own = pl.multiple_of(spot[SPOT_OWN_PLAIN], PLANE)
    mine_ref[...] = total[pl.ds(own, PLANE), :]
    theirs_ref[...] = total[pl.ds(PLANE - own, PLANE), :].astype(BF16)


def fetch_up(item, order, spot, up_hbm, up_in, sem):
    head = order[item * MEMBERS + spot[SPOT_PLAIN if item < 2 else SPOT_SHIFT]]
    copy = pltpu.make_async_copy(up_hbm.at[:, pl.ds(pl.multiple_of(head * HD, HD), HD)], up_in, sem)
    copy.start()

    def wait_up():
        copy.wait()
        return up_in[...]

    return wait_up


def attention_plain(order, spot, arrived, up):
    shapes = [((PLANE, BOTH), F32), ((PLANE, BOTH), BF16), ((GROUP, 4 * HD), BF16)]
    return call(
        attention_plain_kernel,
        "attention_plain",
        2,
        [ANYWHERE] * 2,
        [block(shape) for shape, _ in shapes],
        [jax.ShapeDtypeStruct(*shape) for shape in shapes],
        [
            pltpu.VMEM((2, GROUP, 4 * HD), BF16),
            pltpu.VMEM((HD, GROUP), F32),
            pltpu.VMEM((GROUP, BOTH), F32),
            pltpu.SemaphoreType.DMA((2,)),
            pltpu.VMEM((2, BOTH, HD), BF16),
            pltpu.SemaphoreType.DMA((2,)),
        ],
        (2 * 10**10, 4 * 10**6),
    )(order, spot, arrived, up)


def attention_shifted_kernel(last, order, spot, *refs):
    y, own = spot[SPOT_Y], spot[SPOT_OWN_SHIFT]
    if last:
        arrived, up, before_hbm, mine_hbm, theirs_hbm, back_ref, grads_hbm, x_in, dv_acc, sems, *refs = refs
        up_in, up_sem, total, before_ref, mine_ref, theirs_ref, grads_ref, more_sems = refs
        pltpu.make_async_copy(arrived.at[:, pl.ds(0, 4 * HD)], x_in, sems.at[0]).start()
    else:
        own_ref, other_ref, *pieces = refs[:5]
        up, back_ref, grads_ref, x_in, dv_acc, sems, up_in, up_sem = refs[5:]
        for dy in range(YS):
            for half in range(2):
                at = (own if half == 0 else PLANE - own) // ROWS + (y - dy + YS) % YS
                rows = pl.ds(pl.multiple_of(at * ROWS, ROWS), ROWS)
                if dy == 0:
                    source = (own_ref, other_ref)[half].at[0]
                else:
                    source = pieces[dy - 1].at[:, pl.ds(half * 4 * HD, 4 * HD)]
                pltpu.make_async_copy(source, x_in.at[rows, :], sems.at[2 * dy + half]).start()
    up_of = fetch_up(3 if last else 2, order, spot, up, up_in, up_sem)
    if last:
        pairs = ((before_hbm, before_ref), (mine_hbm, mine_ref), (theirs_hbm, theirs_ref))
        others = [pltpu.make_async_copy(*pair, more_sems.at[t]) for t, pair in enumerate(pairs)]
        for copy in others:
            copy.start()
    if last:
        pltpu.make_async_copy(arrived.at[:, pl.ds(0, 4 * HD)], x_in, sems.at[0]).wait()
    else:
        for t in range(MEMBERS):
            pltpu.make_async_copy(own_ref.at[0], x_in.at[pl.ds(t * ROWS, ROWS), :], sems.at[t]).wait()
    back = attend(x_in, up_of, grads_ref, 0, dv_acc)
    if not last:
        back_ref[...] = back
        return
    save = pltpu.make_async_copy(grads_ref, grads_hbm, more_sems.at[3])
    save.start()
    for copy in others:
        copy.wait()
    total[...] = back + before_ref[...]
    mine_rows = pl.ds(pl.multiple_of(own, PLANE), PLANE)
    total[mine_rows, :] += mine_ref[...] + theirs_ref[...].astype(F32)
    back_ref[...] = total[...].astype(BF16)
    save.wait()


LAST_SCRATCH = [
    pltpu.VMEM((GROUP, BOTH), F32),
    pltpu.VMEM((GROUP, BOTH), F32),
    pltpu.VMEM((PLANE, BOTH), F32),
    pltpu.VMEM((PLANE, BOTH), BF16),
    pltpu.VMEM((GROUP, 2 * HD), BF16),
    pltpu.SemaphoreType.DMA((4,)),
]


def attention_shifted(order, spot, arrived, up, *more):
    last = len(more) > 0
    shapes = [((GROUP, BOTH), BF16 if last else F32), ((GROUP, 2 * HD), BF16)]

    def body(*refs):
        attention_shifted_kernel(last, *refs)

    return call(
        body,
        "attention_last" if last else "attention_third",
        2,
        [pl.BlockSpec(memory_space=pl.ANY) if last else ANYWHERE] * len(arrived)
        + [ANYWHERE] * (1 + len(more)),
        [block(shapes[0][0]), ANYWHERE] if last else [block(shape) for shape, _ in shapes],
        [jax.ShapeDtypeStruct(*shape) for shape in shapes],
        [pltpu.VMEM((GROUP, 4 * HD), BF16), pltpu.VMEM((HD, GROUP), F32), pltpu.SemaphoreType.DMA((2 * YS,))]
        + [pltpu.VMEM((BOTH, HD), BF16), pltpu.SemaphoreType.DMA]
        + LAST_SCRATCH * last,
        (4 * 10**9, 3 * 10**6) if last else (10**10, 10**4),
    )(order, spot, *arrived, up, *more)


def up_gradient_kernel(low_a, low_b, *refs):
    out_ref = refs[-1]
    for item in range(4):
        low = (low_a, low_b)[item // 2][...]
        grads, column = ((refs[0], 0), (refs[0], 2 * HD), (refs[1], 0), (refs[2], 0))[item]
        for m in range(2):
            columns = pl.ds(column + m * HD, HD)
            part = adapter_scale * dot_0(low[:, m * RANK : (m + 1) * RANK], grads[:, columns])
            part = part.astype(BF16)
            for e in range(RANK // PIECE):
                d = m * (RANK // PIECE) + e
                out_ref[d, pl.ds(item * PIECE, PIECE), :] = part[e * PIECE : (e + 1) * PIECE]


def up_gradients(plain, late, grads):
    shape = (SLICES, 4 * PIECE, HD)
    lows = [pl.BlockSpec((GROUP, BOTH), lambda i, column=column: (0, column)) for column in (8, 4)]
    return call(
        up_gradient_kernel,
        "up_gradients",
        0,
        lows + [block(array.shape) for array in grads],
        block(shape),
        jax.ShapeDtypeStruct(shape, BF16),
        [],
        (2 * 10**9, 3 * 10**6),
    )(plain, late, *grads)


def gather_kernel(summed_ref, ups_ref, out_ref):
    back = jnp.sum(summed_ref[...].astype(F32), axis=0).astype(BF16)
    for d in range(SLICES):
        out_ref[d, pl.ds(0, ROWS), :] = back
    out_ref[:, pl.ds(ROWS, 4 * PIECE), :] = ups_ref[...]


def gather_parts(summed, ups):
    shape = (SLICES, ROWS + 4 * PIECE, HD)
    return call(
        gather_kernel,
        "gather_parts",
        0,
        [block(summed.shape), block(ups.shape)],
        block(shape),
        jax.ShapeDtypeStruct(shape, BF16),
        [],
        (10**7, 10**6),
        16,
    )(summed, ups)


def merge_kernel(order, spot, place, both_ref, *refs):
    x_refs, crossed_ref, out_ref = refs[:-2], refs[-2], refs[-1]
    x, core = place[0] // CS, place[0] % CS
    total = jnp.zeros((HEADS * PIECE, BOTH), F32)
    for dx in range(XS):
        for other in range(CS):
            s = (x - dx + XS) % XS * CS + (core + other) % CS
            back = both_ref[s, pl.ds(0, ROWS), :]
            part = x_refs[dx][0] if other == 0 else crossed_ref[dx]
            total += jnp.dot(part, back, preferred_element_type=F32)
    total = (adapter_scale * total).astype(BF16)
    for u in range(HEADS):
        out_ref[u, pl.ds(0, PIECE), :] = total[u * PIECE : (u + 1) * PIECE]
        out_ref[u, pl.ds(PIECE, PIECE), :] = jnp.zeros((PIECE, HD), BF16)
    ups = jnp.sum(both_ref[:, pl.ds(ROWS, 4 * PIECE), :].astype(F32), axis=0).astype(BF16)
    for item in range(4):
        seat = spot[SPOT_PLAIN if item < 2 else SPOT_SHIFT]
        head = order[item * MEMBERS + seat]
        out_ref[head, pl.ds(PIECE, PIECE), :] = ups[item * PIECE : (item + 1) * PIECE]


def merge(order, spot, place, both, pieces, crossed):
    shape = (HEADS, 2 * PIECE, HD)
    return call(
        merge_kernel,
        "merge_gradients",
        3,
        [block(both.shape)] + [block((1, *piece.shape[1:])) for piece in pieces] + [block(crossed.shape)],
        block(shape),
        jax.ShapeDtypeStruct(shape, BF16),
        [],
        (2 * 10**8, 2 * 10**6),
        16,
    )(order, spot, place, both, *pieces, crossed)


def spread_kernel(in_ref, out_ref):
    total = jnp.sum(in_ref[...].astype(F32), axis=0)
    for d in range(SLICES):
        out_ref[d] = total


def spread(both):
    shape = (SLICES, 2 * PIECE, HD)
    return call(
        spread_kernel,
        "spread_sums",
        0,
        [block(both.shape)],
        block(shape),
        jax.ShapeDtypeStruct(shape, F32),
        [],
        (10**6, 10**6),
        16,
    )(both)


def finish_kernel(in_ref, down_ref, up_ref):
    down = in_ref[:, pl.ds(0, PIECE), :].reshape(HD, BOTH).T
    up = in_ref[:, pl.ds(PIECE, PIECE), :].reshape(BOTH, HD)
    for m in range(2):
        down_ref[m] = down[m * RANK : (m + 1) * RANK]
        up_ref[m] = up[m * RANK : (m + 1) * RANK]


def finish(both):
    shape = (2, RANK, HD)
    return call(
        finish_kernel,
        "finish",
        0,
        [block(both.shape)],
        [block(shape)] * 2,
        [jax.ShapeDtypeStruct(shape, F32)] * 2,
        [],
        (10**6, 10**6),
        16,
    )(both)


def per_device(
    normalized_input,
    frozen_queries,
    frozen_keys,
    frozen_values,
    output_gradient,
    adapter_down_maps,
    adapter_up_maps,
    shifted,
):
    tokens = normalized_input[0]
    place = lax.axis_index("dp").reshape(1)
    up = adapter_up_maps.reshape(BOTH, WIDTH)
    down = adapter_down_maps.transpose(0, 2, 1).reshape(BOTH, WIDTH)

    frozen = (frozen_queries[0], frozen_keys[0], frozen_values[0], output_gradient[0], up)
    sent, order, spot, low = prepare_plain(shifted.astype(jnp.int32), tokens, down, frozen)
    plain = exchange(sent, "ulysses", PLAIN_GROUPS).reshape(GROUP, 8 * HD + BOTH)
    own_c, other_c = prepare_shifted(2, order, spot, low, frozen)
    other_c = lax.ppermute(other_c, "ulysses", SHIFT_SWAP)
    turned = turn(place, after(tokens, own_c))
    pieces = [turned[0]] + [lax.ppermute(turned[dx], "dp", x_shift(dx)) for dx in (1, 2, 3)]
    (sent,) = prepare_shifted(3, order, spot, after(low, turned), frozen)

    packed = pack(after(own_c, pieces[0], sent), other_c)
    arrived_c = [lax.ppermute(packed[dy - 1], "ulysses", y_shift(dy)) for dy in (1, 2, 3)]
    plain, pieces, sent = after((plain, pieces, sent), packed)

    arrived_d = exchange(sent, "ulysses", SHIFT_GROUPS).reshape(GROUP, 4 * HD + BOTH)
    crossed = lax.ppermute(jnp.stack([piece[1] for piece in pieces]), "dp", CORE_SWAP)
    mine, theirs, grads_plain = attention_plain(order, spot, plain, up)
    theirs = lax.ppermute(theirs, "ulysses", PLAIN_SWAP)
    arrived_c = after(arrived_c, grads_plain, sent)
    partial, grads_c = attention_shifted(order, spot, [own_c, other_c, *arrived_c], up)

    arrived_d, theirs, crossed = after((arrived_d, theirs, crossed), partial)
    partial, grads_d = attention_shifted(order, spot, [arrived_d], up, partial, mine, theirs)
    summed = exchange(partial.reshape(MEMBERS, ROWS, BOTH), "ulysses", SHIFT_GROUPS)
    ups = up_gradients(plain, arrived_d, (grads_plain, grads_c, grads_d))

    both = exchange(gather_parts(summed, ups), "dp")
    both = exchange(merge(order, spot, place, both, pieces, crossed), "ulysses")
    both = exchange(spread(both), "dp")
    grad_down, grad_up = finish(both)
    return (grad_down.transpose(0, 2, 1), grad_up)


def solution(mesh):
    rows = P("dp", "ulysses", None)
    in_specs = (rows, rows, rows, rows, rows, P(), P(), P())
    out_specs = (P(None, "ulysses", None), P(None, None, "ulysses"))
    return jax.shard_map(
        per_device, mesh=mesh, in_specs=in_specs, out_specs=out_specs, check_vma=False
    )
```

```python
import math

import jax
import jax.numpy as jnp
from jax import lax
from jax.experimental import pallas as pl
from jax.experimental.pallas import tpu as pltpu
from jax.sharding import PartitionSpec as P

HEADS = 32
HD = 128
WIDTH = HEADS * HD
GROUP = 1024
PLANE = 512
RANK = 64
BOTH = 2 * RANK
ROWS = 128
ZS, YS = 8, 4
XS, CS = 4, 2
SLICES = XS * CS
MEMBERS = 8
PIECE = 16
RB = 256
BF16, F32 = jnp.bfloat16, jnp.float32

adapter_scale = 0.5

PLAIN_GROUPS = [[MEMBERS * g + i for i in range(MEMBERS)] for g in range(4)]
SHIFT_GROUPS = [[(MEMBERS * g + 4 + i) % HEADS for i in range(MEMBERS)] for g in range(4)]
PLAIN_SWAP = [(u, u ^ 4) for u in range(HEADS)]
SHIFT_SWAP = [(u, (((u + 4) % HEADS ^ 4) - 4) % HEADS) for u in range(HEADS)]
CORE_SWAP = [(d, d ^ 1) for d in range(SLICES)]
ANYWHERE = pl.BlockSpec(memory_space=pltpu.HBM)
SCALARS = pl.BlockSpec(memory_space=pltpu.SMEM)

SPOT_Y, SPOT_PLAIN, SPOT_SHIFT, SPOT_OWN_PLAIN, SPOT_OWN_SHIFT = range(5)


def y_shift(dy):
    return [(z * YS + y, z * YS + (y + dy) % YS) for z in range(ZS) for y in range(YS)]


def x_shift(dx):
    return [(x * CS + c, ((x + dx) % XS) * CS + c) for x in range(XS) for c in range(CS)]


def exchange(member, axis, groups=None):
    return lax.all_to_all(member, axis, 0, 0, tiled=True, axis_index_groups=groups)


def after(values, *others):
    return lax.optimization_barrier((values, others))[0]


def block(shape):
    return pl.BlockSpec(shape, lambda i, *s: (0,) * len(shape))


def dot_t(a, b):
    return lax.dot_general(a, b, (((1,), (1,)), ((), ())), preferred_element_type=F32)


def dot_0(a, b):
    return lax.dot_general(a, b, (((0,), (0,)), ((), ())), preferred_element_type=F32)


def call(kernel, name, scalars, in_specs, out_specs, out_shape, scratch, cost, vmem=None):
    params = pltpu.CompilerParams(vmem_limit_bytes=vmem and vmem * 2**20)
    return pl.pallas_call(
        kernel,
        name=name,
        out_shape=out_shape,
        grid_spec=pltpu.PrefetchScalarGridSpec(
            num_scalar_prefetch=scalars,
            grid=(1,),
            in_specs=in_specs,
            out_specs=out_specs,
            scratch_shapes=scratch,
        ),
        compiler_params=params,
        cost_estimate=pl.CostEstimate(flops=cost[0], bytes_accessed=cost[1], transcendentals=0),
    )


def order_heads(flags, order):
    def place(h, ones):
        flag = flags[h]
        order[jnp.where(flag > 0, HEADS // 2 + ones, h - ones)] = h
        return ones + jnp.where(flag > 0, 1, 0)

    lax.fori_loop(0, HEADS, place, 0, unroll=True)


def fetch_heads(heads, places, fq_ref, fk_ref, fv_ref, go_ref, up_ref, q_in, v_in, up_in, sems):
    copies = []
    for p, (head, (buffer, entry)) in enumerate(zip(heads, places)):
        cols = pl.ds(pl.multiple_of(head * HD, HD), HD)
        own = pl.ds(p * HD, HD)
        spots = (
            (up_ref, up_in.at[:, own]),
            (fq_ref, q_in.at[:, own]),
            (fv_ref, v_in.at[:, own]),
            (fk_ref, buffer.at[(*entry[:-1], slice(None), pl.ds(entry[-1] + HD, HD))]),
            (go_ref, buffer.at[(*entry[:-1], slice(None), pl.ds(entry[-1] + 3 * HD, HD))]),
        )
        for t, (ref, spot) in enumerate(spots):
            copies.append(pltpu.make_async_copy(ref.at[:, cols], spot, sems.at[p, t]))
            copies[-1].start()
    return copies


def raise_heads(low, copies, places, q_in, v_in, up_in):
    lanes = lax.broadcasted_iota(jnp.int32, (ROWS, BOTH), 1)
    none = jnp.zeros_like(low)
    lows = jnp.concatenate([jnp.where(lanes < RANK, low, none), jnp.where(lanes < RANK, none, low)], axis=0)
    for copy in copies:
        copy.wait()
    raised = jnp.dot(lows, up_in[...], preferred_element_type=F32)
    for p, (buffer, entry) in enumerate(places):
        own = slice(p * HD, (p + 1) * HD)
        q = (q_in[:, own].astype(F32) + adapter_scale * raised[:ROWS, own]).astype(BF16)
        v = (v_in[:, own].astype(F32) + adapter_scale * raised[ROWS:, own]).astype(BF16)
        buffer[(*entry[:-1], slice(None), pl.ds(entry[-1], HD))] = q
        buffer[(*entry[:-1], slice(None), pl.ds(entry[-1] + 2 * HD, HD))] = v


HALF = HEADS // 2


def head_scratch(count):
    return [
        pltpu.VMEM((ROWS, count * HD), BF16),
        pltpu.VMEM((ROWS, count * HD), BF16),
        pltpu.VMEM((BOTH, count * HD), BF16),
        pltpu.SemaphoreType.DMA((count, 5)),
    ]


def prepare_plain_kernel(flags, x_hbm, down_hbm, *refs):
    frozen, (out_ref, order, spot, low_ref, x_in, down_in, whole_sems, q_in, v_in, up_in, sems) = refs[:5], refs[5:]
    wholes = [
        pltpu.make_async_copy(x_hbm, x_in, whole_sems.at[0]),
        pltpu.make_async_copy(down_hbm, down_in, whole_sems.at[1]),
    ]
    for copy in wholes:
        copy.start()
    order_heads(flags, order)
    me = lax.axis_index("ulysses")
    spot[SPOT_Y] = me % YS
    spot[SPOT_PLAIN] = me % MEMBERS
    spot[SPOT_SHIFT] = (me + YS) % MEMBERS
    spot[SPOT_OWN_PLAIN] = me // YS % 2 * PLANE
    spot[SPOT_OWN_SHIFT] = (1 - me // YS % 2) * PLANE
    places = [(out_ref, (p % MEMBERS, p // MEMBERS * 4 * HD)) for p in range(HALF)]
    copies = fetch_heads([order[p] for p in range(HALF)], places, *frozen, q_in, v_in, up_in, sems)
    for copy in wholes:
        copy.wait()
    low = dot_t(x_in[...], down_in[...]).astype(BF16)
    low_ref[...] = low
    for seat in range(MEMBERS):
        out_ref[seat, :, pl.ds(8 * HD, BOTH)] = low
    raise_heads(low, copies, places, q_in, v_in, up_in)


def prepare_plain(flags, x, down, frozen):
    return call(
        prepare_plain_kernel,
        "prepare_plain",
        1,
        [ANYWHERE] * 7,
        [block((MEMBERS, ROWS, 8 * HD + BOTH)), SCALARS, SCALARS, block((ROWS, BOTH))],
        (
            jax.ShapeDtypeStruct((MEMBERS, ROWS, 8 * HD + BOTH), BF16),
            jax.ShapeDtypeStruct((HEADS,), jnp.int32),
            jax.ShapeDtypeStruct((MEMBERS,), jnp.int32),
            jax.ShapeDtypeStruct((ROWS, BOTH), BF16),
        ),
        [pltpu.VMEM((ROWS, WIDTH), BF16), pltpu.VMEM((BOTH, WIDTH), BF16), pltpu.SemaphoreType.DMA((2,))]
        + head_scratch(HALF),
        (10**9, 8 * 10**6),
    )(flags, x, down, *frozen)


def prepare_third_kernel(order, spot, low_ref, *refs):
    frozen, outs, scratch = refs[:5], refs[5:7], refs[7:]
    y, own_half = spot[SPOT_Y], spot[SPOT_OWN_SHIFT] // PLANE
    heads, places = [], []
    for other in range(2):
        for dy in range(YS):
            seat = (own_half + other) % 2 * YS + (y + dy) % YS
            heads.append(order[2 * MEMBERS + seat])
            places.append((outs[other], (dy, 0)))
    copies = fetch_heads(heads, places, *frozen, *scratch)
    raise_heads(low_ref[...], copies, places, *scratch[:3])


def prepare_last_kernel(order, spot, low_ref, *refs):
    frozen, out_ref, scratch = refs[:5], refs[5], refs[6:]
    heads = [order[3 * MEMBERS + seat] for seat in range(MEMBERS)]
    places = [(out_ref, (seat, 0)) for seat in range(MEMBERS)]
    for seat in range(MEMBERS):
        out_ref[seat, :, pl.ds(4 * HD, BOTH)] = low_ref[...]
    copies = fetch_heads(heads, places, *frozen, *scratch)
    raise_heads(low_ref[...], copies, places, *scratch[:3])


def prepare_shifted(item, order, spot, low, frozen):
    shapes = [(YS, ROWS, 4 * HD)] * 2 if item == 2 else [(MEMBERS, ROWS, 4 * HD + BOTH)]
    return call(
        prepare_third_kernel if item == 2 else prepare_last_kernel,
        "prepare_third" if item == 2 else "prepare_last",
        2,
        [block((ROWS, BOTH))] + [ANYWHERE] * 5,
        [block(shape) for shape in shapes],
        [jax.ShapeDtypeStruct(shape, BF16) for shape in shapes],
        head_scratch(MEMBERS),
        (10**9, 8 * 10**6),
    )(order, spot, low, *frozen)


def pack_kernel(own_ref, other_ref, *out_refs):
    for dy, out_ref in enumerate(out_refs, 1):
        out_ref[:, pl.ds(0, 4 * HD)] = own_ref[dy]
        out_ref[:, pl.ds(4 * HD, 4 * HD)] = other_ref[dy]


def pack(own, other):
    shape = (ROWS, 8 * HD)
    return call(
        pack_kernel,
        "pack_third",
        0,
        [block(own.shape)] * 2,
        [block(shape)] * 3,
        (jax.ShapeDtypeStruct(shape, BF16),) * 3,
        [],
        (0, 4 * 10**6),
    )(own, other)


def turn_kernel(spot, x_ref, *out_refs):
    x, core = spot[0] // CS, spot[0] % CS
    *out_refs, stage = out_refs
    for u in range(HEADS):
        stage[pl.ds(u * HD, HD), :] = x_ref[:, pl.ds(u * HD, HD)].T
    for step, out_ref in enumerate(out_refs):
        for other in range(CS):
            d = (x + step) % XS * CS + (core + other) % CS
            for u in range(HEADS):
                rows = pl.ds(pl.multiple_of(u * HD + d * PIECE, PIECE), PIECE)
                out_ref[other, pl.ds(u * PIECE, PIECE), :] = stage[rows, :]


def turn(place, x):
    shape = (CS, HEADS * PIECE, ROWS)
    return call(
        turn_kernel,
        "turn_input",
        1,
        [block(x.shape)],
        [block(shape)] * XS,
        (jax.ShapeDtypeStruct(shape, BF16),) * XS,
        [pltpu.VMEM((WIDTH, ROWS), BF16)],
        (10**9, 2 * 10**6),
    )(place, x)


def attend(x_ref, up_of, grads_ref, column, dv_acc):
    factor = 1.0 / math.sqrt(HD)
    bend = factor * math.log2(math.e)
    row_ids = lax.broadcasted_iota(jnp.int32, (RB, RB), 0)
    column_ids = lax.broadcasted_iota(jnp.int32, (RB, RB), 1)
    keep = column_ids <= row_ids
    for i in range(GROUP // RB):
        n = (i + 1) * RB
        rows = pl.ds(i * RB, RB)
        q = x_ref[rows, pl.ds(0, HD)]
        g = x_ref[rows, pl.ds(3 * HD, HD)]
        k = x_ref[pl.ds(0, n), pl.ds(HD, HD)]
        v = x_ref[pl.ds(0, n), pl.ds(2 * HD, HD)]
        scores = dot_t(q, k)
        last = jnp.where(keep, scores[:, i * RB :], -1e30)
        scores = last if i == 0 else jnp.concatenate([scores[:, : i * RB], last], axis=1)
        top = jnp.max(scores, axis=1, keepdims=True)
        weights = jnp.exp2((scores - top) * bend)
        total = jnp.sum(weights, axis=1, keepdims=True)
        attention = (weights * (1.0 / total)).astype(BF16)
        grad_attention = dot_t(g, v)
        center = jnp.sum(attention.astype(F32) * grad_attention, axis=1, keepdims=True)
        grad_scores = (attention.astype(F32) * (grad_attention - center)).astype(BF16)
        dq = jnp.dot(grad_scores, k, preferred_element_type=F32) * factor
        grads_ref[rows, pl.ds(column, HD)] = dq.astype(BF16)
        dv = dot_0(g, attention)
        if i:
            dv_acc[:, pl.ds(0, i * RB)] += dv[:, : i * RB]
        dv_acc[:, rows] = dv[:, i * RB :]
    dq = grads_ref[:, pl.ds(column, HD)]
    dv = dv_acc[...].T.astype(BF16)
    grads_ref[:, pl.ds(column + HD, HD)] = dv
    lanes = lax.broadcasted_iota(jnp.int32, (GROUP, BOTH), 1)
    up = up_of()
    return jnp.where(lanes < RANK, dot_t(dq, up), dot_t(dv, up))


def attention_plain_kernel(order, spot, arrived, up_hbm, mine_ref, theirs_ref, grads_ref, xs, dv_acc, total, sems, *ups):
    up_in, up_sems = ups
    copies = []
    for item in range(2):
        source = arrived.at[:, pl.ds(item * 4 * HD, 4 * HD)]
        copies.append(pltpu.make_async_copy(source, xs.at[item], sems.at[item]))
        copies[-1].start()
    up_of = [fetch_up(item, order, spot, up_hbm, up_in.at[item], up_sems.at[item]) for item in range(2)]
    copies[0].wait()
    total[...] = attend(xs.at[0], up_of[0], grads_ref, 0, dv_acc)
    copies[1].wait()
    total[...] += attend(xs.at[1], up_of[1], grads_ref, 2 * HD, dv_acc)
    own = pl.multiple_of(spot[SPOT_OWN_PLAIN], PLANE)
    mine_ref[...] = total[pl.ds(own, PLANE), :]
    theirs_ref[...] = total[pl.ds(PLANE - own, PLANE), :].astype(BF16)


def fetch_up(item, order, spot, up_hbm, up_in, sem):
    head = order[item * MEMBERS + spot[SPOT_PLAIN if item < 2 else SPOT_SHIFT]]
    copy = pltpu.make_async_copy(up_hbm.at[:, pl.ds(pl.multiple_of(head * HD, HD), HD)], up_in, sem)
    copy.start()

    def wait_up():
        copy.wait()
        return up_in[...]

    return wait_up


def attention_plain(order, spot, arrived, up):
    shapes = [((PLANE, BOTH), F32), ((PLANE, BOTH), BF16), ((GROUP, 4 * HD), BF16)]
    return call(
        attention_plain_kernel,
        "attention_plain",
        2,
        [ANYWHERE] * 2,
        [block(shape) for shape, _ in shapes],
        [jax.ShapeDtypeStruct(*shape) for shape in shapes],
        [
            pltpu.VMEM((2, GROUP, 4 * HD), BF16),
            pltpu.VMEM((HD, GROUP), F32),
            pltpu.VMEM((GROUP, BOTH), F32),
            pltpu.SemaphoreType.DMA((2,)),
            pltpu.VMEM((2, BOTH, HD), BF16),
            pltpu.SemaphoreType.DMA((2,)),
        ],
        (2 * 10**10, 4 * 10**6),
    )(order, spot, arrived, up)


def attention_shifted_kernel(last, order, spot, *refs):
    y, own = spot[SPOT_Y], spot[SPOT_OWN_SHIFT]
    if last:
        arrived, up, before_hbm, mine_hbm, theirs_hbm, back_ref, grads_hbm, x_in, dv_acc, sems, *refs = refs
        up_in, up_sem, total, before_ref, mine_ref, theirs_ref, grads_ref, more_sems = refs
        pltpu.make_async_copy(arrived.at[:, pl.ds(0, 4 * HD)], x_in, sems.at[0]).start()
    else:
        own_ref, other_ref, *pieces = refs[:5]
        up, back_ref, grads_ref, x_in, dv_acc, sems, up_in, up_sem = refs[5:]
        for dy in range(YS):
            for half in range(2):
                at = (own if half == 0 else PLANE - own) // ROWS + (y - dy + YS) % YS
                rows = pl.ds(pl.multiple_of(at * ROWS, ROWS), ROWS)
                if dy == 0:
                    source = (own_ref, other_ref)[half].at[0]
                else:
                    source = pieces[dy - 1].at[:, pl.ds(half * 4 * HD, 4 * HD)]
                pltpu.make_async_copy(source, x_in.at[rows, :], sems.at[2 * dy + half]).start()
    up_of = fetch_up(3 if last else 2, order, spot, up, up_in, up_sem)
    if last:
        pairs = ((before_hbm, before_ref), (mine_hbm, mine_ref), (theirs_hbm, theirs_ref))
        others = [pltpu.make_async_copy(*pair, more_sems.at[t]) for t, pair in enumerate(pairs)]
        for copy in others:
            copy.start()
    if last:
        pltpu.make_async_copy(arrived.at[:, pl.ds(0, 4 * HD)], x_in, sems.at[0]).wait()
    else:
        for t in range(MEMBERS):
            pltpu.make_async_copy(own_ref.at[0], x_in.at[pl.ds(t * ROWS, ROWS), :], sems.at[t]).wait()
    back = attend(x_in, up_of, grads_ref, 0, dv_acc)
    if not last:
        back_ref[...] = back
        return
    save = pltpu.make_async_copy(grads_ref, grads_hbm, more_sems.at[3])
    save.start()
    for copy in others:
        copy.wait()
    total[...] = back + before_ref[...]
    mine_rows = pl.ds(pl.multiple_of(own, PLANE), PLANE)
    total[mine_rows, :] += mine_ref[...] + theirs_ref[...].astype(F32)
    back_ref[...] = total[...].astype(BF16)
    save.wait()


LAST_SCRATCH = [
    pltpu.VMEM((GROUP, BOTH), F32),
    pltpu.VMEM((GROUP, BOTH), F32),
    pltpu.VMEM((PLANE, BOTH), F32),
    pltpu.VMEM((PLANE, BOTH), BF16),
    pltpu.VMEM((GROUP, 2 * HD), BF16),
    pltpu.SemaphoreType.DMA((4,)),
]


def attention_shifted(order, spot, arrived, up, *more):
    last = len(more) > 0
    shapes = [((GROUP, BOTH), BF16 if last else F32), ((GROUP, 2 * HD), BF16)]

    def body(*refs):
        attention_shifted_kernel(last, *refs)

    return call(
        body,
        "attention_last" if last else "attention_third",
        2,
        [pl.BlockSpec(memory_space=pl.ANY) if last else ANYWHERE] * len(arrived)
        + [ANYWHERE] * (1 + len(more)),
        [block(shapes[0][0]), ANYWHERE] if last else [block(shape) for shape, _ in shapes],
        [jax.ShapeDtypeStruct(*shape) for shape in shapes],
        [pltpu.VMEM((GROUP, 4 * HD), BF16), pltpu.VMEM((HD, GROUP), F32), pltpu.SemaphoreType.DMA((2 * YS,))]
        + [pltpu.VMEM((BOTH, HD), BF16), pltpu.SemaphoreType.DMA]
        + LAST_SCRATCH * last,
        (4 * 10**9, 3 * 10**6) if last else (10**10, 10**4),
    )(order, spot, *arrived, up, *more)


def up_gradient_kernel(low_a, low_b, *refs):
    out_ref = refs[-1]
    for item in range(4):
        low = (low_a, low_b)[item // 2][...]
        grads, column = ((refs[0], 0), (refs[0], 2 * HD), (refs[1], 0), (refs[2], 0))[item]
        for m in range(2):
            columns = pl.ds(column + m * HD, HD)
            part = adapter_scale * dot_0(low[:, m * RANK : (m + 1) * RANK], grads[:, columns])
            part = part.astype(BF16)
            for e in range(RANK // PIECE):
                d = m * (RANK // PIECE) + e
                out_ref[d, pl.ds(item * PIECE, PIECE), :] = part[e * PIECE : (e + 1) * PIECE]


def up_gradients(plain, late, grads):
    shape = (SLICES, 4 * PIECE, HD)
    lows = [pl.BlockSpec((GROUP, BOTH), lambda i, column=column: (0, column)) for column in (8, 4)]
    return call(
        up_gradient_kernel,
        "up_gradients",
        0,
        lows + [block(array.shape) for array in grads],
        block(shape),
        jax.ShapeDtypeStruct(shape, BF16),
        [],
        (2 * 10**9, 3 * 10**6),
    )(plain, late, *grads)


def gather_kernel(summed_ref, ups_ref, out_ref):
    back = jnp.sum(summed_ref[...].astype(F32), axis=0).astype(BF16)
    for d in range(SLICES):
        out_ref[d, pl.ds(0, ROWS), :] = back
    out_ref[:, pl.ds(ROWS, 4 * PIECE), :] = ups_ref[...]


def gather_parts(summed, ups):
    shape = (SLICES, ROWS + 4 * PIECE, HD)
    return call(
        gather_kernel,
        "gather_parts",
        0,
        [block(summed.shape), block(ups.shape)],
        block(shape),
        jax.ShapeDtypeStruct(shape, BF16),
        [],
        (10**7, 10**6),
        16,
    )(summed, ups)


def merge_kernel(order, spot, place, both_ref, *refs):
    x_refs, crossed_ref, out_ref = refs[:-2], refs[-2], refs[-1]
    x, core = place[0] // CS, place[0] % CS
    total = jnp.zeros((HEADS * PIECE, BOTH), F32)
    for dx in range(XS):
        for other in range(CS):
            s = (x - dx + XS) % XS * CS + (core + other) % CS
            back = both_ref[s, pl.ds(0, ROWS), :]
            part = x_refs[dx][0] if other == 0 else crossed_ref[dx]
            total += jnp.dot(part, back, preferred_element_type=F32)
    total = (adapter_scale * total).astype(BF16)
    for u in range(HEADS):
        out_ref[u, pl.ds(0, PIECE), :] = total[u * PIECE : (u + 1) * PIECE]
        out_ref[u, pl.ds(PIECE, PIECE), :] = jnp.zeros((PIECE, HD), BF16)
    ups = jnp.sum(both_ref[:, pl.ds(ROWS, 4 * PIECE), :].astype(F32), axis=0).astype(BF16)
    for item in range(4):
        seat = spot[SPOT_PLAIN if item < 2 else SPOT_SHIFT]
        head = order[item * MEMBERS + seat]
        out_ref[head, pl.ds(PIECE, PIECE), :] = ups[item * PIECE : (item + 1) * PIECE]


def merge(order, spot, place, both, pieces, crossed):
    shape = (HEADS, 2 * PIECE, HD)
    return call(
        merge_kernel,
        "merge_gradients",
        3,
        [block(both.shape)] + [block((1, *piece.shape[1:])) for piece in pieces] + [block(crossed.shape)],
        block(shape),
        jax.ShapeDtypeStruct(shape, BF16),
        [],
        (2 * 10**8, 2 * 10**6),
        16,
    )(order, spot, place, both, *pieces, crossed)


def spread_kernel(in_ref, out_ref):
    total = jnp.sum(in_ref[...].astype(F32), axis=0)
    for d in range(SLICES):
        out_ref[d] = total


def spread(both):
    shape = (SLICES, 2 * PIECE, HD)
    return call(
        spread_kernel,
        "spread_sums",
        0,
        [block(both.shape)],
        block(shape),
        jax.ShapeDtypeStruct(shape, F32),
        [],
        (10**6, 10**6),
        16,
    )(both)


def finish_kernel(in_ref, down_ref, up_ref):
    down = in_ref[:, pl.ds(0, PIECE), :].reshape(HD, BOTH).T
    up = in_ref[:, pl.ds(PIECE, PIECE), :].reshape(BOTH, HD)
    for m in range(2):
        down_ref[m] = down[m * RANK : (m + 1) * RANK]
        up_ref[m] = up[m * RANK : (m + 1) * RANK]


def finish(both):
    shape = (2, RANK, HD)
    return call(
        finish_kernel,
        "finish",
        0,
        [block(both.shape)],
        [block(shape)] * 2,
        [jax.ShapeDtypeStruct(shape, F32)] * 2,
        [],
        (10**6, 10**6),
        16,
    )(both)


def per_device(
    normalized_input,
    frozen_queries,
    frozen_keys,
    frozen_values,
    output_gradient,
    adapter_down_maps,
    adapter_up_maps,
    shifted,
):
    tokens = normalized_input[0]
    place = lax.axis_index("dp").reshape(1)
    up = adapter_up_maps.reshape(BOTH, WIDTH)
    down = adapter_down_maps.transpose(0, 2, 1).reshape(BOTH, WIDTH)

    frozen = (frozen_queries[0], frozen_keys[0], frozen_values[0], output_gradient[0], up)
    sent, order, spot, low = prepare_plain(shifted.astype(jnp.int32), tokens, down, frozen)
    plain = exchange(sent, "ulysses", PLAIN_GROUPS).reshape(GROUP, 8 * HD + BOTH)
    own_c, other_c = prepare_shifted(2, order, spot, low, frozen)
    other_c = lax.ppermute(other_c, "ulysses", SHIFT_SWAP)
    turned = turn(place, after(tokens, own_c))
    pieces = [turned[0]] + [lax.ppermute(turned[dx], "dp", x_shift(dx)) for dx in (1, 2, 3)]
    (sent,) = prepare_shifted(3, order, spot, after(low, turned), frozen)

    packed = pack(after(own_c, pieces[0], sent), other_c)
    arrived_c = [lax.ppermute(packed[dy - 1], "ulysses", y_shift(dy)) for dy in (1, 2, 3)]
    plain, pieces, sent = after((plain, pieces, sent), packed)

    arrived_d = exchange(sent, "ulysses", SHIFT_GROUPS).reshape(GROUP, 4 * HD + BOTH)
    crossed = lax.ppermute(jnp.stack([piece[1] for piece in pieces]), "dp", CORE_SWAP)
    mine, theirs, grads_plain = attention_plain(order, spot, plain, up)
    theirs = lax.ppermute(theirs, "ulysses", PLAIN_SWAP)
    arrived_c = after(arrived_c, grads_plain, sent)
    partial, grads_c = attention_shifted(order, spot, [own_c, other_c, *arrived_c], up)

    arrived_d, theirs, crossed = after((arrived_d, theirs, crossed), partial)
    partial, grads_d = attention_shifted(order, spot, [arrived_d], up, partial, mine, theirs)
    summed = exchange(partial.reshape(MEMBERS, ROWS, BOTH), "ulysses", SHIFT_GROUPS)
    ups = up_gradients(plain, arrived_d, (grads_plain, grads_c, grads_d))

    both = exchange(gather_parts(summed, ups), "dp")
    both = exchange(merge(order, spot, place, both, pieces, crossed), "ulysses")
    both = exchange(spread(both), "dp")
    grad_down, grad_up = finish(both)
    return (grad_down.transpose(0, 2, 1), grad_up)


def solution(mesh):
    rows = P("dp", "ulysses", None)
    in_specs = (rows, rows, rows, rows, rows, P(), P(), P())
    out_specs = (P(None, "ulysses", None), P(None, None, "ulysses"))
    return jax.shard_map(
        per_device, mesh=mesh, in_specs=in_specs, out_specs=out_specs, check_vma=False
    )
```

```python
import math

import jax
import jax.numpy as jnp
from jax import lax
from jax.experimental import pallas as pl
from jax.experimental.pallas import tpu as pltpu
from jax.sharding import PartitionSpec as P

HEADS = 32
HD = 128
WIDTH = HEADS * HD
GROUP = 1024
PLANE = 512
RANK = 64
BOTH = 2 * RANK
ROWS = 128
ZS, YS = 8, 4
XS, CS = 4, 2
SLICES = XS * CS
MEMBERS = 8
PIECE = 16
RB = 256
BF16, F32 = jnp.bfloat16, jnp.float32

adapter_scale = 0.5

PLAIN_GROUPS = [[MEMBERS * g + i for i in range(MEMBERS)] for g in range(4)]
SHIFT_GROUPS = [[(MEMBERS * g + 4 + i) % HEADS for i in range(MEMBERS)] for g in range(4)]
PLAIN_SWAP = [(u, u ^ 4) for u in range(HEADS)]
SHIFT_SWAP = [(u, (((u + 4) % HEADS ^ 4) - 4) % HEADS) for u in range(HEADS)]
CORE_SWAP = [(d, d ^ 1) for d in range(SLICES)]
ANYWHERE = pl.BlockSpec(memory_space=pltpu.HBM)
SCALARS = pl.BlockSpec(memory_space=pltpu.SMEM)

SPOT_Y, SPOT_PLAIN, SPOT_SHIFT, SPOT_OWN_PLAIN, SPOT_OWN_SHIFT = range(5)


def y_shift(dy):
    return [(z * YS + y, z * YS + (y + dy) % YS) for z in range(ZS) for y in range(YS)]


def x_shift(dx):
    return [(x * CS + c, ((x + dx) % XS) * CS + c) for x in range(XS) for c in range(CS)]


def exchange(member, axis, groups=None):
    return lax.all_to_all(member, axis, 0, 0, tiled=True, axis_index_groups=groups)


def after(values, *others):
    return lax.optimization_barrier((values, others))[0]


def block(shape):
    return pl.BlockSpec(shape, lambda i, *s: (0,) * len(shape))


def dot_t(a, b):
    return lax.dot_general(a, b, (((1,), (1,)), ((), ())), preferred_element_type=F32)


def dot_0(a, b):
    return lax.dot_general(a, b, (((0,), (0,)), ((), ())), preferred_element_type=F32)


def call(kernel, name, scalars, in_specs, out_specs, out_shape, scratch, cost, vmem=None):
    params = pltpu.CompilerParams(vmem_limit_bytes=vmem and vmem * 2**20)
    return pl.pallas_call(
        kernel,
        name=name,
        out_shape=out_shape,
        grid_spec=pltpu.PrefetchScalarGridSpec(
            num_scalar_prefetch=scalars,
            grid=(1,),
            in_specs=in_specs,
            out_specs=out_specs,
            scratch_shapes=scratch,
        ),
        compiler_params=params,
        cost_estimate=pl.CostEstimate(flops=cost[0], bytes_accessed=cost[1], transcendentals=0),
    )


def order_heads(flags, order):
    def place(h, ones):
        flag = flags[h]
        order[jnp.where(flag > 0, HEADS // 2 + ones, h - ones)] = h
        return ones + jnp.where(flag > 0, 1, 0)

    lax.fori_loop(0, HEADS, place, 0, unroll=True)


def fetch_heads(heads, places, fq_ref, fk_ref, fv_ref, go_ref, up_ref, q_in, v_in, up_in, sems):
    copies = []
    for p, (head, (buffer, entry)) in enumerate(zip(heads, places)):
        cols = pl.ds(pl.multiple_of(head * HD, HD), HD)
        own = pl.ds(p * HD, HD)
        spots = (
            (up_ref, up_in.at[:, own]),
            (fq_ref, q_in.at[:, own]),
            (fv_ref, v_in.at[:, own]),
            (fk_ref, buffer.at[(*entry[:-1], slice(None), pl.ds(entry[-1] + HD, HD))]),
            (go_ref, buffer.at[(*entry[:-1], slice(None), pl.ds(entry[-1] + 3 * HD, HD))]),
        )
        for t, (ref, spot) in enumerate(spots):
            copies.append(pltpu.make_async_copy(ref.at[:, cols], spot, sems.at[p, t]))
            copies[-1].start()
    return copies


def raise_heads(low, copies, places, q_in, v_in, up_in):
    lanes = lax.broadcasted_iota(jnp.int32, (ROWS, BOTH), 1)
    none = jnp.zeros_like(low)
    lows = jnp.concatenate([jnp.where(lanes < RANK, low, none), jnp.where(lanes < RANK, none, low)], axis=0)
    for copy in copies:
        copy.wait()
    raised = jnp.dot(lows, up_in[...], preferred_element_type=F32)
    for p, (buffer, entry) in enumerate(places):
        own = slice(p * HD, (p + 1) * HD)
        q = (q_in[:, own].astype(F32) + adapter_scale * raised[:ROWS, own]).astype(BF16)
        v = (v_in[:, own].astype(F32) + adapter_scale * raised[ROWS:, own]).astype(BF16)
        buffer[(*entry[:-1], slice(None), pl.ds(entry[-1], HD))] = q
        buffer[(*entry[:-1], slice(None), pl.ds(entry[-1] + 2 * HD, HD))] = v


HALF = HEADS // 2


def head_scratch(count):
    return [
        pltpu.VMEM((ROWS, count * HD), BF16),
        pltpu.VMEM((ROWS, count * HD), BF16),
        pltpu.VMEM((BOTH, count * HD), BF16),
        pltpu.SemaphoreType.DMA((count, 5)),
    ]


def prepare_plain_kernel(flags, x_hbm, down_hbm, *refs):
    frozen, (out_ref, order, spot, low_ref, x_in, down_in, whole_sems, q_in, v_in, up_in, sems) = refs[:5], refs[5:]
    wholes = [
        pltpu.make_async_copy(x_hbm, x_in, whole_sems.at[0]),
        pltpu.make_async_copy(down_hbm, down_in, whole_sems.at[1]),
    ]
    for copy in wholes:
        copy.start()
    order_heads(flags, order)
    me = lax.axis_index("ulysses")
    spot[SPOT_Y] = me % YS
    spot[SPOT_PLAIN] = me % MEMBERS
    spot[SPOT_SHIFT] = (me + YS) % MEMBERS
    spot[SPOT_OWN_PLAIN] = me // YS % 2 * PLANE
    spot[SPOT_OWN_SHIFT] = (1 - me // YS % 2) * PLANE
    places = [(out_ref, (p % MEMBERS, p // MEMBERS * 4 * HD)) for p in range(HALF)]
    copies = fetch_heads([order[p] for p in range(HALF)], places, *frozen, q_in, v_in, up_in, sems)
    for copy in wholes:
        copy.wait()
    low = dot_t(x_in[...], down_in[...]).astype(BF16)
    low_ref[...] = low
    for seat in range(MEMBERS):
        out_ref[seat, :, pl.ds(8 * HD, BOTH)] = low
    raise_heads(low, copies, places, q_in, v_in, up_in)


def prepare_plain(flags, x, down, frozen):
    return call(
        prepare_plain_kernel,
        "prepare_plain",
        1,
        [ANYWHERE] * 7,
        [block((MEMBERS, ROWS, 8 * HD + BOTH)), SCALARS, SCALARS, block((ROWS, BOTH))],
        (
            jax.ShapeDtypeStruct((MEMBERS, ROWS, 8 * HD + BOTH), BF16),
            jax.ShapeDtypeStruct((HEADS,), jnp.int32),
            jax.ShapeDtypeStruct((MEMBERS,), jnp.int32),
            jax.ShapeDtypeStruct((ROWS, BOTH), BF16),
        ),
        [pltpu.VMEM((ROWS, WIDTH), BF16), pltpu.VMEM((BOTH, WIDTH), BF16), pltpu.SemaphoreType.DMA((2,))]
        + head_scratch(HALF),
        (10**9, 8 * 10**6),
    )(flags, x, down, *frozen)


def prepare_third_kernel(order, spot, low_ref, *refs):
    frozen, outs, scratch = refs[:5], refs[5:7], refs[7:]
    y, own_half = spot[SPOT_Y], spot[SPOT_OWN_SHIFT] // PLANE
    heads, places = [], []
    for other in range(2):
        for dy in range(YS):
            seat = (own_half + other) % 2 * YS + (y + dy) % YS
            heads.append(order[2 * MEMBERS + seat])
            places.append((outs[other], (dy, 0)))
    copies = fetch_heads(heads, places, *frozen, *scratch)
    raise_heads(low_ref[...], copies, places, *scratch[:3])


def prepare_last_kernel(order, spot, low_ref, *refs):
    frozen, out_ref, scratch = refs[:5], refs[5], refs[6:]
    heads = [order[3 * MEMBERS + seat] for seat in range(MEMBERS)]
    places = [(out_ref, (seat, 0)) for seat in range(MEMBERS)]
    for seat in range(MEMBERS):
        out_ref[seat, :, pl.ds(4 * HD, BOTH)] = low_ref[...]
    copies = fetch_heads(heads, places, *frozen, *scratch)
    raise_heads(low_ref[...], copies, places, *scratch[:3])


def prepare_shifted(item, order, spot, low, frozen):
    shapes = [(YS, ROWS, 4 * HD)] * 2 if item == 2 else [(MEMBERS, ROWS, 4 * HD + BOTH)]
    return call(
        prepare_third_kernel if item == 2 else prepare_last_kernel,
        "prepare_third" if item == 2 else "prepare_last",
        2,
        [block((ROWS, BOTH))] + [ANYWHERE] * 5,
        [block(shape) for shape in shapes],
        [jax.ShapeDtypeStruct(shape, BF16) for shape in shapes],
        head_scratch(MEMBERS),
        (10**9, 8 * 10**6),
    )(order, spot, low, *frozen)


def pack_kernel(own_ref, other_ref, *out_refs):
    for dy, out_ref in enumerate(out_refs, 1):
        out_ref[:, pl.ds(0, 4 * HD)] = own_ref[dy]
        out_ref[:, pl.ds(4 * HD, 4 * HD)] = other_ref[dy]


def pack(own, other):
    shape = (ROWS, 8 * HD)
    return call(
        pack_kernel,
        "pack_third",
        0,
        [block(own.shape)] * 2,
        [block(shape)] * 3,
        (jax.ShapeDtypeStruct(shape, BF16),) * 3,
        [],
        (0, 4 * 10**6),
    )(own, other)


def turn_kernel(spot, x_ref, *out_refs):
    x, core = spot[0] // CS, spot[0] % CS
    *out_refs, stage = out_refs
    for u in range(HEADS):
        stage[pl.ds(u * HD, HD), :] = x_ref[:, pl.ds(u * HD, HD)].T
    for step, out_ref in enumerate(out_refs):
        for other in range(CS):
            d = (x + step) % XS * CS + (core + other) % CS
            for u in range(HEADS):
                rows = pl.ds(pl.multiple_of(u * HD + d * PIECE, PIECE), PIECE)
                out_ref[other, pl.ds(u * PIECE, PIECE), :] = stage[rows, :]


def turn(place, x):
    shape = (CS, HEADS * PIECE, ROWS)
    return call(
        turn_kernel,
        "turn_input",
        1,
        [block(x.shape)],
        [block(shape)] * XS,
        (jax.ShapeDtypeStruct(shape, BF16),) * XS,
        [pltpu.VMEM((WIDTH, ROWS), BF16)],
        (10**9, 2 * 10**6),
    )(place, x)


def attend(x_ref, up_of, grads_ref, column, dv_acc):
    factor = 1.0 / math.sqrt(HD)
    bend = factor * math.log2(math.e)
    row_ids = lax.broadcasted_iota(jnp.int32, (RB, RB), 0)
    column_ids = lax.broadcasted_iota(jnp.int32, (RB, RB), 1)
    keep = column_ids <= row_ids
    for i in range(GROUP // RB):
        n = (i + 1) * RB
        rows = pl.ds(i * RB, RB)
        q = x_ref[rows, pl.ds(0, HD)]
        g = x_ref[rows, pl.ds(3 * HD, HD)]
        k = x_ref[pl.ds(0, n), pl.ds(HD, HD)]
        v = x_ref[pl.ds(0, n), pl.ds(2 * HD, HD)]
        scores = dot_t(q, k)
        last = jnp.where(keep, scores[:, i * RB :], -1e30)
        scores = last if i == 0 else jnp.concatenate([scores[:, : i * RB], last], axis=1)
        top = jnp.max(scores, axis=1, keepdims=True)
        weights = jnp.exp2((scores - top) * bend)
        total = jnp.sum(weights, axis=1, keepdims=True)
        attention = (weights * (1.0 / total)).astype(BF16)
        grad_attention = dot_t(g, v)
        center = jnp.sum(attention.astype(F32) * grad_attention, axis=1, keepdims=True)
        grad_scores = (attention.astype(F32) * (grad_attention - center)).astype(BF16)
        dq = jnp.dot(grad_scores, k, preferred_element_type=F32) * factor
        grads_ref[rows, pl.ds(column, HD)] = dq.astype(BF16)
        dv = dot_0(g, attention)
        if i:
            dv_acc[:, pl.ds(0, i * RB)] += dv[:, : i * RB]
        dv_acc[:, rows] = dv[:, i * RB :]
    dq = grads_ref[:, pl.ds(column, HD)]
    dv = dv_acc[...].T.astype(BF16)
    grads_ref[:, pl.ds(column + HD, HD)] = dv
    lanes = lax.broadcasted_iota(jnp.int32, (GROUP, BOTH), 1)
    up = up_of()
    return jnp.where(lanes < RANK, dot_t(dq, up), dot_t(dv, up))


def attention_plain_kernel(order, spot, arrived, up_hbm, mine_ref, theirs_ref, grads_ref, xs, dv_acc, total, sems, *ups):
    up_in, up_sems = ups
    copies = []
    for item in range(2):
        source = arrived.at[:, pl.ds(item * 4 * HD, 4 * HD)]
        copies.append(pltpu.make_async_copy(source, xs.at[item], sems.at[item]))
        copies[-1].start()
    up_of = [fetch_up(item, order, spot, up_hbm, up_in.at[item], up_sems.at[item]) for item in range(2)]
    copies[0].wait()
    total[...] = attend(xs.at[0], up_of[0], grads_ref, 0, dv_acc)
    copies[1].wait()
    total[...] += attend(xs.at[1], up_of[1], grads_ref, 2 * HD, dv_acc)
    own = pl.multiple_of(spot[SPOT_OWN_PLAIN], PLANE)
    mine_ref[...] = total[pl.ds(own, PLANE), :]
    theirs_ref[...] = total[pl.ds(PLANE - own, PLANE), :].astype(BF16)


def fetch_up(item, order, spot, up_hbm, up_in, sem):
    head = order[item * MEMBERS + spot[SPOT_PLAIN if item < 2 else SPOT_SHIFT]]
    copy = pltpu.make_async_copy(up_hbm.at[:, pl.ds(pl.multiple_of(head * HD, HD), HD)], up_in, sem)
    copy.start()

    def wait_up():
        copy.wait()
        return up_in[...]

    return wait_up


def attention_plain(order, spot, arrived, up):
    shapes = [((PLANE, BOTH), F32), ((PLANE, BOTH), BF16), ((GROUP, 4 * HD), BF16)]
    return call(
        attention_plain_kernel,
        "attention_plain",
        2,
        [ANYWHERE] * 2,
        [block(shape) for shape, _ in shapes],
        [jax.ShapeDtypeStruct(*shape) for shape in shapes],
        [
            pltpu.VMEM((2, GROUP, 4 * HD), BF16),
            pltpu.VMEM((HD, GROUP), F32),
            pltpu.VMEM((GROUP, BOTH), F32),
            pltpu.SemaphoreType.DMA((2,)),
            pltpu.VMEM((2, BOTH, HD), BF16),
            pltpu.SemaphoreType.DMA((2,)),
        ],
        (2 * 10**10, 4 * 10**6),
    )(order, spot, arrived, up)


def attention_shifted_kernel(last, order, spot, *refs):
    y, own = spot[SPOT_Y], spot[SPOT_OWN_SHIFT]
    if last:
        arrived, up, before_hbm, mine_hbm, theirs_hbm, back_ref, grads_hbm, x_in, dv_acc, sems, *refs = refs
        up_in, up_sem, total, before_ref, mine_ref, theirs_ref, grads_ref, more_sems = refs
        pltpu.make_async_copy(arrived.at[:, pl.ds(0, 4 * HD)], x_in, sems.at[0]).start()
    else:
        own_ref, other_ref, *pieces = refs[:5]
        up, back_ref, grads_ref, x_in, dv_acc, sems, up_in, up_sem = refs[5:]
        for dy in range(YS):
            for half in range(2):
                at = (own if half == 0 else PLANE - own) // ROWS + (y - dy + YS) % YS
                rows = pl.ds(pl.multiple_of(at * ROWS, ROWS), ROWS)
                if dy == 0:
                    source = (own_ref, other_ref)[half].at[0]
                else:
                    source = pieces[dy - 1].at[:, pl.ds(half * 4 * HD, 4 * HD)]
                pltpu.make_async_copy(source, x_in.at[rows, :], sems.at[2 * dy + half]).start()
    up_of = fetch_up(3 if last else 2, order, spot, up, up_in, up_sem)
    if last:
        pairs = ((before_hbm, before_ref), (mine_hbm, mine_ref), (theirs_hbm, theirs_ref))
        others = [pltpu.make_async_copy(*pair, more_sems.at[t]) for t, pair in enumerate(pairs)]
        for copy in others:
            copy.start()
    if last:
        pltpu.make_async_copy(arrived.at[:, pl.ds(0, 4 * HD)], x_in, sems.at[0]).wait()
    else:
        for t in range(MEMBERS):
            pltpu.make_async_copy(own_ref.at[0], x_in.at[pl.ds(t * ROWS, ROWS), :], sems.at[t]).wait()
    back = attend(x_in, up_of, grads_ref, 0, dv_acc)
    if not last:
        back_ref[...] = back
        return
    save = pltpu.make_async_copy(grads_ref, grads_hbm, more_sems.at[3])
    save.start()
    for copy in others:
        copy.wait()
    total[...] = back + before_ref[...]
    mine_rows = pl.ds(pl.multiple_of(own, PLANE), PLANE)
    total[mine_rows, :] += mine_ref[...] + theirs_ref[...].astype(F32)
    back_ref[...] = total[...].astype(BF16)
    save.wait()


LAST_SCRATCH = [
    pltpu.VMEM((GROUP, BOTH), F32),
    pltpu.VMEM((GROUP, BOTH), F32),
    pltpu.VMEM((PLANE, BOTH), F32),
    pltpu.VMEM((PLANE, BOTH), BF16),
    pltpu.VMEM((GROUP, 2 * HD), BF16),
    pltpu.SemaphoreType.DMA((4,)),
]


def attention_shifted(order, spot, arrived, up, *more):
    last = len(more) > 0
    shapes = [((GROUP, BOTH), BF16 if last else F32), ((GROUP, 2 * HD), BF16)]

    def body(*refs):
        attention_shifted_kernel(last, *refs)

    return call(
        body,
        "attention_last" if last else "attention_third",
        2,
        [pl.BlockSpec(memory_space=pl.ANY) if last else ANYWHERE] * len(arrived)
        + [ANYWHERE] * (1 + len(more)),
        [block(shapes[0][0]), ANYWHERE] if last else [block(shape) for shape, _ in shapes],
        [jax.ShapeDtypeStruct(*shape) for shape in shapes],
        [pltpu.VMEM((GROUP, 4 * HD), BF16), pltpu.VMEM((HD, GROUP), F32), pltpu.SemaphoreType.DMA((2 * YS,))]
        + [pltpu.VMEM((BOTH, HD), BF16), pltpu.SemaphoreType.DMA]
        + LAST_SCRATCH * last,
        (4 * 10**9, 3 * 10**6) if last else (10**10, 10**4),
    )(order, spot, *arrived, up, *more)


def up_gradient_kernel(low_a, low_b, *refs):
    out_ref = refs[-1]
    for item in range(4):
        low = (low_a, low_b)[item // 2][...]
        grads, column = ((refs[0], 0), (refs[0], 2 * HD), (refs[1], 0), (refs[2], 0))[item]
        for m in range(2):
            columns = pl.ds(column + m * HD, HD)
            part = adapter_scale * dot_0(low[:, m * RANK : (m + 1) * RANK], grads[:, columns])
            part = part.astype(BF16)
            for e in range(RANK // PIECE):
                d = m * (RANK // PIECE) + e
                out_ref[d, pl.ds(item * PIECE, PIECE), :] = part[e * PIECE : (e + 1) * PIECE]


def up_gradients(plain, late, grads):
    shape = (SLICES, 4 * PIECE, HD)
    lows = [pl.BlockSpec((GROUP, BOTH), lambda i, column=column: (0, column)) for column in (8, 4)]
    return call(
        up_gradient_kernel,
        "up_gradients",
        0,
        lows + [block(array.shape) for array in grads],
        block(shape),
        jax.ShapeDtypeStruct(shape, BF16),
        [],
        (2 * 10**9, 3 * 10**6),
    )(plain, late, *grads)


def gather_kernel(summed_ref, ups_ref, out_ref):
    back = jnp.sum(summed_ref[...].astype(F32), axis=0).astype(BF16)
    for d in range(SLICES):
        out_ref[d, pl.ds(0, ROWS), :] = back
    out_ref[:, pl.ds(ROWS, 4 * PIECE), :] = ups_ref[...]


def gather_parts(summed, ups):
    shape = (SLICES, ROWS + 4 * PIECE, HD)
    return call(
        gather_kernel,
        "gather_parts",
        0,
        [block(summed.shape), block(ups.shape)],
        block(shape),
        jax.ShapeDtypeStruct(shape, BF16),
        [],
        (10**7, 10**6),
        16,
    )(summed, ups)


def merge_kernel(order, spot, place, both_ref, *refs):
    x_refs, crossed_refs, out_ref = refs[:XS], refs[XS:-1], refs[-1]
    x, core = place[0] // CS, place[0] % CS
    total = jnp.zeros((HEADS * PIECE, BOTH), F32)
    for dx in range(XS):
        for other in range(CS):
            s = (x - dx + XS) % XS * CS + (core + other) % CS
            back = both_ref[s, pl.ds(0, ROWS), :]
            part = (x_refs, crossed_refs)[other][dx][0]
            total += jnp.dot(part, back, preferred_element_type=F32)
    total = (adapter_scale * total).astype(BF16)
    for u in range(HEADS):
        out_ref[u, pl.ds(0, PIECE), :] = total[u * PIECE : (u + 1) * PIECE]
        out_ref[u, pl.ds(PIECE, PIECE), :] = jnp.zeros((PIECE, HD), BF16)
    ups = jnp.sum(both_ref[:, pl.ds(ROWS, 4 * PIECE), :].astype(F32), axis=0).astype(BF16)
    for item in range(4):
        seat = spot[SPOT_PLAIN if item < 2 else SPOT_SHIFT]
        head = order[item * MEMBERS + seat]
        out_ref[head, pl.ds(PIECE, PIECE), :] = ups[item * PIECE : (item + 1) * PIECE]


def merge(order, spot, place, both, pieces, crossed):
    shape = (HEADS, 2 * PIECE, HD)
    return call(
        merge_kernel,
        "merge_gradients",
        3,
        [block(both.shape)]
        + [
            pl.BlockSpec((1, *piece.shape[1:]), lambda i, *s, half=half: (half, 0, 0))
            for half in range(2)
            for piece in (pieces, crossed)[half]
        ],
        block(shape),
        jax.ShapeDtypeStruct(shape, BF16),
        [],
        (2 * 10**8, 2 * 10**6),
        16,
    )(order, spot, place, both, *pieces, *crossed)


def spread_kernel(in_ref, out_ref):
    total = jnp.sum(in_ref[...].astype(F32), axis=0)
    for d in range(SLICES):
        out_ref[d] = total


def spread(both):
    shape = (SLICES, 2 * PIECE, HD)
    return call(
        spread_kernel,
        "spread_sums",
        0,
        [block(both.shape)],
        block(shape),
        jax.ShapeDtypeStruct(shape, F32),
        [],
        (10**6, 10**6),
        16,
    )(both)


def finish_kernel(in_ref, down_ref, up_ref):
    down = in_ref[:, pl.ds(0, PIECE), :].reshape(HD, BOTH).T
    up = in_ref[:, pl.ds(PIECE, PIECE), :].reshape(BOTH, HD)
    for m in range(2):
        down_ref[m] = down[m * RANK : (m + 1) * RANK]
        up_ref[m] = up[m * RANK : (m + 1) * RANK]


def finish(both):
    shape = (2, RANK, HD)
    return call(
        finish_kernel,
        "finish",
        0,
        [block(both.shape)],
        [block(shape)] * 2,
        [jax.ShapeDtypeStruct(shape, F32)] * 2,
        [],
        (10**6, 10**6),
        16,
    )(both)


def per_device(
    normalized_input,
    frozen_queries,
    frozen_keys,
    frozen_values,
    output_gradient,
    adapter_down_maps,
    adapter_up_maps,
    shifted,
):
    tokens = normalized_input[0]
    place = lax.axis_index("dp").reshape(1)
    up = adapter_up_maps.reshape(BOTH, WIDTH)
    down = adapter_down_maps.transpose(0, 2, 1).reshape(BOTH, WIDTH)

    frozen = (frozen_queries[0], frozen_keys[0], frozen_values[0], output_gradient[0], up)
    sent, order, spot, low = prepare_plain(shifted.astype(jnp.int32), tokens, down, frozen)
    plain = exchange(sent, "ulysses", PLAIN_GROUPS).reshape(GROUP, 8 * HD + BOTH)
    own_c, other_c = prepare_shifted(2, order, spot, low, frozen)
    other_c = lax.ppermute(other_c, "ulysses", SHIFT_SWAP)
    turned = turn(place, after(tokens, own_c))
    pieces = [turned[0]] + [lax.ppermute(turned[dx], "dp", x_shift(dx)) for dx in (1, 2, 3)]
    (sent,) = prepare_shifted(3, order, spot, after(low, turned), frozen)

    packed = pack(after(own_c, pieces[0], sent), other_c)
    arrived_c = [lax.ppermute(packed[dy - 1], "ulysses", y_shift(dy)) for dy in (1, 2, 3)]
    plain, pieces, sent = after((plain, pieces, sent), packed)

    arrived_d = exchange(sent, "ulysses", SHIFT_GROUPS).reshape(GROUP, 4 * HD + BOTH)
    mine, theirs, grads_plain = attention_plain(order, spot, plain, up)
    theirs = lax.ppermute(theirs, "ulysses", PLAIN_SWAP)
    arrived_c = after(arrived_c, grads_plain, sent)
    partial, grads_c = attention_shifted(order, spot, [own_c, other_c, *arrived_c], up)

    arrived_d, theirs = after((arrived_d, theirs), partial)
    partial, grads_d = attention_shifted(order, spot, [arrived_d], up, partial, mine, theirs)
    crossed = [lax.ppermute(piece, "dp", CORE_SWAP) for piece in after(pieces, partial)]
    summed = exchange(partial.reshape(MEMBERS, ROWS, BOTH), "ulysses", SHIFT_GROUPS)
    ups = up_gradients(plain, arrived_d, (grads_plain, grads_c, grads_d))

    both = exchange(gather_parts(summed, ups), "dp")
    both = exchange(merge(order, spot, place, both, pieces, crossed), "ulysses")
    both = exchange(spread(both), "dp")
    grad_down, grad_up = finish(both)
    return (grad_down.transpose(0, 2, 1), grad_up)


def solution(mesh):
    rows = P("dp", "ulysses", None)
    in_specs = (rows, rows, rows, rows, rows, P(), P(), P())
    out_specs = (P(None, "ulysses", None), P(None, None, "ulysses"))
    return jax.shard_map(
        per_device, mesh=mesh, in_specs=in_specs, out_specs=out_specs, check_vma=False
    )
```

```python
import math

import jax
import jax.numpy as jnp
from jax import lax
from jax.experimental import pallas as pl
from jax.experimental.pallas import tpu as pltpu
from jax.sharding import PartitionSpec as P

HEADS = 32
HD = 128
WIDTH = HEADS * HD
GROUP = 1024
PLANE = 512
RANK = 64
BOTH = 2 * RANK
ROWS = 128
ZS, YS = 8, 4
XS, CS = 4, 2
SLICES = XS * CS
MEMBERS = 8
PIECE = 16
RB = 256
BF16, F32 = jnp.bfloat16, jnp.float32

adapter_scale = 0.5

PLAIN_GROUPS = [[MEMBERS * g + i for i in range(MEMBERS)] for g in range(4)]
SHIFT_GROUPS = [[(MEMBERS * g + 4 + i) % HEADS for i in range(MEMBERS)] for g in range(4)]
PLAIN_SWAP = [(u, u ^ 4) for u in range(HEADS)]
SHIFT_SWAP = [(u, (((u + 4) % HEADS ^ 4) - 4) % HEADS) for u in range(HEADS)]
CORE_SWAP = [(d, d ^ 1) for d in range(SLICES)]
ANYWHERE = pl.BlockSpec(memory_space=pltpu.HBM)
SCALARS = pl.BlockSpec(memory_space=pltpu.SMEM)

SPOT_Y, SPOT_PLAIN, SPOT_SHIFT, SPOT_OWN_PLAIN, SPOT_OWN_SHIFT = range(5)


def y_shift(dy):
    return [(z * YS + y, z * YS + (y + dy) % YS) for z in range(ZS) for y in range(YS)]


def x_shift(dx):
    return [(x * CS + c, ((x + dx) % XS) * CS + c) for x in range(XS) for c in range(CS)]


def exchange(member, axis, groups=None):
    return lax.all_to_all(member, axis, 0, 0, tiled=True, axis_index_groups=groups)


def after(values, *others):
    return lax.optimization_barrier((values, others))[0]


def block(shape):
    return pl.BlockSpec(shape, lambda i, *s: (0,) * len(shape))


def dot_t(a, b):
    return lax.dot_general(a, b, (((1,), (1,)), ((), ())), preferred_element_type=F32)


def dot_0(a, b):
    return lax.dot_general(a, b, (((0,), (0,)), ((), ())), preferred_element_type=F32)


def call(kernel, name, scalars, in_specs, out_specs, out_shape, scratch, cost, vmem=None):
    params = pltpu.CompilerParams(vmem_limit_bytes=vmem and vmem * 2**20)
    return pl.pallas_call(
        kernel,
        name=name,
        out_shape=out_shape,
        grid_spec=pltpu.PrefetchScalarGridSpec(
            num_scalar_prefetch=scalars,
            grid=(1,),
            in_specs=in_specs,
            out_specs=out_specs,
            scratch_shapes=scratch,
        ),
        compiler_params=params,
        cost_estimate=pl.CostEstimate(flops=cost[0], bytes_accessed=cost[1], transcendentals=0),
    )


def order_heads(flags, order):
    def place(h, ones):
        flag = flags[h]
        order[jnp.where(flag > 0, HEADS // 2 + ones, h - ones)] = h
        return ones + jnp.where(flag > 0, 1, 0)

    lax.fori_loop(0, HEADS, place, 0, unroll=True)


def fetch_heads(heads, places, fq_ref, fk_ref, fv_ref, go_ref, up_ref, q_in, v_in, up_in, sems):
    copies = []
    for p, (head, (buffer, entry)) in enumerate(zip(heads, places)):
        cols = pl.ds(pl.multiple_of(head * HD, HD), HD)
        own = pl.ds(p * HD, HD)
        spots = (
            (up_ref, up_in.at[:, own]),
            (fq_ref, q_in.at[:, own]),
            (fv_ref, v_in.at[:, own]),
            (fk_ref, buffer.at[(*entry[:-1], slice(None), pl.ds(entry[-1] + HD, HD))]),
            (go_ref, buffer.at[(*entry[:-1], slice(None), pl.ds(entry[-1] + 3 * HD, HD))]),
        )
        for t, (ref, spot) in enumerate(spots):
            copies.append(pltpu.make_async_copy(ref.at[:, cols], spot, sems.at[p, t]))
            copies[-1].start()
    return copies


def raise_heads(low, copies, places, q_in, v_in, up_in):
    lanes = lax.broadcasted_iota(jnp.int32, (ROWS, BOTH), 1)
    none = jnp.zeros_like(low)
    lows = jnp.concatenate([jnp.where(lanes < RANK, low, none), jnp.where(lanes < RANK, none, low)], axis=0)
    for copy in copies[0::5]:
        copy.wait()
    raised = jnp.dot(lows, up_in[...], preferred_element_type=F32)
    for copy in copies[1::5] + copies[2::5]:
        copy.wait()
    for p, (buffer, entry) in enumerate(places):
        own = slice(p * HD, (p + 1) * HD)
        q = (q_in[:, own].astype(F32) + adapter_scale * raised[:ROWS, own]).astype(BF16)
        v = (v_in[:, own].astype(F32) + adapter_scale * raised[ROWS:, own]).astype(BF16)
        buffer[(*entry[:-1], slice(None), pl.ds(entry[-1], HD))] = q
        buffer[(*entry[:-1], slice(None), pl.ds(entry[-1] + 2 * HD, HD))] = v
    for copy in copies[3::5] + copies[4::5]:
        copy.wait()


HALF = HEADS // 2


def head_scratch(count):
    return [
        pltpu.VMEM((ROWS, count * HD), BF16),
        pltpu.VMEM((ROWS, count * HD), BF16),
        pltpu.VMEM((BOTH, count * HD), BF16),
        pltpu.SemaphoreType.DMA((count, 5)),
    ]


def prepare_plain_kernel(flags, x_hbm, down_hbm, *refs):
    frozen, (out_ref, order, spot, low_ref, x_in, down_in, whole_sems, q_in, v_in, up_in, sems) = refs[:5], refs[5:]
    wholes = [
        pltpu.make_async_copy(x_hbm, x_in, whole_sems.at[0]),
        pltpu.make_async_copy(down_hbm, down_in, whole_sems.at[1]),
    ]
    for copy in wholes:
        copy.start()
    order_heads(flags, order)
    me = lax.axis_index("ulysses")
    spot[SPOT_Y] = me % YS
    spot[SPOT_PLAIN] = me % MEMBERS
    spot[SPOT_SHIFT] = (me + YS) % MEMBERS
    spot[SPOT_OWN_PLAIN] = me // YS % 2 * PLANE
    spot[SPOT_OWN_SHIFT] = (1 - me // YS % 2) * PLANE
    places = [(out_ref, (p % MEMBERS, p // MEMBERS * 4 * HD)) for p in range(HALF)]
    copies = fetch_heads([order[p] for p in range(HALF)], places, *frozen, q_in, v_in, up_in, sems)
    for copy in wholes:
        copy.wait()
    low = dot_t(x_in[...], down_in[...]).astype(BF16)
    low_ref[...] = low
    for seat in range(MEMBERS):
        out_ref[seat, :, pl.ds(8 * HD, BOTH)] = low
    raise_heads(low, copies, places, q_in, v_in, up_in)


def prepare_plain(flags, x, down, frozen):
    return call(
        prepare_plain_kernel,
        "prepare_plain",
        1,
        [ANYWHERE] * 7,
        [block((MEMBERS, ROWS, 8 * HD + BOTH)), SCALARS, SCALARS, block((ROWS, BOTH))],
        (
            jax.ShapeDtypeStruct((MEMBERS, ROWS, 8 * HD + BOTH), BF16),
            jax.ShapeDtypeStruct((HEADS,), jnp.int32),
            jax.ShapeDtypeStruct((MEMBERS,), jnp.int32),
            jax.ShapeDtypeStruct((ROWS, BOTH), BF16),
        ),
        [pltpu.VMEM((ROWS, WIDTH), BF16), pltpu.VMEM((BOTH, WIDTH), BF16), pltpu.SemaphoreType.DMA((2,))]
        + head_scratch(HALF),
        (10**9, 8 * 10**6),
    )(flags, x, down, *frozen)


def prepare_third_kernel(order, spot, low_ref, *refs):
    frozen, outs, scratch = refs[:5], refs[5:7], refs[7:]
    y, own_half = spot[SPOT_Y], spot[SPOT_OWN_SHIFT] // PLANE
    heads, places = [], []
    for other in range(2):
        for dy in range(YS):
            seat = (own_half + other) % 2 * YS + (y + dy) % YS
            heads.append(order[2 * MEMBERS + seat])
            places.append((outs[other], (dy, 0)))
    copies = fetch_heads(heads, places, *frozen, *scratch)
    raise_heads(low_ref[...], copies, places, *scratch[:3])


def prepare_last_kernel(order, spot, low_ref, *refs):
    frozen, out_ref, scratch = refs[:5], refs[5], refs[6:]
    heads = [order[3 * MEMBERS + seat] for seat in range(MEMBERS)]
    places = [(out_ref, (seat, 0)) for seat in range(MEMBERS)]
    for seat in range(MEMBERS):
        out_ref[seat, :, pl.ds(4 * HD, BOTH)] = low_ref[...]
    copies = fetch_heads(heads, places, *frozen, *scratch)
    raise_heads(low_ref[...], copies, places, *scratch[:3])


def prepare_shifted(item, order, spot, low, frozen):
    shapes = [(YS, ROWS, 4 * HD)] * 2 if item == 2 else [(MEMBERS, ROWS, 4 * HD + BOTH)]
    return call(
        prepare_third_kernel if item == 2 else prepare_last_kernel,
        "prepare_third" if item == 2 else "prepare_last",
        2,
        [block((ROWS, BOTH))] + [ANYWHERE] * 5,
        [block(shape) for shape in shapes],
        [jax.ShapeDtypeStruct(shape, BF16) for shape in shapes],
        head_scratch(MEMBERS),
        (10**9, 8 * 10**6),
    )(order, spot, low, *frozen)


def pack_kernel(own_ref, other_ref, *out_refs):
    for dy, out_ref in enumerate(out_refs, 1):
        out_ref[:, pl.ds(0, 4 * HD)] = own_ref[dy]
        out_ref[:, pl.ds(4 * HD, 4 * HD)] = other_ref[dy]


def pack(own, other):
    shape = (ROWS, 8 * HD)
    return call(
        pack_kernel,
        "pack_third",
        0,
        [block(own.shape)] * 2,
        [block(shape)] * 3,
        (jax.ShapeDtypeStruct(shape, BF16),) * 3,
        [],
        (0, 4 * 10**6),
    )(own, other)


def turn_kernel(spot, x_ref, *out_refs):
    x, core = spot[0] // CS, spot[0] % CS
    *out_refs, stage = out_refs
    for u in range(HEADS):
        stage[pl.ds(u * HD, HD), :] = x_ref[:, pl.ds(u * HD, HD)].T
    for step, out_ref in enumerate(out_refs):
        for other in range(CS):
            d = (x + step) % XS * CS + (core + other) % CS
            for u in range(HEADS):
                rows = pl.ds(pl.multiple_of(u * HD + d * PIECE, PIECE), PIECE)
                out_ref[other, pl.ds(u * PIECE, PIECE), :] = stage[rows, :]


def turn(place, x):
    shape = (CS, HEADS * PIECE, ROWS)
    return call(
        turn_kernel,
        "turn_input",
        1,
        [block(x.shape)],
        [block(shape)] * XS,
        (jax.ShapeDtypeStruct(shape, BF16),) * XS,
        [pltpu.VMEM((WIDTH, ROWS), BF16)],
        (10**9, 2 * 10**6),
    )(place, x)


def attend(x_ref, up_of, grads_ref, column, dv_acc):
    factor = 1.0 / math.sqrt(HD)
    bend = factor * math.log2(math.e)
    row_ids = lax.broadcasted_iota(jnp.int32, (RB, RB), 0)
    column_ids = lax.broadcasted_iota(jnp.int32, (RB, RB), 1)
    keep = column_ids <= row_ids
    for i in range(GROUP // RB):
        n = (i + 1) * RB
        rows = pl.ds(i * RB, RB)
        q = x_ref[rows, pl.ds(0, HD)]
        g = x_ref[rows, pl.ds(3 * HD, HD)]
        k = x_ref[pl.ds(0, n), pl.ds(HD, HD)]
        v = x_ref[pl.ds(0, n), pl.ds(2 * HD, HD)]
        scores = dot_t(q, k)
        last = jnp.where(keep, scores[:, i * RB :], -1e30)
        scores = last if i == 0 else jnp.concatenate([scores[:, : i * RB], last], axis=1)
        top = jnp.max(scores, axis=1, keepdims=True)
        weights = jnp.exp2((scores - top) * bend)
        total = jnp.sum(weights, axis=1, keepdims=True)
        attention = (weights * (1.0 / total)).astype(BF16)
        grad_attention = dot_t(g, v)
        center = jnp.sum(attention.astype(F32) * grad_attention, axis=1, keepdims=True)
        grad_scores = (attention.astype(F32) * (grad_attention - center)).astype(BF16)
        dq = jnp.dot(grad_scores, k, preferred_element_type=F32) * factor
        grads_ref[rows, pl.ds(column, HD)] = dq.astype(BF16)
        dv = dot_0(g, attention)
        if i:
            dv_acc[:, pl.ds(0, i * RB)] += dv[:, : i * RB]
        dv_acc[:, rows] = dv[:, i * RB :]
    dq = grads_ref[:, pl.ds(column, HD)]
    dv = dv_acc[...].T.astype(BF16)
    grads_ref[:, pl.ds(column + HD, HD)] = dv
    lanes = lax.broadcasted_iota(jnp.int32, (GROUP, BOTH), 1)
    up = up_of()
    return jnp.where(lanes < RANK, dot_t(dq, up), dot_t(dv, up))


def attention_plain_kernel(order, spot, arrived, up_hbm, mine_ref, theirs_ref, grads_ref, xs, dv_acc, total, sems, *ups):
    up_in, up_sems = ups
    copies = []
    for item in range(2):
        source = arrived.at[:, pl.ds(item * 4 * HD, 4 * HD)]
        copies.append(pltpu.make_async_copy(source, xs.at[item], sems.at[item]))
        copies[-1].start()
    up_of = [fetch_up(item, order, spot, up_hbm, up_in.at[item], up_sems.at[item]) for item in range(2)]
    copies[0].wait()
    total[...] = attend(xs.at[0], up_of[0], grads_ref, 0, dv_acc)
    copies[1].wait()
    total[...] += attend(xs.at[1], up_of[1], grads_ref, 2 * HD, dv_acc)
    own = pl.multiple_of(spot[SPOT_OWN_PLAIN], PLANE)
    mine_ref[...] = total[pl.ds(own, PLANE), :]
    theirs_ref[...] = total[pl.ds(PLANE - own, PLANE), :].astype(BF16)


def fetch_up(item, order, spot, up_hbm, up_in, sem):
    head = order[item * MEMBERS + spot[SPOT_PLAIN if item < 2 else SPOT_SHIFT]]
    copy = pltpu.make_async_copy(up_hbm.at[:, pl.ds(pl.multiple_of(head * HD, HD), HD)], up_in, sem)
    copy.start()

    def wait_up():
        copy.wait()
        return up_in[...]

    return wait_up


def attention_plain(order, spot, arrived, up):
    shapes = [((PLANE, BOTH), F32), ((PLANE, BOTH), BF16), ((GROUP, 4 * HD), BF16)]
    return call(
        attention_plain_kernel,
        "attention_plain",
        2,
        [ANYWHERE] * 2,
        [block(shape) for shape, _ in shapes],
        [jax.ShapeDtypeStruct(*shape) for shape in shapes],
        [
            pltpu.VMEM((2, GROUP, 4 * HD), BF16),
            pltpu.VMEM((HD, GROUP), F32),
            pltpu.VMEM((GROUP, BOTH), F32),
            pltpu.SemaphoreType.DMA((2,)),
            pltpu.VMEM((2, BOTH, HD), BF16),
            pltpu.SemaphoreType.DMA((2,)),
        ],
        (2 * 10**10, 4 * 10**6),
    )(order, spot, arrived, up)


def attention_shifted_kernel(last, order, spot, *refs):
    y, own = spot[SPOT_Y], spot[SPOT_OWN_SHIFT]
    if last:
        arrived, up, before_hbm, mine_hbm, theirs_hbm, back_ref, grads_hbm, x_in, dv_acc, sems, *refs = refs
        up_in, up_sem, total, before_ref, mine_ref, theirs_ref, grads_ref, more_sems = refs
        pltpu.make_async_copy(arrived.at[:, pl.ds(0, 4 * HD)], x_in, sems.at[0]).start()
    else:
        own_ref, other_ref, *pieces = refs[:5]
        up, back_ref, grads_ref, x_in, dv_acc, sems, up_in, up_sem = refs[5:]
        for dy in range(YS):
            for half in range(2):
                at = (own if half == 0 else PLANE - own) // ROWS + (y - dy + YS) % YS
                rows = pl.ds(pl.multiple_of(at * ROWS, ROWS), ROWS)
                if dy == 0:
                    source = (own_ref, other_ref)[half].at[0]
                else:
                    source = pieces[dy - 1].at[:, pl.ds(half * 4 * HD, 4 * HD)]
                pltpu.make_async_copy(source, x_in.at[rows, :], sems.at[2 * dy + half]).start()
    up_of = fetch_up(3 if last else 2, order, spot, up, up_in, up_sem)
    if last:
        pairs = ((before_hbm, before_ref), (mine_hbm, mine_ref), (theirs_hbm, theirs_ref))
        others = [pltpu.make_async_copy(*pair, more_sems.at[t]) for t, pair in enumerate(pairs)]
        for copy in others:
            copy.start()
    if last:
        pltpu.make_async_copy(arrived.at[:, pl.ds(0, 4 * HD)], x_in, sems.at[0]).wait()
    else:
        for t in range(MEMBERS):
            pltpu.make_async_copy(own_ref.at[0], x_in.at[pl.ds(t * ROWS, ROWS), :], sems.at[t]).wait()
    back = attend(x_in, up_of, grads_ref, 0, dv_acc)
    if not last:
        back_ref[...] = back
        return
    save = pltpu.make_async_copy(grads_ref, grads_hbm, more_sems.at[3])
    save.start()
    for copy in others:
        copy.wait()
    total[...] = back + before_ref[...]
    mine_rows = pl.ds(pl.multiple_of(own, PLANE), PLANE)
    total[mine_rows, :] += mine_ref[...] + theirs_ref[...].astype(F32)
    back_ref[...] = total[...].astype(BF16)
    save.wait()


LAST_SCRATCH = [
    pltpu.VMEM((GROUP, BOTH), F32),
    pltpu.VMEM((GROUP, BOTH), F32),
    pltpu.VMEM((PLANE, BOTH), F32),
    pltpu.VMEM((PLANE, BOTH), BF16),
    pltpu.VMEM((GROUP, 2 * HD), BF16),
    pltpu.SemaphoreType.DMA((4,)),
]


def attention_shifted(order, spot, arrived, up, *more):
    last = len(more) > 0
    shapes = [((GROUP, BOTH), BF16 if last else F32), ((GROUP, 2 * HD), BF16)]

    def body(*refs):
        attention_shifted_kernel(last, *refs)

    return call(
        body,
        "attention_last" if last else "attention_third",
        2,
        [pl.BlockSpec(memory_space=pl.ANY) if last else ANYWHERE] * len(arrived)
        + [ANYWHERE] * (1 + len(more)),
        [block(shapes[0][0]), ANYWHERE] if last else [block(shape) for shape, _ in shapes],
        [jax.ShapeDtypeStruct(*shape) for shape in shapes],
        [pltpu.VMEM((GROUP, 4 * HD), BF16), pltpu.VMEM((HD, GROUP), F32), pltpu.SemaphoreType.DMA((2 * YS,))]
        + [pltpu.VMEM((BOTH, HD), BF16), pltpu.SemaphoreType.DMA]
        + LAST_SCRATCH * last,
        (4 * 10**9, 3 * 10**6) if last else (10**10, 10**4),
    )(order, spot, *arrived, up, *more)


def up_gradient_kernel(low_a, low_b, *refs):
    out_ref = refs[-1]
    for item in range(4):
        low = (low_a, low_b)[item // 2][...]
        grads, column = ((refs[0], 0), (refs[0], 2 * HD), (refs[1], 0), (refs[2], 0))[item]
        for m in range(2):
            columns = pl.ds(column + m * HD, HD)
            part = adapter_scale * dot_0(low[:, m * RANK : (m + 1) * RANK], grads[:, columns])
            part = part.astype(BF16)
            for e in range(RANK // PIECE):
                d = m * (RANK // PIECE) + e
                out_ref[d, pl.ds(item * PIECE, PIECE), :] = part[e * PIECE : (e + 1) * PIECE]


def up_gradients(plain, late, grads):
    shape = (SLICES, 4 * PIECE, HD)
    lows = [pl.BlockSpec((GROUP, BOTH), lambda i, column=column: (0, column)) for column in (8, 4)]
    return call(
        up_gradient_kernel,
        "up_gradients",
        0,
        lows + [block(array.shape) for array in grads],
        block(shape),
        jax.ShapeDtypeStruct(shape, BF16),
        [],
        (2 * 10**9, 3 * 10**6),
    )(plain, late, *grads)


def gather_kernel(summed_ref, ups_ref, out_ref):
    back = jnp.sum(summed_ref[...].astype(F32), axis=0).astype(BF16)
    for d in range(SLICES):
        out_ref[d, pl.ds(0, ROWS), :] = back
    out_ref[:, pl.ds(ROWS, 4 * PIECE), :] = ups_ref[...]


def gather_parts(summed, ups):
    shape = (SLICES, ROWS + 4 * PIECE, HD)
    return call(
        gather_kernel,
        "gather_parts",
        0,
        [block(summed.shape), block(ups.shape)],
        block(shape),
        jax.ShapeDtypeStruct(shape, BF16),
        [],
        (10**7, 10**6),
        16,
    )(summed, ups)


def merge_kernel(order, spot, place, both_ref, *refs):
    x_refs, crossed_ref, out_ref = refs[:-2], refs[-2], refs[-1]
    x, core = place[0] // CS, place[0] % CS
    total = jnp.zeros((HEADS * PIECE, BOTH), F32)
    for dx in range(XS):
        for other in range(CS):
            s = (x - dx + XS) % XS * CS + (core + other) % CS
            back = both_ref[s, pl.ds(0, ROWS), :]
            part = x_refs[dx][0] if other == 0 else crossed_ref[dx]
            total += jnp.dot(part, back, preferred_element_type=F32)
    total = (adapter_scale * total).astype(BF16)
    for u in range(HEADS):
        out_ref[u, pl.ds(0, PIECE), :] = total[u * PIECE : (u + 1) * PIECE]
        out_ref[u, pl.ds(PIECE, PIECE), :] = jnp.zeros((PIECE, HD), BF16)
    ups = jnp.sum(both_ref[:, pl.ds(ROWS, 4 * PIECE), :].astype(F32), axis=0).astype(BF16)
    for item in range(4):
        seat = spot[SPOT_PLAIN if item < 2 else SPOT_SHIFT]
        head = order[item * MEMBERS + seat]
        out_ref[head, pl.ds(PIECE, PIECE), :] = ups[item * PIECE : (item + 1) * PIECE]


def merge(order, spot, place, both, pieces, crossed):
    shape = (HEADS, 2 * PIECE, HD)
    return call(
        merge_kernel,
        "merge_gradients",
        3,
        [block(both.shape)] + [block((1, *piece.shape[1:])) for piece in pieces] + [block(crossed.shape)],
        block(shape),
        jax.ShapeDtypeStruct(shape, BF16),
        [],
        (2 * 10**8, 2 * 10**6),
        16,
    )(order, spot, place, both, *pieces, crossed)


def spread_kernel(in_ref, out_ref):
    total = jnp.sum(in_ref[...].astype(F32), axis=0)
    for d in range(SLICES):
        out_ref[d] = total


def spread(both):
    shape = (SLICES, 2 * PIECE, HD)
    return call(
        spread_kernel,
        "spread_sums",
        0,
        [block(both.shape)],
        block(shape),
        jax.ShapeDtypeStruct(shape, F32),
        [],
        (10**6, 10**6),
        16,
    )(both)


def finish_kernel(in_ref, down_ref, up_ref):
    down = in_ref[:, pl.ds(0, PIECE), :].reshape(HD, BOTH).T
    up = in_ref[:, pl.ds(PIECE, PIECE), :].reshape(BOTH, HD)
    for m in range(2):
        down_ref[m] = down[m * RANK : (m + 1) * RANK]
        up_ref[m] = up[m * RANK : (m + 1) * RANK]


def finish(both):
    shape = (2, RANK, HD)
    return call(
        finish_kernel,
        "finish",
        0,
        [block(both.shape)],
        [block(shape)] * 2,
        [jax.ShapeDtypeStruct(shape, F32)] * 2,
        [],
        (10**6, 10**6),
        16,
    )(both)


def per_device(
    normalized_input,
    frozen_queries,
    frozen_keys,
    frozen_values,
    output_gradient,
    adapter_down_maps,
    adapter_up_maps,
    shifted,
):
    tokens = normalized_input[0]
    place = lax.axis_index("dp").reshape(1)
    up = adapter_up_maps.reshape(BOTH, WIDTH)
    down = adapter_down_maps.transpose(0, 2, 1).reshape(BOTH, WIDTH)

    frozen = (frozen_queries[0], frozen_keys[0], frozen_values[0], output_gradient[0], up)
    sent, order, spot, low = prepare_plain(shifted.astype(jnp.int32), tokens, down, frozen)
    plain = exchange(sent, "ulysses", PLAIN_GROUPS).reshape(GROUP, 8 * HD + BOTH)
    own_c, other_c = prepare_shifted(2, order, spot, low, frozen)
    other_c = lax.ppermute(other_c, "ulysses", SHIFT_SWAP)
    turned = turn(place, after(tokens, own_c))
    pieces = [turned[0]] + [lax.ppermute(turned[dx], "dp", x_shift(dx)) for dx in (1, 2, 3)]
    (sent,) = prepare_shifted(3, order, spot, after(low, turned), frozen)

    packed = pack(after(own_c, pieces[0], sent), other_c)
    arrived_c = [lax.ppermute(packed[dy - 1], "ulysses", y_shift(dy)) for dy in (1, 2, 3)]
    plain, pieces, sent = after((plain, pieces, sent), packed)

    arrived_d = exchange(sent, "ulysses", SHIFT_GROUPS).reshape(GROUP, 4 * HD + BOTH)
    crossed = lax.ppermute(jnp.stack([piece[1] for piece in pieces]), "dp", CORE_SWAP)
    mine, theirs, grads_plain = attention_plain(order, spot, plain, up)
    theirs = lax.ppermute(theirs, "ulysses", PLAIN_SWAP)
    arrived_c = after(arrived_c, grads_plain, sent)
    partial, grads_c = attention_shifted(order, spot, [own_c, other_c, *arrived_c], up)

    arrived_d, theirs, crossed = after((arrived_d, theirs, crossed), partial)
    partial, grads_d = attention_shifted(order, spot, [arrived_d], up, partial, mine, theirs)
    summed = exchange(partial.reshape(MEMBERS, ROWS, BOTH), "ulysses", SHIFT_GROUPS)
    ups = up_gradients(plain, arrived_d, (grads_plain, grads_c, grads_d))

    both = exchange(gather_parts(summed, ups), "dp")
    both = exchange(merge(order, spot, place, both, pieces, crossed), "ulysses")
    both = exchange(spread(both), "dp")
    grad_down, grad_up = finish(both)
    return (grad_down.transpose(0, 2, 1), grad_up)


def solution(mesh):
    rows = P("dp", "ulysses", None)
    in_specs = (rows, rows, rows, rows, rows, P(), P(), P())
    out_specs = (P(None, "ulysses", None), P(None, None, "ulysses"))
    return jax.shard_map(
        per_device, mesh=mesh, in_specs=in_specs, out_specs=out_specs, check_vma=False
    )
```
